256 devices in a mesh: cluster: 8 (over z_hi, core), shard: 32 (over x, z_lo, y).
Axes of the slice: x: 4, y: 4, z: 8 (z_hi: 4, z_lo: 2; z = z_hi * 2 + z_lo), core: 2. Of those that a mesh axis runs over, the one named last changes fastest.
Arguments:
- flow_start: float32 [4096, 256], P(('cluster', 'shard')), may hold values from 0 to 1
- demand: float32 [4096, 256], P(('cluster', 'shard')), may hold values from 0.25 to 2
- utility: float32 [4096, 256], P(('cluster', 'shard')), may hold values from 1 to 16
- path_count: int32 [4096], P(('cluster', 'shard')), may hold values from 1 to 256, as said below
- cluster_size: int32 [8], P('cluster'), may hold values from 1 to 16, as said below
- incidence: float32 [8192, 256, 128], P(('cluster', 'shard')), may hold values from 0 to 1, as said below
- inc_path: int32 [8192], P(('cluster', 'shard')), may hold values from 0 to 511, as said below
- inc_edge: int32 [8192], P(('cluster', 'shard')), may hold values from 0 to 6
- capacity: float32 [1792, 128], P(('cluster', 'shard')), may hold values from 0.25 to 4
- dual_start: float32 [1792, 128], P(('cluster', 'shard')), may hold values from 0 to 7
- partner: int32 [8, 3], P('cluster'), may hold values from 0 to 7, as said below
Outputs:
- flows: float32 [4096, 256], P(('cluster', 'shard'))
- duals: float32 [1792, 128], P(('cluster', 'shard'))
The draws below stay inside these ranges and needn't reach their ends.
Inputs may be any that keep to these rules, and one draw needn't show every extreme that they name: `path_count`: some path block has 256 live paths. `cluster_size`: some cluster has 16. partner[c, k] = q implies partner[q, k] = c; the partners of a cluster are distinct and differ from it. `incidence`: every entry is 0 or 1. Among the 32 incidence blocks of one device, at most 2 have the same value of inc_path // 16, and on every device some value is taken by exactly 2.
All inputs are finite; a program needn't handle non-finite values.
Results may differ from the reference program's by a relative error of at most 0.0001.
Values sent between devices are 32-bit elements; how exact they have to be, the bound alone decides.
A program may use at most 64 MiB of HBM per device.

```python
import math
import jax
import jax.numpy as jnp
from jax import lax

PATH = 256
EDGE = 128
PB_DEV = 16
NI = 32
EB_DEV = 4
ITERS = 3
KP = 3
NBL = 7
PB_C = 512
PATHBLK = 4096
INCBLK = 8192
EDGEBLK = 1792
REQ = 2
LOAD_UNIT = 7
NORM_BOUND = 292
N_CLUSTER = 8
N_SHARD = 32


def draw_path_count(key, part):
    key_full, key_ragged = jax.random.split(key)
    full_flag = jax.random.randint(key_full, (PATHBLK,), 0, 2)
    ragged = jax.random.randint(key_ragged, (PATHBLK,), 1, PATH + 1)
    counts = jnp.where(full_flag == 1, PATH, ragged)
    return counts.at[0].set(PATH).astype(jnp.int32)


def draw_cluster_size(key, part):
    key_sizes, key_chosen = jax.random.split(key)
    sizes = jax.random.randint(key_sizes, (N_CLUSTER,), 1, PB_DEV + 1)
    chosen = jax.random.randint(key_chosen, (), 0, N_CLUSTER)
    return sizes.at[chosen].set(PB_DEV).astype(jnp.int32)


def draw_partner(key, part):
    ordering = jax.random.permutation(key, N_CLUSTER).astype(jnp.int32)
    inverse = jnp.argsort(ordering).astype(jnp.int32)
    slot_ids = jnp.arange(1, KP + 1, dtype=jnp.int32)
    return inverse[jnp.bitwise_xor(ordering[:, None], slot_ids[None, :])].astype(jnp.int32)


def draw_incidence(key, part):
    picks = jax.random.randint(key, (INCBLK, PATH, EDGE), 0, 32)
    return (picks == 0).astype(jnp.float32)


def draw_inc_path(key, part):
    base_key = jax.random.fold_in(key, 7001)
    slot_total = N_SHARD * REQ
    slot_ids = jnp.arange(slot_total, dtype=jnp.int32)
    slot_owner = slot_ids // REQ

    def one_device(device):
        device_key = jax.random.fold_in(base_key, device)
        key_chosen, key_rank, key_block, key_order = jax.random.split(device_key, 4)
        chosen = jax.random.randint(key_chosen, (), 0, N_SHARD)
        ranking = jax.random.permutation(key_rank, slot_total).astype(jnp.int32)
        score = jnp.where(slot_owner == chosen, slot_ids, slot_total + ranking)
        order = jnp.argsort(score, stable=True)
        owners = slot_owner[order[:NI]]
        owners = owners[jax.random.permutation(key_order, NI)]
        blocks = jax.random.randint(key_block, (NI,), 0, PB_DEV)
        return (owners * PB_DEV + blocks).astype(jnp.int32)
    devices = jnp.arange(INCBLK // NI, dtype=jnp.int32)
    return jax.vmap(one_device)(devices).reshape(INCBLK).astype(jnp.int32)


def plant(array, rng, least, largest):
    longest = array.shape.index(max(array.shape))
    spots = []
    for shift in (0, 1):
        where = [jax.random.randint(jax.random.fold_in(rng, axis), (), 0, length) for axis, length in enumerate(array.shape)]
        where[longest] = (where[longest] + shift) % array.shape[longest]
        spots.append(tuple(where))
    return array.at[spots[0]].set(least).at[spots[1]].set(largest)


def shard_levels(stream_key, shape, cuts, low, high):
    loudness, own = 1.0, jax.random.fold_in(stream_key, 6)
    for position, parts in cuts:
        steps = jnp.exp(jax.random.uniform(jax.random.fold_in(own, position), (parts,), jnp.float32, low / len(cuts), high / len(cuts)))
        loudness = loudness * jnp.repeat(steps, shape[position] // parts).reshape([-1 if axis == position else 1 for axis in range(len(shape))])
    return loudness


def setup_inputs(seed: int = 0) -> dict:
    seeds = jax.random.split(jax.random.key(seed), 12)
    flow_start = jnp.clip(1.0 * jax.random.uniform(seeds[0], (PATHBLK, PATH), jnp.float32) ** shard_levels(seeds[0], (PATHBLK, PATH), ((0, 256),), -0.2, 0.2), 0.0, 1.0)
    demand = jnp.clip(jnp.exp(math.log(2.0) - 2.0794415 * jax.random.uniform(seeds[1], (PATHBLK, PATH), jnp.float32) ** shard_levels(seeds[1], (PATHBLK, PATH), ((0, 256),), -0.2, 0.2)), 0.25, 2.0)
    utility = jnp.clip(jnp.exp(math.log(16.0) - 2.7725887 * jax.random.uniform(seeds[2], (PATHBLK, PATH), jnp.float32) ** shard_levels(seeds[2], (PATHBLK, PATH), ((0, 256),), -0.2, 0.2)), 1.0, 16.0)
    path_count = draw_path_count(jax.random.fold_in(seeds[11], 71), 0)
    cluster_size = draw_cluster_size(jax.random.fold_in(seeds[11], 71), 0)
    incidence = draw_incidence(jax.random.fold_in(seeds[11], 71), 0)
    inc_path = draw_inc_path(jax.random.fold_in(seeds[11], 71), 0)
    inc_edge = plant(jax.random.randint(seeds[7], (INCBLK,), 0, NBL), jax.random.fold_in(seeds[7], 1), 0, NBL - 1).astype(jnp.int32)
    capacity = jnp.clip(jnp.exp(math.log(4.0) - 2.7725887 * jax.random.uniform(seeds[8], (EDGEBLK, EDGE), jnp.float32) ** shard_levels(seeds[8], (EDGEBLK, EDGE), ((0, 256),), -0.2, 0.2)), 0.25, 4.0)
    dual_start = jnp.clip(7.0 * jax.random.uniform(seeds[9], (EDGEBLK, EDGE), jnp.float32) ** shard_levels(seeds[9], (EDGEBLK, EDGE), ((0, 256),), -0.2, 0.2), 0.0, 7.0)
    partner = draw_partner(jax.random.fold_in(seeds[11], 71), 0)
    return dict(flow_start=flow_start, demand=demand, utility=utility, path_count=path_count, cluster_size=cluster_size, incidence=incidence, inc_path=inc_path, inc_edge=inc_edge, capacity=capacity, dual_start=dual_start, partner=partner)


def twin_blocks(blocks, partner):
    layout = blocks.reshape(N_CLUSTER, N_SHARD, NBL, EDGE)
    border = layout[:, :, EB_DEV:, :]
    slot_ids = jnp.arange(KP, dtype=jnp.int32)
    twin_part = border[partner, :, slot_ids[None, :]]
    return layout, border, jnp.transpose(twin_part, (0, 2, 1, 3))


def rebuild(layout, border_new):
    joined = jnp.concatenate([layout[:, :, :EB_DEV, :], border_new], axis=2)
    return joined.reshape(EDGEBLK, EDGE)


def reference(flow_start, demand, utility, path_count, cluster_size, incidence, inc_path, inc_edge, capacity, dual_start, partner):
    exact_mode = lax.Precision.HIGHEST
    block_ids = jnp.arange(PATHBLK, dtype=jnp.int32)
    cluster_of = block_ids // PB_C
    live_block = (block_ids % PB_DEV) < cluster_size[cluster_of]
    path_ids = jnp.arange(PATH, dtype=jnp.int32)
    live_mask = (live_block[:, None] & (path_ids[None, :] < path_count[:, None])).astype(jnp.float32)
    inc_ids = jnp.arange(INCBLK, dtype=jnp.int32)
    device_of = inc_ids // NI
    path_rows = ((device_of // N_SHARD) * PB_C + inc_path).astype(jnp.int32)
    edge_rows = (device_of * NBL + inc_edge).astype(jnp.int32)
    capacity_unit = float(LOAD_UNIT)
    step_size = 1.0 / (2.0 * NORM_BOUND)

    layout, border, twin_part = twin_blocks(capacity, partner)
    limit = capacity_unit * rebuild(layout, 0.5 * (border + twin_part))
    layout, border, twin_part = twin_blocks(dual_start, partner)
    duals = rebuild(layout, 0.5 * (border + twin_part))

    def total_load(flows_now):
        picked = flows_now[path_rows]
        terms = jnp.einsum("ipe,ip->ie", incidence, picked, precision=exact_mode)
        own_load = jax.ops.segment_sum(terms, edge_rows, num_segments=EDGEBLK)
        layout_now, border_now, twin_now = twin_blocks(own_load, partner)
        return rebuild(layout_now, border_now + twin_now)

    flows = jnp.minimum(jnp.maximum(flow_start, 0.0), demand) * live_mask
    load = total_load(flows)
    split = jnp.minimum(limit, load + duals)
    duals = (duals + load) - split
    for iteration in range(ITERS):
        residual = (load - split) + duals
        back_terms = jnp.einsum("ipe,ie->ip", incidence, residual[edge_rows], precision=exact_mode)
        gradient = jax.ops.segment_sum(back_terms, path_rows, num_segments=PATHBLK)
        flows = jnp.minimum(jnp.maximum(flows - step_size * (gradient - utility), 0.0), demand) * live_mask
        load = total_load(flows)
        split = jnp.minimum(limit, load + duals)
        duals = (duals + load) - split
    return flows, duals
```

```python
import functools

import jax
import jax.numpy as jnp
from jax import lax
from jax.experimental import pallas as pl
from jax.experimental.pallas import tpu as pltpu
from jax.sharding import PartitionSpec as P

ITERS = 3
MESH = pl.DeviceIdType.MESH
F32, BF16, I32 = jnp.float32, jnp.bfloat16, jnp.int32


def iota(shape, axis):
    return lax.broadcasted_iota(I32, shape, axis)


def thirds(x):
    high = x.astype(BF16).astype(F32)
    rest = x - high
    mid = rest.astype(BF16).astype(F32)
    return high, mid, rest - mid


def dot(a, b):
    return jnp.dot(a.astype(BF16), b.astype(BF16), preferred_element_type=F32)


def dot_nt(a, b):
    dims = (((1,), (1,)), ((), ()))
    return lax.dot_general(a.astype(BF16), b.astype(BF16), dims, preferred_element_type=F32)


def pick(selector, x):
    high, mid, low = thirds(x)
    return (dot(selector, low) + dot(selector, mid)) + dot(selector, high)


def kernel(
    dims,
    path_count, cluster_size, inc_path, inc_edge, partner,
    flow_start, demand, utility, incidence, capacity, dual_start,
    flows_out, duals_out,
    inc_f32, inc, slot_edge, slot_edge_t, choose, choose_t,
    ask_send, ask_recv, flow_send, flow_recv, sum_send, sum_recv,
    edge_send, edge_recv, border_send, border_recv,
    load_sem, send_sem, ask_sem, flow_sem, sum_sem, edge_sem, border_sem,
):
    clusters, shards, blocks, paths, incs, edges, slots, norm_bound, unit = dims
    step_size = 1.0 / (2.0 * norm_bound)
    cluster, shard = lax.axis_index("cluster"), lax.axis_index("shard")
    interior = edges - slots

    load = pltpu.make_async_copy(incidence, inc_f32, load_sem)
    load.start()

    barrier = pltpu.get_barrier_semaphore()

    def greet_shard(k, _):
        pl.semaphore_signal(barrier, inc=1, device_id=(cluster, lax.rem(shard + k, shards)), device_id_type=MESH)
        return 0

    def greet_cluster(k, _):
        pl.semaphore_signal(barrier, inc=1, device_id=(lax.rem(cluster + k, clusters), shard), device_id_type=MESH)
        return 0

    lax.fori_loop(1, shards, greet_shard, 0)
    lax.fori_loop(1, clusters, greet_cluster, 0)
    pl.semaphore_wait(barrier, shards + clusters - 2)

    def to_shards(src, dst, sem):
        def one(k, _):
            peer = lax.rem(shard + k, shards)
            pltpu.make_async_remote_copy(
                src_ref=src.at[peer], dst_ref=dst.at[shard], send_sem=send_sem.at[sem[1]], recv_sem=sem[0],
                device_id=(cluster, peer), device_id_type=MESH).start()
            return 0
        lax.fori_loop(1, shards, one, 0)
        dst[shard] = src[shard]

    def to_clusters(src, dst, sem):
        def one(k, _):
            peer = lax.rem(cluster + k, clusters)
            pltpu.make_async_remote_copy(
                src_ref=src, dst_ref=dst.at[cluster], send_sem=send_sem.at[sem[1]], recv_sem=sem[0],
                device_id=(peer, shard), device_id_type=MESH).start()
            return 0
        lax.fori_loop(1, clusters, one, 0)
        dst[cluster] = src[...]

    def wait(dst, sem, count):
        whole = pltpu.make_async_remote_copy(
            src_ref=dst.at[pl.ds(0, count)], dst_ref=dst.at[pl.ds(0, count)], send_sem=send_sem.at[sem[1]],
            recv_sem=sem[0], device_id=(cluster, lax.rem(shard + 1, shards)), device_id_type=MESH)
        whole.wait_recv()
        whole.wait_send()

    ask, flow, total, edge = (ask_sem, 0), (flow_sem, 1), (sum_sem, 2), (edge_sem, 3)

    def border_first(ref):
        x = ref[...]
        return jnp.concatenate([x[interior:], jnp.zeros((8 - edges, x.shape[1]), F32), x[:interior]], axis=0)

    cap = border_first(capacity)
    dual = border_first(dual_start)
    edge_send[...] = jnp.concatenate([cap[:4], dual[:4]], axis=0)
    to_clusters(edge_send, edge_recv, edge)

    rows, lanes = iota((128, 128), 0), iota((128, 128), 1)
    row_dev, row_slot, row_half = rows >> 2, (rows >> 1) & 1, rows & 1
    lane1 = iota((1, 128), 1)
    lane_path = jnp.full((1, 128), -1, I32)
    for i in range(incs):
        lane_path = jnp.where(lane1 == i, inc_path[i], lane_path)
    owner = (lane_path >> 4) == row_dev
    before = dot(owner.astype(F32), (rows < lanes).astype(F32))
    slot = owner & (before == row_slot.astype(F32))
    wanted = jnp.sum(jnp.where(slot, (lane_path & 15) + 1, 0).astype(F32), axis=1, keepdims=True) - 1.0
    ask_send[...] = jnp.broadcast_to(wanted, (128, 128)).reshape(ask_send.shape)
    to_shards(ask_send, ask_recv, ask)

    lane_q = iota((1, 512), 1)
    lane_edge = jnp.full((1, 512), -1, I32)
    for i in range(incs):
        lane_edge = jnp.where((lane_q >> 4) == i, (inc_edge[i] + (8 - interior)) & 7, lane_edge)
    spread = (iota((128, 512), 0) == (iota((128, 512), 1) >> 4)).astype(F32)
    fits = (lane_edge == (lane_q & 7)) & (((lane_q >> 3) & 1) == (iota((128, 512), 0) & 1))
    both = jnp.where(fits, dot(slot.astype(F32), spread), 0.0)
    slot_edge[...] = both.astype(BF16)
    slot_edge_t[...] = both.T.astype(BF16)

    def halves(ref):
        x = ref[...]
        return jnp.concatenate([x[:, :128], x[:, 128:]], axis=0)

    low_flow, top_flow, gain = halves(flow_start), halves(demand), halves(utility)
    row32 = iota((32, 128), 0)
    count = jnp.zeros((32, 128), I32)
    for b in range(blocks):
        count = jnp.where((row32 & 15) == b, path_count[b], count)
    live = (((row32 & 15) < cluster_size[0]) & ((row32 >> 4) * 128 + iota((32, 128), 1) < count)).astype(F32)
    flows = jnp.minimum(jnp.maximum(low_flow, 0.0), top_flow) * live

    load.wait()

    def shrink(i, _):
        inc[pl.ds(pl.multiple_of(i * paths, paths), paths), :] = inc_f32[i].astype(BF16)
        return 0
    lax.fori_loop(0, incs, shrink, 0)

    partner_row = jnp.full((4, 128), -1, I32)
    for k in range(slots):
        partner_row = jnp.where(iota((4, 128), 0) == k, partner[0, k], partner_row)
    partner8 = jnp.concatenate([partner_row, partner_row], axis=0)
    wait(edge_recv, edge, clusters - 1)
    twin = jnp.zeros((8, 128), F32)
    for c in range(clusters):
        twin = twin + jnp.where(partner8 == c, edge_recv[c], 0.0)
    limit = unit * jnp.concatenate([0.5 * (cap[:4] + twin[:4]), cap[4:]], axis=0)
    duals = jnp.concatenate([0.5 * (dual[:4] + twin[4:]), dual[4:]], axis=0)

    wait(ask_recv, ask, shards - 1)
    asked = ask_recv[...].reshape(128, 128)
    chosen = ((asked == (lanes & 15).astype(F32)) & ((lanes >> 4) == row_half)).astype(F32)
    choose[...] = chosen.astype(BF16)
    choose_t[...] = chosen.T.astype(BF16)

    def share(flows):
        flow_send[...] = pick(choose[:, :32], flows).reshape(flow_send.shape)
        to_shards(flow_send, flow_recv, flow)

    def total_load(t):
        wait(flow_recv, flow, shards - 1)
        got = flow_recv[...].reshape(128, 128)
        parts = dot(slot_edge_t[...], jnp.concatenate(thirds(got), axis=1))
        columns = []
        for q in range(2 * incs):
            chunk = parts[q * 8:q * 8 + 8]
            columns.append(jnp.concatenate([chunk[:, :128], chunk[:, 128:256], chunk[:, 256:]], axis=0).astype(BF16))
        sums = dot(jnp.concatenate(columns, axis=1), inc[...])
        own = (sums[16:] + sums[8:16]) + sums[:8]
        border_send[...] = own[:4]
        border = (border_sem.at[t], 4)
        to_clusters(border_send, border_recv.at[t], border)
        wait(border_recv.at[t], border, clusters - 1)
        twin = jnp.zeros((4, 128), F32)
        for c in range(clusters):
            twin = twin + jnp.where(partner_row == c, border_recv[t, c], 0.0)
        return jnp.concatenate([own[:4] + twin, own[4:]], axis=0)

    def settle(load, duals):
        split = jnp.minimum(limit, load + duals)
        duals = (duals + load) - split
        return (load - split) + duals, duals

    share(flows)
    residual, duals = settle(total_load(0), duals)

    def iterate(t, carry):
        flows, residual, duals = carry
        parts = dot_nt(jnp.concatenate(thirds(residual), axis=0), inc[...])
        back = (parts[16:] + parts[8:16]) + parts[:8]
        back = jnp.concatenate([back[:, q * 128:q * 128 + 128] for q in range(2 * incs)], axis=0)
        sum_send[...] = pick(slot_edge[...], back).reshape(sum_send.shape)
        to_shards(sum_send, sum_recv, total)
        wait(sum_recv, total, shards - 1)
        grad = pick(choose_t[:32, :], sum_recv[...].reshape(128, 128))
        flows = jnp.minimum(jnp.maximum(flows - step_size * (grad - gain), 0.0), top_flow) * live
        share(flows)
        residual, duals = settle(total_load(t), duals)
        return flows, residual, duals

    flows, residual, duals = lax.fori_loop(1, ITERS + 1, iterate, (flows, residual, duals))
    flows_out[...] = jnp.concatenate([flows[:16], flows[16:]], axis=1)
    duals_out[...] = jnp.concatenate([duals[4:], duals[:slots]], axis=0)


def body(flow_start, demand, utility, path_count, cluster_size, incidence, inc_path, inc_edge, capacity, dual_start, partner):
    blocks, paths = flow_start.shape
    incs, _, width = incidence.shape
    edges, slots = capacity.shape[0], partner.shape[1]
    clusters, shards = lax.axis_size("cluster"), lax.axis_size("shard")
    norm_bound = max(2, incs * incs * paths * width // (1024 * edges * blocks))
    unit = float(max(1, incs * paths // (160 * edges)))
    dims = (clusters, shards, blocks, paths, incs, edges, slots, norm_bound, unit)
    smem, vmem, hbm = (pl.BlockSpec(memory_space=m) for m in (pltpu.SMEM, pltpu.VMEM, pl.ANY))
    dma = pltpu.SemaphoreType.DMA
    message = pltpu.VMEM((shards, 4, 128), F32)
    return pl.pallas_call(
        functools.partial(kernel, dims),
        out_shape=(jax.ShapeDtypeStruct(flow_start.shape, F32), jax.ShapeDtypeStruct(capacity.shape, F32)),
        in_specs=[smem] * 5 + [vmem, vmem, vmem, hbm, vmem, vmem],
        out_specs=(vmem, vmem),
        scratch_shapes=[
            pltpu.VMEM((incs, paths, width), F32),
            pltpu.VMEM((incs * paths, width), BF16),
            pltpu.VMEM((128, 512), BF16),
            pltpu.VMEM((512, 128), BF16),
            pltpu.VMEM((128, 128), BF16),
            pltpu.VMEM((128, 128), BF16),
            message, message, message, message, message, message,
            pltpu.VMEM((8, 128), F32),
            pltpu.VMEM((clusters, 8, 128), F32),
            pltpu.VMEM((4, 128), F32),
            pltpu.VMEM((ITERS + 1, clusters, 4, 128), F32),
            dma(()), dma((5,)), dma(()), dma(()), dma(()), dma(()), dma((ITERS + 1,)),
        ],
        compiler_params=pltpu.CompilerParams(
            collective_id=0, has_side_effects=True, vmem_limit_bytes=40 * 1024 * 1024),
    )(path_count, cluster_size, inc_path, inc_edge, partner, flow_start, demand, utility, incidence, capacity, dual_start)


def solution(mesh):
    both = P(("cluster", "shard"))
    rows = P(("cluster", "shard"), None)
    return jax.shard_map(
        body,
        mesh=mesh,
        in_specs=(rows, rows, rows, both, P("cluster"), P(("cluster", "shard"), None, None), both, both, rows, rows, P("cluster", None)),
        out_specs=(rows, rows),
        check_vma=False,
    )
```

```python
import functools

import jax
import jax.numpy as jnp
from jax import lax
from jax.experimental import pallas as pl
from jax.experimental.pallas import tpu as pltpu
from jax.sharding import PartitionSpec as P

ITERS = 3
GRID = (4, 2, 4)
MESH = pl.DeviceIdType.MESH
F32, BF16, I32 = jnp.float32, jnp.bfloat16, jnp.int32


def iota(shape, axis):
    return lax.broadcasted_iota(I32, shape, axis)


def thirds(x):
    high = x.astype(BF16).astype(F32)
    rest = x - high
    mid = rest.astype(BF16).astype(F32)
    return high, mid, rest - mid


def dot(a, b):
    return jnp.dot(a.astype(BF16), b.astype(BF16), preferred_element_type=F32)


def dot_nt(a, b):
    dims = (((1,), (1,)), ((), ()))
    return lax.dot_general(a.astype(BF16), b.astype(BF16), dims, preferred_element_type=F32)


def pick(selector, x):
    high, mid, low = thirds(x)
    return (dot(selector, low) + dot(selector, mid)) + dot(selector, high)


def hops(offset):
    return sum(min(d, n - d) for d, n in zip(offset, GRID))


NEAR = sorted(((x, z, y) for x in range(4) for z in range(2) for y in range(4) if hops((x, z, y)) <= 2), key=hops)
BACK = [NEAR.index(tuple(-d % n for d, n in zip(offset, GRID))) for offset in NEAR]
FAR_FIRST = sorted(range(1, 32), key=lambda u: -(hops(NEAR[u]) if u < 16 else 5 - hops(NEAR[u - 16])))
NEAR_FAR_FIRST = [u for u in FAR_FIRST if u < 16]


def kernel(
    dims,
    path_count_hbm, cluster_size_hbm, inc_path_hbm, inc_edge_hbm, partner_hbm,
    flow_start_hbm, demand_hbm, utility_hbm, incidence_hbm, capacity_hbm, dual_start_hbm,
    flows_out, duals_out,
    path_count, cluster_size, inc_path, inc_edge, partner,
    flow_start, demand, utility, incidence, capacity, dual_start,
    inc, slot_edge, slot_edge_t, choose, choose_t,
    ask_send, ask_recv, flow_send, flow_recv, sum_send, sum_recv,
    edge_send, edge_recv, border_send, border_recv, start_send, start_recv, rest_send, rest_recv,
    load_sem, send_sem, ask_sem, flow_sem, sum_sem, edge_sem, border_sem, start_sem, rest_sem,
):
    clusters, shards, blocks, paths, incs, edges, slots, norm_bound, unit = dims
    step_size = 1.0 / (2.0 * norm_bound)
    cluster, shard = lax.axis_index("cluster"), lax.axis_index("shard")
    interior = edges - slots

    barrier = pltpu.get_barrier_semaphore()

    def greet_shard(k, _):
        pl.semaphore_signal(barrier, inc=1, device_id=(cluster, lax.rem(shard + k, shards)), device_id_type=MESH)
        return 0

    def greet_cluster(k, _):
        pl.semaphore_signal(barrier, inc=1, device_id=(lax.rem(cluster + k, clusters), shard), device_id_type=MESH)
        return 0

    lax.fori_loop(1, shards, greet_shard, 0)
    lax.fori_loop(1, clusters, greet_cluster, 0)

    loads = [
        pltpu.make_async_copy(src, dst, load_sem.at[n])
        for n, (src, dst) in enumerate((
            (inc_path_hbm, inc_path), (capacity_hbm, capacity), (dual_start_hbm, dual_start),
            (path_count_hbm, path_count), (cluster_size_hbm, cluster_size), (flow_start_hbm, flow_start),
            (demand_hbm, demand), (utility_hbm, utility), (inc_edge_hbm, inc_edge), (partner_hbm, partner),
            (incidence_hbm, incidence)))]
    for copy in loads:
        copy.start()

    at_x = [lax.rem(shard // 8 + d, 4) * 8 for d in range(4)]
    at_z = [lax.rem(shard // 4 + d, 2) * 4 for d in range(2)]
    at_y = [lax.rem(shard + d, 4) for d in range(4)]
    near = [at_x[x] + at_z[z] + at_y[y] for x, z, y in NEAR]

    def other_end(index):
        return lax.rem(index // 8 + 2, 4) * 8 + lax.rem(index // 4 + 1, 2) * 4 + lax.rem(index + 2, 4)

    far = [other_end(index) for index in near]

    def send(src, dst, send_to, recv_to, peer):
        pltpu.make_async_remote_copy(
            src_ref=src, dst_ref=dst, send_sem=send_to, recv_sem=recv_to,
            device_id=(cluster, peer), device_id_type=MESH).start()

    def to_all(src, dst, send_to, recv_to):
        for u in FAR_FIRST:
            peer, place = (near[u], BACK[u]) if u < 16 else (far[u - 16], 16 + BACK[u - 16])
            send(src.at[u], dst.at[place], send_to, recv_to, peer)

    def to_near(src, dst, send_to, recv_to):
        for u in NEAR_FAR_FIRST:
            send(src.at[u], dst.at[BACK[u]], send_to, recv_to, near[u])

    def to_clusters(src, dst, send_to, recv_to):
        for k in (4, 3, 5, 2, 6, 1, 7):
            pltpu.make_async_remote_copy(
                src_ref=src, dst_ref=dst.at[cluster], send_sem=send_to, recv_sem=recv_to,
                device_id=(lax.rem(cluster + k, clusters), shard), device_id_type=MESH).start()
        dst[cluster] = src[...]

    def wait(dst, send_to, recv_to):
        whole = pltpu.make_async_remote_copy(
            src_ref=dst, dst_ref=dst, send_sem=send_to, recv_sem=recv_to,
            device_id=(cluster, far[0]), device_id_type=MESH)
        whole.wait_recv()
        whole.wait_send()

    tile_role = iota((8, 128), 0) >> 2
    rows, lanes = iota((128, 128), 0), iota((128, 128), 1)
    row_slot, row_half = (rows >> 1) & 1, rows & 1
    row_dev = jnp.concatenate([jnp.where(tile_role == 0, near[q], far[q]) for q in range(16)], axis=0)
    lane1 = iota((1, 128), 1)
    loads[0].wait()
    lane_path = jnp.full((1, 128), -1, I32)
    for i in range(incs):
        lane_path = jnp.where(lane1 == i, inc_path[i], lane_path)
    owner = (lane_path >> 4) == row_dev
    before = dot(owner.astype(F32), (rows < lanes).astype(F32))
    slot = owner & (before == row_slot.astype(F32))

    def fill(dst, x):
        for q in range(16):
            tile = x[q * 8:q * 8 + 8]
            dst[q] = tile
            dst[16 + q] = pltpu.roll(tile, 4, 0)

    wanted = jnp.sum(jnp.where(slot, (lane_path & 15) + 1, 0).astype(F32), axis=1, keepdims=True) - 1.0
    fill(ask_send, jnp.broadcast_to(wanted, (128, 128)))

    def border_first(ref):
        x = ref[...]
        return jnp.concatenate([x[interior:], jnp.zeros((8 - edges, x.shape[1]), F32), x[:interior]], axis=0)

    loads[1].wait()
    loads[2].wait()
    cap = border_first(capacity)
    dual = border_first(dual_start)
    edge_send[...] = jnp.concatenate([cap[:4], dual[:4]], axis=0)

    def halves(ref):
        x = ref[...]
        return jnp.concatenate([x[:, :128], x[:, 128:]], axis=0)

    for copy in loads[3:8]:
        copy.wait()
    row32 = iota((32, 128), 0)
    count = jnp.zeros((32, 128), I32)
    for b in range(blocks):
        count = jnp.where((row32 & 15) == b, path_count[b], count)
    live = (((row32 & 15) < cluster_size[0]) & ((row32 >> 4) * 128 + iota((32, 128), 1) < count)).astype(F32)
    top = halves(demand) * live
    start = jnp.minimum(jnp.maximum(halves(flow_start), 0.0), top)
    gain = halves(utility)
    start_send[...] = start
    rest_send[0] = top
    rest_send[1] = gain

    pl.semaphore_wait(barrier, shards + clusters - 2)
    send(start_send, start_recv, send_sem.at[4], start_sem, far[0])
    to_all(ask_send, ask_recv, send_sem.at[0], ask_sem)
    ask_recv[0] = ask_send[0]
    to_clusters(edge_send, edge_recv, send_sem.at[1], edge_sem)
    send(rest_send, rest_recv, send_sem.at[5], rest_sem, far[0])

    loads[8].wait()
    lane_q = iota((1, 512), 1)
    lane_edge = jnp.full((1, 512), -1, I32)
    for i in range(incs):
        lane_edge = jnp.where((lane_q >> 4) == i, (inc_edge[i] + (8 - interior)) & 7, lane_edge)
    spread = (iota((128, 512), 0) == (iota((128, 512), 1) >> 4)).astype(F32)
    fits = (lane_edge == (lane_q & 7)) & (((lane_q >> 3) & 1) == (iota((128, 512), 0) & 1))
    both = jnp.where(fits, dot(slot.astype(F32), spread), 0.0)
    slot_edge[...] = both.astype(BF16)
    slot_edge_t[...] = both.T.astype(BF16)

    loads[9].wait()
    partner_row = jnp.full((4, 128), -1, I32)
    for k in range(slots):
        partner_row = jnp.where(iota((4, 128), 0) == k, partner[0, k], partner_row)
    partner8 = jnp.concatenate([partner_row, partner_row], axis=0)

    loads[10].wait()

    def shrink(i, _):
        inc[pl.ds(pl.multiple_of(i * paths, paths), paths), :] = incidence[i].astype(BF16)
        return 0
    lax.fori_loop(0, incs, shrink, 0)

    wait(ask_recv.at[pl.ds(0, shards - 1)], send_sem.at[0], ask_sem)
    asked = ask_recv[...].reshape(256, 128)
    rows2, lanes2 = iota((256, 128), 0), iota((256, 128), 1)
    chosen = ((asked == (lanes2 & 15).astype(F32)) & (((lanes2 >> 4) & 1) == (rows2 & 1))
              & ((lanes2 >> 5) == ((rows2 >> 2) & 1))).astype(F32)
    choose[...] = chosen[:128].astype(BF16)
    choose_t[...] = chosen.T.astype(BF16)

    def share(flows):
        x = pick(choose[:, :64], flows)
        for q in range(16):
            flow_send[q] = x[q * 8:q * 8 + 8]
        to_near(flow_send, flow_recv, send_sem.at[2], flow_sem)
        flow_recv[0] = flow_send[0]

    def total_load(t):
        wait(flow_recv.at[pl.ds(0, 15)], send_sem.at[2], flow_sem)
        got = flow_recv[...].reshape(128, 128)
        parts = dot(slot_edge_t[...], jnp.concatenate(thirds(got), axis=1))
        columns = []
        for q in range(2 * incs):
            chunk = parts[q * 8:q * 8 + 8]
            columns.append(jnp.concatenate([chunk[:, :128], chunk[:, 128:256], chunk[:, 256:]], axis=0).astype(BF16))
        sums = dot(jnp.concatenate(columns, axis=1), inc[...])
        own = (sums[16:] + sums[8:16]) + sums[:8]
        border_send[...] = own[:4]
        to_clusters(border_send, border_recv.at[t], send_sem.at[3], border_sem.at[t])
        wait(border_recv.at[t, pl.ds(0, clusters - 1)], send_sem.at[3], border_sem.at[t])
        twin = jnp.zeros((4, 128), F32)
        for c in range(clusters):
            twin = twin + jnp.where(partner_row == c, border_recv[t, c], 0.0)
        return jnp.concatenate([own[:4] + twin, own[4:]], axis=0)

    def settle(load, duals):
        split = jnp.minimum(limit, load + duals)
        duals = (duals + load) - split
        return (load - split) + duals, duals

    wait(start_recv, send_sem.at[4], start_sem)
    flows = jnp.concatenate([start, start_recv[...]], axis=0)
    share(flows)

    wait(rest_recv, send_sem.at[5], rest_sem)
    top = jnp.concatenate([top, rest_recv[0]], axis=0)
    gain = jnp.concatenate([gain, rest_recv[1]], axis=0)
    wait(edge_recv.at[pl.ds(0, clusters - 1)], send_sem.at[1], edge_sem)
    twin = jnp.zeros((8, 128), F32)
    for c in range(clusters):
        twin = twin + jnp.where(partner8 == c, edge_recv[c], 0.0)
    limit = unit * jnp.concatenate([0.5 * (cap[:4] + twin[:4]), cap[4:]], axis=0)
    duals = jnp.concatenate([0.5 * (dual[:4] + twin[4:]), dual[4:]], axis=0)

    residual, duals = settle(total_load(0), duals)

    def iterate(t, carry):
        flows, residual, duals = carry
        turn = lax.rem(t, 2)
        parts = dot_nt(jnp.concatenate(thirds(residual), axis=0), inc[...])
        back = (parts[16:] + parts[8:16]) + parts[:8]
        back = jnp.concatenate([back[:, q * 128:q * 128 + 128] for q in range(2 * incs)], axis=0)
        fill(sum_send, pick(slot_edge[...], back))
        to_all(sum_send, sum_recv.at[turn], send_sem.at[0], sum_sem.at[turn])
        sum_recv[turn, 0] = sum_send[0]
        wait(sum_recv.at[turn, pl.ds(0, shards - 1)], send_sem.at[0], sum_sem.at[turn])
        grad = pick(choose_t[:64, :], sum_recv[turn].reshape(256, 128))
        flows = jnp.minimum(jnp.maximum(flows - step_size * (grad - gain), 0.0), top)
        share(flows)
        residual, duals = settle(total_load(t), duals)
        return flows, residual, duals

    flows, residual, duals = lax.fori_loop(1, ITERS + 1, iterate, (flows, residual, duals))
    flows_out[...] = jnp.concatenate([flows[:16], flows[16:32]], axis=1)
    duals_out[...] = jnp.concatenate([duals[4:], duals[:slots]], axis=0)


def body(flow_start, demand, utility, path_count, cluster_size, incidence, inc_path, inc_edge, capacity, dual_start, partner):
    blocks, paths = flow_start.shape
    incs, _, width = incidence.shape
    edges, slots = capacity.shape[0], partner.shape[1]
    clusters, shards = lax.axis_size("cluster"), lax.axis_size("shard")
    norm_bound = max(2, incs * incs * paths * width // (1024 * edges * blocks))
    unit = float(max(1, incs * paths // (160 * edges)))
    dims = (clusters, shards, blocks, paths, incs, edges, slots, norm_bound, unit)
    scalars = (path_count, cluster_size, inc_path, inc_edge, partner)
    arrays = (flow_start, demand, utility, incidence, capacity, dual_start)
    dma = pltpu.SemaphoreType.DMA
    message = pltpu.VMEM((shards, 8, 128), F32)
    near = pltpu.VMEM((16, 8, 128), F32)
    return pl.pallas_call(
        functools.partial(kernel, dims),
        out_shape=(jax.ShapeDtypeStruct(flow_start.shape, F32), jax.ShapeDtypeStruct(capacity.shape, F32)),
        in_specs=[pl.BlockSpec(memory_space=pltpu.HBM)] * (len(scalars) + len(arrays)),
        out_specs=[pl.BlockSpec(memory_space=pltpu.VMEM)] * 2,
        scratch_shapes=[pltpu.SMEM(x.shape, I32) for x in scalars] + [pltpu.VMEM(x.shape, F32) for x in arrays] + [
            pltpu.VMEM((incs * paths, width), BF16),
            pltpu.VMEM((128, 512), BF16),
            pltpu.VMEM((512, 128), BF16),
            pltpu.VMEM((128, 128), BF16),
            pltpu.VMEM((128, 256), BF16),
            message, message, near, near, message, pltpu.VMEM((2, shards, 8, 128), F32),
            pltpu.VMEM((8, 128), F32),
            pltpu.VMEM((clusters, 8, 128), F32),
            pltpu.VMEM((4, 128), F32),
            pltpu.VMEM((ITERS + 1, clusters, 4, 128), F32),
            pltpu.VMEM((32, 128), F32), pltpu.VMEM((32, 128), F32),
            pltpu.VMEM((2, 32, 128), F32), pltpu.VMEM((2, 32, 128), F32),
            dma((11,)), dma((6,)), dma(()), dma(()), dma((2,)), dma(()), dma((ITERS + 1,)), dma(()), dma(()),
        ],
        compiler_params=pltpu.CompilerParams(
            collective_id=0, has_side_effects=True, vmem_limit_bytes=40 * 1024 * 1024),
    )(*scalars, *arrays)


def solution(mesh):
    both = P(("cluster", "shard"))
    rows = P(("cluster", "shard"), None)
    return jax.shard_map(
        body,
        mesh=mesh,
        in_specs=(rows, rows, rows, both, P("cluster"), P(("cluster", "shard"), None, None), both, both, rows, rows, P("cluster", None)),
        out_specs=(rows, rows),
        check_vma=False,
    )
```

```python
import functools

import jax
import jax.numpy as jnp
from jax import lax
from jax.experimental import pallas as pl
from jax.experimental.pallas import tpu as pltpu
from jax.sharding import PartitionSpec as P

ITERS = 3
GRID = (4, 2, 4)
MESH = pl.DeviceIdType.MESH
F32, BF16, I32 = jnp.float32, jnp.bfloat16, jnp.int32


def iota(shape, axis):
    return lax.broadcasted_iota(I32, shape, axis)


def thirds(x):
    high = x.astype(BF16).astype(F32)
    rest = x - high
    mid = rest.astype(BF16).astype(F32)
    return high, mid, rest - mid


def dot(a, b):
    return jnp.dot(a.astype(BF16), b.astype(BF16), preferred_element_type=F32)


def dot_nt(a, b):
    dims = (((1,), (1,)), ((), ()))
    return lax.dot_general(a.astype(BF16), b.astype(BF16), dims, preferred_element_type=F32)


def pick(selector, x):
    high, mid, low = thirds(x)
    return (dot(selector, low) + dot(selector, mid)) + dot(selector, high)


def hops(offset):
    return sum(min(d, n - d) for d, n in zip(offset, GRID))


NEAR = sorted(((x, z, y) for x in range(4) for z in range(2) for y in range(4) if hops((x, z, y)) <= 2), key=hops)
BACK = [NEAR.index(tuple(-d % n for d, n in zip(offset, GRID))) for offset in NEAR]
FAR_FIRST = sorted(range(1, 32), key=lambda u: -(hops(NEAR[u]) if u < 16 else 5 - hops(NEAR[u - 16])))
NEAR_FAR_FIRST = [u for u in FAR_FIRST if u < 16]


def kernel(
    dims,
    path_count_hbm, cluster_size_hbm, inc_path_hbm, inc_edge_hbm, partner_hbm,
    flow_start_hbm, demand_hbm, utility_hbm, incidence_hbm, capacity_hbm, dual_start_hbm,
    flows_out, duals_out,
    path_count, cluster_size, inc_path, inc_edge, partner,
    flow_start, demand, utility, incidence, capacity, dual_start,
    inc, slot_edge, slot_edge_t, choose, choose_t,
    ask_send, ask_recv, flow_send, flow_recv, sum_send, sum_recv,
    edge_send, edge_recv, border_send, border_recv, start_send, start_recv, rest_send, rest_recv,
    load_sem, send_sem, ask_sem, flow_sem, sum_sem, edge_sem, border_sem, start_sem, rest_sem,
):
    clusters, shards, blocks, paths, incs, edges, slots, norm_bound, unit = dims
    step_size = 1.0 / (2.0 * norm_bound)
    cluster, shard = lax.axis_index("cluster"), lax.axis_index("shard")
    interior = edges - slots

    barrier = pltpu.get_barrier_semaphore()

    def greet_shard(k, _):
        pl.semaphore_signal(barrier, inc=1, device_id=(cluster, lax.rem(shard + k, shards)), device_id_type=MESH)
        return 0

    def greet_cluster(k, _):
        pl.semaphore_signal(barrier, inc=1, device_id=(lax.rem(cluster + k, clusters), shard), device_id_type=MESH)
        return 0

    lax.fori_loop(1, shards, greet_shard, 0)
    lax.fori_loop(1, clusters, greet_cluster, 0)

    loads = [
        pltpu.make_async_copy(src, dst, load_sem.at[n])
        for n, (src, dst) in enumerate((
            (inc_path_hbm, inc_path), (capacity_hbm, capacity), (dual_start_hbm, dual_start),
            (path_count_hbm, path_count), (cluster_size_hbm, cluster_size), (flow_start_hbm, flow_start),
            (demand_hbm, demand), (utility_hbm, utility), (inc_edge_hbm, inc_edge), (partner_hbm, partner),
            (incidence_hbm, incidence)))]
    for copy in loads:
        copy.start()

    at_x = [lax.rem(shard // 8 + d, 4) * 8 for d in range(4)]
    at_z = [lax.rem(shard // 4 + d, 2) * 4 for d in range(2)]
    at_y = [lax.rem(shard + d, 4) for d in range(4)]
    near = [at_x[x] + at_z[z] + at_y[y] for x, z, y in NEAR]

    def other_end(index):
        return lax.rem(index // 8 + 2, 4) * 8 + lax.rem(index // 4 + 1, 2) * 4 + lax.rem(index + 2, 4)

    far = [other_end(index) for index in near]

    def send(src, dst, send_to, recv_to, peer):
        pltpu.make_async_remote_copy(
            src_ref=src, dst_ref=dst, send_sem=send_to, recv_sem=recv_to,
            device_id=(cluster, peer), device_id_type=MESH).start()

    def to_all(src, dst, send_to, recv_to):
        for u in FAR_FIRST:
            peer, place = (near[u], BACK[u]) if u < 16 else (far[u - 16], 16 + BACK[u - 16])
            send(src.at[u], dst.at[place], send_to, recv_to, peer)

    def to_near(src, dst, send_to, recv_to):
        for u in NEAR_FAR_FIRST:
            send(src.at[u], dst.at[BACK[u]], send_to, recv_to, near[u])

    def to_clusters(src, dst, send_to, recv_to):
        for k in (4, 3, 5, 2, 6, 1, 7):
            pltpu.make_async_remote_copy(
                src_ref=src, dst_ref=dst.at[cluster], send_sem=send_to, recv_sem=recv_to,
                device_id=(lax.rem(cluster + k, clusters), shard), device_id_type=MESH).start()
        dst[cluster] = src[...]

    def wait(dst, send_to, recv_to):
        whole = pltpu.make_async_remote_copy(
            src_ref=dst, dst_ref=dst, send_sem=send_to, recv_sem=recv_to,
            device_id=(cluster, far[0]), device_id_type=MESH)
        whole.wait_recv()
        whole.wait_send()

    tile_role = iota((8, 128), 0) >> 2
    rows, lanes = iota((128, 128), 0), iota((128, 128), 1)
    row_slot, row_half = (rows >> 1) & 1, rows & 1
    row_dev = jnp.concatenate([jnp.where(tile_role == 0, near[q], far[q]) for q in range(16)], axis=0)
    lane1 = iota((1, 128), 1)
    loads[0].wait()
    lane_path = jnp.full((1, 128), -1, I32)
    for i in range(incs):
        lane_path = jnp.where(lane1 == i, inc_path[i], lane_path)
    owner = (lane_path >> 4) == row_dev
    before = dot(owner.astype(F32), (rows < lanes).astype(F32))
    slot = owner & (before == row_slot.astype(F32))

    def fill(dst, x):
        for q in range(16):
            tile = x[q * 8:q * 8 + 8]
            dst[q] = tile
            dst[16 + q] = pltpu.roll(tile, 4, 0)

    wanted = jnp.sum(jnp.where(slot, (lane_path & 15) + 1, 0).astype(F32), axis=1, keepdims=True) - 1.0
    fill(ask_send, jnp.broadcast_to(wanted, (128, 128)))

    def border_first(ref):
        x = ref[...]
        return jnp.concatenate([x[interior:], jnp.zeros((8 - edges, x.shape[1]), F32), x[:interior]], axis=0)

    loads[1].wait()
    loads[2].wait()
    cap = border_first(capacity)
    dual = border_first(dual_start)
    edge_send[...] = jnp.concatenate([cap[:4], dual[:4]], axis=0)

    def halves(ref):
        x = ref[...]
        return jnp.concatenate([x[:, :128], x[:, 128:]], axis=0)

    for copy in loads[3:8]:
        copy.wait()
    row32 = iota((32, 128), 0)
    count = jnp.zeros((32, 128), I32)
    for b in range(blocks):
        count = jnp.where((row32 & 15) == b, path_count[b], count)
    live = (((row32 & 15) < cluster_size[0]) & ((row32 >> 4) * 128 + iota((32, 128), 1) < count)).astype(F32)
    top = halves(demand) * live
    start = jnp.minimum(jnp.maximum(halves(flow_start), 0.0), top)
    gain = halves(utility)
    start_send[...] = start
    rest_send[0] = top
    rest_send[1] = gain

    pl.semaphore_wait(barrier, shards + clusters - 2)
    send(start_send, start_recv, send_sem.at[4], start_sem, far[0])
    to_all(ask_send, ask_recv, send_sem.at[0], ask_sem)
    ask_recv[0] = ask_send[0]
    to_clusters(edge_send, edge_recv, send_sem.at[1], edge_sem)
    send(rest_send, rest_recv, send_sem.at[5], rest_sem, far[0])

    loads[8].wait()
    lane_q = iota((1, 512), 1)
    lane_edge = jnp.full((1, 512), -1, I32)
    for i in range(incs):
        lane_edge = jnp.where((lane_q >> 4) == i, (inc_edge[i] + (8 - interior)) & 7, lane_edge)
    spread = (iota((128, 512), 0) == (iota((128, 512), 1) >> 4)).astype(F32)
    fits = (lane_edge == (lane_q & 7)) & (((lane_q >> 3) & 1) == (iota((128, 512), 0) & 1))
    both = jnp.where(fits, dot(slot.astype(F32), spread), 0.0)
    slot_edge[...] = both.astype(BF16)
    slot_edge_t[...] = both.T.astype(BF16)

    loads[9].wait()
    partner_row = jnp.full((4, 128), -1, I32)
    for k in range(slots):
        partner_row = jnp.where(iota((4, 128), 0) == k, partner[0, k], partner_row)
    partner8 = jnp.concatenate([partner_row, partner_row], axis=0)

    loads[10].wait()

    def shrink(i, _):
        inc[pl.ds(pl.multiple_of(i * paths, paths), paths), :] = incidence[i].astype(BF16)
        return 0
    lax.fori_loop(0, incs, shrink, 0)

    wait(ask_recv.at[pl.ds(0, shards - 1)], send_sem.at[0], ask_sem)
    asked = ask_recv[...].reshape(256, 128)
    rows2, lanes2 = iota((256, 128), 0), iota((256, 128), 1)
    chosen = ((asked == (lanes2 & 15).astype(F32)) & (((lanes2 >> 4) & 1) == (rows2 & 1))
              & ((lanes2 >> 5) == ((rows2 >> 2) & 1))).astype(F32)
    choose[...] = chosen[:128].astype(BF16)
    choose_t[...] = chosen.T.astype(BF16)

    def share(flows):
        x = pick(choose[:, :64], flows)
        for q in range(16):
            flow_send[q] = x[q * 8:q * 8 + 8]
        to_near(flow_send, flow_recv, send_sem.at[2], flow_sem)
        flow_recv[0] = flow_send[0]

    def total_load(t):
        wait(flow_recv.at[pl.ds(0, 15)], send_sem.at[2], flow_sem)
        got = flow_recv[...].reshape(128, 128)
        parts = dot(slot_edge_t[...], jnp.concatenate(thirds(got), axis=1))
        columns = []
        for q in range(2 * incs):
            chunk = parts[q * 8:q * 8 + 8]
            columns.append(jnp.concatenate([chunk[:, :128], chunk[:, 128:256], chunk[:, 256:]], axis=0).astype(BF16))
        sums = dot(jnp.concatenate(columns, axis=1), inc[...])
        own = (sums[16:] + sums[8:16]) + sums[:8]
        border_send[...] = own[:4]
        to_clusters(border_send, border_recv.at[t], send_sem.at[3], border_sem.at[t])
        wait(border_recv.at[t, pl.ds(0, clusters - 1)], send_sem.at[3], border_sem.at[t])
        twin = jnp.zeros((4, 128), F32)
        for c in range(clusters):
            twin = twin + jnp.where(partner_row == c, border_recv[t, c], 0.0)
        return jnp.concatenate([own[:4] + twin, own[4:]], axis=0)

    def settle(load, duals):
        split = jnp.minimum(limit, load + duals)
        duals = (duals + load) - split
        return (load - split) + duals, duals

    wait(start_recv, send_sem.at[4], start_sem)
    flows = jnp.concatenate([start, start_recv[...]], axis=0)
    share(flows)

    wait(rest_recv, send_sem.at[5], rest_sem)
    top = jnp.concatenate([top, rest_recv[0]], axis=0)
    gain = jnp.concatenate([gain, rest_recv[1]], axis=0)
    wait(edge_recv.at[pl.ds(0, clusters - 1)], send_sem.at[1], edge_sem)
    twin = jnp.zeros((8, 128), F32)
    for c in range(clusters):
        twin = twin + jnp.where(partner8 == c, edge_recv[c], 0.0)
    limit = unit * jnp.concatenate([0.5 * (cap[:4] + twin[:4]), cap[4:]], axis=0)
    duals = jnp.concatenate([0.5 * (dual[:4] + twin[4:]), dual[4:]], axis=0)

    residual, duals = settle(total_load(0), duals)

    def iterate(t, carry):
        flows, residual, duals = carry
        turn = lax.rem(t, 2)
        parts = dot_nt(jnp.concatenate(thirds(residual), axis=0), inc[...])
        back = (parts[16:] + parts[8:16]) + parts[:8]
        back = jnp.concatenate([back[:, q * 128:q * 128 + 128] for q in range(2 * incs)], axis=0)
        fill(sum_send, pick(slot_edge[...], back))
        to_all(sum_send, sum_recv.at[turn], send_sem.at[0], sum_sem.at[turn])
        sum_recv[turn, 0] = sum_send[0]
        wait(sum_recv.at[turn, pl.ds(0, shards - 1)], send_sem.at[0], sum_sem.at[turn])
        grad = pick(choose_t[:64, :], sum_recv[turn].reshape(256, 128))
        flows = jnp.minimum(jnp.maximum(flows - step_size * (grad - gain), 0.0), top)
        share(flows)
        residual, duals = settle(total_load(t), duals)
        return flows, residual, duals

    flows, residual, duals = lax.fori_loop(1, ITERS + 1, iterate, (flows, residual, duals))
    flows_out[...] = jnp.concatenate([flows[:16], flows[16:32]], axis=1)
    duals_out[...] = jnp.concatenate([duals[4:], duals[:slots]], axis=0)


def body(flow_start, demand, utility, path_count, cluster_size, incidence, inc_path, inc_edge, capacity, dual_start, partner):
    blocks, paths = flow_start.shape
    incs, _, width = incidence.shape
    edges, slots = capacity.shape[0], partner.shape[1]
    clusters, shards = lax.axis_size("cluster"), lax.axis_size("shard")
    norm_bound = max(2, incs * incs * paths * width // (1024 * edges * blocks))
    unit = float(max(1, incs * paths // (160 * edges)))
    dims = (clusters, shards, blocks, paths, incs, edges, slots, norm_bound, unit)
    scalars = (path_count, cluster_size, inc_path, inc_edge, partner)
    arrays = (flow_start, demand, utility, incidence, capacity, dual_start)
    dma = pltpu.SemaphoreType.DMA
    message = pltpu.VMEM((shards, 8, 128), F32)
    near = pltpu.VMEM((16, 8, 128), F32)
    return pl.pallas_call(
        functools.partial(kernel, dims),
        out_shape=(jax.ShapeDtypeStruct(flow_start.shape, F32), jax.ShapeDtypeStruct(capacity.shape, F32)),
        in_specs=[pl.BlockSpec(memory_space=pltpu.HBM)] * (len(scalars) + len(arrays)),
        out_specs=[pl.BlockSpec(memory_space=pltpu.VMEM)] * 2,
        scratch_shapes=[pltpu.SMEM(x.shape, I32) for x in scalars] + [pltpu.VMEM(x.shape, F32) for x in arrays] + [
            pltpu.VMEM((incs * paths, width), BF16),
            pltpu.VMEM((128, 512), BF16),
            pltpu.VMEM((512, 128), BF16),
            pltpu.VMEM((128, 128), BF16),
            pltpu.VMEM((128, 256), BF16),
            message, message, near, near, message, pltpu.VMEM((2, shards, 8, 128), F32),
            pltpu.VMEM((8, 128), F32),
            pltpu.VMEM((clusters, 8, 128), F32),
            pltpu.VMEM((4, 128), F32),
            pltpu.VMEM((ITERS + 1, clusters, 4, 128), F32),
            pltpu.VMEM((32, 128), F32), pltpu.VMEM((32, 128), F32),
            pltpu.VMEM((2, 32, 128), F32), pltpu.VMEM((2, 32, 128), F32),
            dma((11,)), dma((6,)), dma(()), dma(()), dma((2,)), dma(()), dma((ITERS + 1,)), dma(()), dma(()),
        ],
        compiler_params=pltpu.CompilerParams(
            collective_id=0, has_side_effects=True, vmem_limit_bytes=60 * 1024 * 1024),
    )(*scalars, *arrays)


def solution(mesh):
    both = P(("cluster", "shard"))
    rows = P(("cluster", "shard"), None)
    return jax.shard_map(
        body,
        mesh=mesh,
        in_specs=(rows, rows, rows, both, P("cluster"), P(("cluster", "shard"), None, None), both, both, rows, rows, P("cluster", None)),
        out_specs=(rows, rows),
        check_vma=False,
    )
```

```python
import functools

import jax
import jax.numpy as jnp
from jax import lax
from jax.experimental import pallas as pl
from jax.experimental.pallas import tpu as pltpu
from jax.sharding import PartitionSpec as P

ITERS = 3
GRID = (4, 2, 4)
MESH = pl.DeviceIdType.MESH
F32, BF16, I32 = jnp.float32, jnp.bfloat16, jnp.int32


def iota(shape, axis):
    return lax.broadcasted_iota(I32, shape, axis)


def thirds(x):
    high = x.astype(BF16).astype(F32)
    rest = x - high
    mid = rest.astype(BF16).astype(F32)
    return high, mid, rest - mid


def dot(a, b):
    return jnp.dot(a.astype(BF16), b.astype(BF16), preferred_element_type=F32)


def pick(selector, x):
    high, mid, low = thirds(x)
    return (dot(selector, low) + dot(selector, mid)) + dot(selector, high)


def hops(offset):
    return sum(min(d, n - d) for d, n in zip(offset, GRID))


NEAR = sorted(((x, z, y) for x in range(4) for z in range(2) for y in range(4) if hops((x, z, y)) <= 2), key=hops)
BACK = [NEAR.index(tuple(-d % n for d, n in zip(offset, GRID))) for offset in NEAR]
FAR_FIRST = sorted(range(1, 32), key=lambda u: -(hops(NEAR[u]) if u < 16 else 5 - hops(NEAR[u - 16])))
NEAR_FAR_FIRST = [u for u in FAR_FIRST if u < 16]


def kernel(
    dims,
    cluster_size, path_count_hbm, inc_path_hbm, inc_edge_hbm, partner_hbm,
    flow_start_hbm, demand_hbm, utility_hbm, incidence_hbm, capacity_hbm, dual_start_hbm,
    flows_out, duals_out,
    path_count, inc_path, inc_edge, partner,
    flow_start, demand, utility, incidence, capacity, dual_start,
    inc, inc_t, slot_edge, slot_edge_t, choose, choose_t,
    ask_send, ask_recv, flow_send, flow_recv, sum_send, sum_recv,
    edge_send, edge_recv, border_send, border_recv, start_send, start_recv, rest_send, rest_recv,
    load_sem, send_sem, ask_sem, flow_sem, sum_sem, edge_sem, border_sem, start_sem, rest_sem,
):
    clusters, shards, blocks, paths, incs, edges, slots, norm_bound, unit = dims
    step_size = 1.0 / (2.0 * norm_bound)
    cluster, shard = lax.axis_index("cluster"), lax.axis_index("shard")
    interior = edges - slots

    barrier = pltpu.get_barrier_semaphore()

    def greet_shard(k, _):
        pl.semaphore_signal(barrier, inc=1, device_id=(cluster, lax.rem(shard + k, shards)), device_id_type=MESH)
        return 0

    def greet_cluster(k, _):
        pl.semaphore_signal(barrier, inc=1, device_id=(lax.rem(cluster + k, clusters), shard), device_id_type=MESH)
        return 0

    lax.fori_loop(1, shards, greet_shard, 0)
    lax.fori_loop(1, clusters, greet_cluster, 0)

    loads = [
        pltpu.make_async_copy(src, dst, load_sem.at[n])
        for n, (src, dst) in enumerate((
            (inc_path_hbm, inc_path), (capacity_hbm, capacity), (dual_start_hbm, dual_start),
            (path_count_hbm, path_count), (flow_start_hbm, flow_start),
            (demand_hbm, demand), (utility_hbm, utility), (inc_edge_hbm, inc_edge), (partner_hbm, partner),
            (incidence_hbm, incidence)))]
    for copy in loads:
        copy.start()

    at_x = [lax.rem(shard // 8 + d, 4) * 8 for d in range(4)]
    at_z = [lax.rem(shard // 4 + d, 2) * 4 for d in range(2)]
    at_y = [lax.rem(shard + d, 4) for d in range(4)]
    near = [at_x[x] + at_z[z] + at_y[y] for x, z, y in NEAR]

    def other_end(index):
        return lax.rem(index // 8 + 2, 4) * 8 + lax.rem(index // 4 + 1, 2) * 4 + lax.rem(index + 2, 4)

    far = [other_end(index) for index in near]

    def send(src, dst, send_to, recv_to, peer):
        pltpu.make_async_remote_copy(
            src_ref=src, dst_ref=dst, send_sem=send_to, recv_sem=recv_to,
            device_id=(cluster, peer), device_id_type=MESH).start()

    def to_all(src, dst, send_to, recv_to):
        for u in FAR_FIRST:
            peer, place = (near[u], BACK[u]) if u < 16 else (far[u - 16], 16 + BACK[u - 16])
            send(src.at[u], dst.at[place], send_to, recv_to, peer)

    def to_near(src, dst, send_to, recv_to):
        for u in NEAR_FAR_FIRST:
            send(src.at[u], dst.at[BACK[u]], send_to, recv_to, near[u])

    def to_clusters(src, dst, send_to, recv_to):
        for k in (4, 3, 5, 2, 6, 1, 7):
            pltpu.make_async_remote_copy(
                src_ref=src, dst_ref=dst.at[cluster], send_sem=send_to, recv_sem=recv_to,
                device_id=(lax.rem(cluster + k, clusters), shard), device_id_type=MESH).start()
        dst[cluster] = src[...]

    def wait(dst, send_to, recv_to):
        whole = pltpu.make_async_remote_copy(
            src_ref=dst, dst_ref=dst, send_sem=send_to, recv_sem=recv_to,
            device_id=(cluster, far[0]), device_id_type=MESH)
        whole.wait_recv()
        whole.wait_send()

    tile_role = iota((8, 128), 0) >> 2
    rows, lanes = iota((128, 128), 0), iota((128, 128), 1)
    row_slot, row_half = (rows >> 1) & 1, rows & 1
    row_dev = jnp.concatenate([jnp.where(tile_role == 0, near[q], far[q]) for q in range(16)], axis=0)
    lane1 = iota((1, 128), 1)
    loads[0].wait()
    lane_path = jnp.full((1, 128), -1, I32)
    for i in range(incs):
        lane_path = jnp.where(lane1 == i, inc_path[i], lane_path)
    owner = (lane_path >> 4) == row_dev
    before = dot(owner.astype(F32), (rows < lanes).astype(F32))
    slot = owner & (before == row_slot.astype(F32))

    def fill(dst, x):
        for q in range(16):
            tile = x[q * 8:q * 8 + 8]
            dst[q] = tile
            dst[16 + q] = pltpu.roll(tile, 4, 0)

    wanted = jnp.sum(jnp.where(slot, (lane_path & 15) + 1, 0).astype(F32), axis=1, keepdims=True) - 1.0
    fill(ask_send, jnp.broadcast_to(wanted, (128, 128)))

    def border_first(ref):
        x = ref[...]
        return jnp.concatenate([x[interior:], jnp.zeros((8 - edges, x.shape[1]), F32), x[:interior]], axis=0)

    loads[1].wait()
    loads[2].wait()
    cap = border_first(capacity)
    dual = border_first(dual_start)
    edge_send[...] = jnp.concatenate([cap[:4], dual[:4]], axis=0)

    def halves(ref):
        x = ref[...]
        return jnp.concatenate([x[:, :128], x[:, 128:]], axis=0)

    for copy in loads[3:7]:
        copy.wait()
    row32 = iota((32, 128), 0)
    count = jnp.zeros((32, 128), I32)
    for b in range(blocks):
        count = jnp.where((row32 & 15) == b, path_count[b], count)
    live = (((row32 & 15) < cluster_size[0]) & ((row32 >> 4) * 128 + iota((32, 128), 1) < count)).astype(F32)
    top = halves(demand) * live
    start = jnp.minimum(jnp.maximum(halves(flow_start), 0.0), top)
    gain = halves(utility)
    start_send[...] = start
    rest_send[0] = top
    rest_send[1] = gain

    pl.semaphore_wait(barrier, shards + clusters - 2)
    send(start_send, start_recv, send_sem.at[4], start_sem, far[0])
    to_all(ask_send, ask_recv, send_sem.at[0], ask_sem)
    ask_recv[0] = ask_send[0]
    to_clusters(edge_send, edge_recv, send_sem.at[1], edge_sem)
    send(rest_send, rest_recv, send_sem.at[5], rest_sem, far[0])

    loads[7].wait()
    lane_q = iota((1, 512), 1)
    lane_edge = jnp.full((1, 512), -1, I32)
    for i in range(incs):
        lane_edge = jnp.where((lane_q >> 4) == i, (inc_edge[i] + (8 - interior)) & 7, lane_edge)
    spread = (iota((128, 512), 0) == (iota((128, 512), 1) >> 4)).astype(F32)
    fits = (lane_edge == (lane_q & 7)) & (((lane_q >> 3) & 1) == (iota((128, 512), 0) & 1))
    both = jnp.where(fits, dot(slot.astype(F32), spread), 0.0)
    slot_edge[...] = both.astype(BF16)
    slot_edge_t[...] = both.T.astype(BF16)

    loads[8].wait()
    partner_row = jnp.full((4, 128), -1, I32)
    for k in range(slots):
        partner_row = jnp.where(iota((4, 128), 0) == k, partner[0, k], partner_row)
    partner8 = jnp.concatenate([partner_row, partner_row], axis=0)

    loads[9].wait()

    def shrink(i, _):
        at = pl.ds(pl.multiple_of(i * paths, paths), paths)
        block = incidence[i].astype(BF16)
        inc[at, :] = block
        inc_t[:, at] = block.T
        return 0
    lax.fori_loop(0, incs, shrink, 0)

    wait(ask_recv.at[pl.ds(0, shards - 1)], send_sem.at[0], ask_sem)
    asked = ask_recv[...].reshape(256, 128)
    rows2, lanes2 = iota((256, 128), 0), iota((256, 128), 1)
    chosen = ((asked == (lanes2 & 15).astype(F32)) & (((lanes2 >> 4) & 1) == (rows2 & 1))
              & ((lanes2 >> 5) == ((rows2 >> 2) & 1))).astype(F32)
    choose[...] = chosen[:128].astype(BF16)
    choose_t[...] = chosen.T.astype(BF16)

    def share(flows):
        x = pick(choose[:, :64], flows)
        for q in range(16):
            flow_send[q] = x[q * 8:q * 8 + 8]
        to_near(flow_send, flow_recv, send_sem.at[2], flow_sem)
        flow_recv[0] = flow_send[0]

    def total_load(t):
        wait(flow_recv.at[pl.ds(0, 15)], send_sem.at[2], flow_sem)
        got = flow_recv[...].reshape(128, 128)
        parts = dot(slot_edge_t[...], jnp.concatenate(thirds(got), axis=1))
        columns = []
        for q in range(2 * incs):
            chunk = parts[q * 8:q * 8 + 8]
            columns.append(jnp.concatenate([chunk[:, :128], chunk[:, 128:256], chunk[:, 256:]], axis=0).astype(BF16))
        sums = dot(jnp.concatenate(columns, axis=1), inc[...])
        own = (sums[16:] + sums[8:16]) + sums[:8]
        border_send[...] = own[:4]
        to_clusters(border_send, border_recv.at[t], send_sem.at[3], border_sem.at[t])
        wait(border_recv.at[t, pl.ds(0, clusters - 1)], send_sem.at[3], border_sem.at[t])
        twin = jnp.zeros((4, 128), F32)
        for c in range(clusters):
            twin = twin + jnp.where(partner_row == c, border_recv[t, c], 0.0)
        return jnp.concatenate([own[:4] + twin, own[4:]], axis=0)

    def settle(load, duals):
        split = jnp.minimum(limit, load + duals)
        duals = (duals + load) - split
        return (load - split) + duals, duals

    wait(start_recv, send_sem.at[4], start_sem)
    flows = jnp.concatenate([start, start_recv[...]], axis=0)
    share(flows)

    wait(rest_recv, send_sem.at[5], rest_sem)
    top = jnp.concatenate([top, rest_recv[0]], axis=0)
    gain = jnp.concatenate([gain, rest_recv[1]], axis=0)
    wait(edge_recv.at[pl.ds(0, clusters - 1)], send_sem.at[1], edge_sem)
    twin = jnp.zeros((8, 128), F32)
    for c in range(clusters):
        twin = twin + jnp.where(partner8 == c, edge_recv[c], 0.0)
    limit = unit * jnp.concatenate([0.5 * (cap[:4] + twin[:4]), cap[4:]], axis=0)
    duals = jnp.concatenate([0.5 * (dual[:4] + twin[4:]), dual[4:]], axis=0)

    residual, duals = settle(total_load(0), duals)

    def iterate(t, carry):
        flows, residual, duals = carry
        turn = lax.rem(t, 2)
        parts = dot(jnp.concatenate(thirds(residual), axis=0), inc_t[...])
        back = (parts[16:] + parts[8:16]) + parts[:8]
        back = jnp.concatenate([back[:, q * 128:q * 128 + 128] for q in range(2 * incs)], axis=0)
        fill(sum_send, pick(slot_edge[...], back))
        to_all(sum_send, sum_recv.at[turn], send_sem.at[0], sum_sem.at[turn])
        sum_recv[turn, 0] = sum_send[0]
        wait(sum_recv.at[turn, pl.ds(0, shards - 1)], send_sem.at[0], sum_sem.at[turn])
        grad = pick(choose_t[:64, :], sum_recv[turn].reshape(256, 128))
        flows = jnp.minimum(jnp.maximum(flows - step_size * (grad - gain), 0.0), top)
        share(flows)
        residual, duals = settle(total_load(t), duals)
        return flows, residual, duals

    flows, residual, duals = lax.fori_loop(1, ITERS + 1, iterate, (flows, residual, duals))
    flows_out[...] = jnp.concatenate([flows[:16], flows[16:32]], axis=1)
    duals_out[...] = jnp.concatenate([duals[4:], duals[:slots]], axis=0)


def write_out(flows, duals, flows_out, duals_out, sems):
    copies = [pltpu.make_async_copy(flows, flows_out, sems.at[0]), pltpu.make_async_copy(duals, duals_out, sems.at[1])]
    for copy in copies:
        copy.start()
    for copy in copies:
        copy.wait()


def body(flow_start, demand, utility, path_count, cluster_size, incidence, inc_path, inc_edge, capacity, dual_start, partner):
    blocks, paths = flow_start.shape
    incs, _, width = incidence.shape
    edges, slots = capacity.shape[0], partner.shape[1]
    clusters, shards = lax.axis_size("cluster"), lax.axis_size("shard")
    norm_bound = max(2, incs * incs * paths * width // (1024 * edges * blocks))
    unit = float(max(1, incs * paths // (160 * edges)))
    dims = (clusters, shards, blocks, paths, incs, edges, slots, norm_bound, unit)
    scalars = (path_count, inc_path, inc_edge, partner)
    arrays = (flow_start, demand, utility, incidence, capacity, dual_start)
    dma = pltpu.SemaphoreType.DMA
    message = pltpu.VMEM((shards, 8, 128), F32)
    near = pltpu.VMEM((16, 8, 128), F32)
    results = pl.pallas_call(
        functools.partial(kernel, dims),
        out_shape=(pltpu.VMEM(flow_start.shape, F32), pltpu.VMEM(capacity.shape, F32)),
        in_specs=[pl.BlockSpec(memory_space=pltpu.SMEM)] + [pl.BlockSpec(memory_space=pltpu.HBM)] * (len(scalars) + len(arrays)),
        out_specs=[pl.BlockSpec(memory_space=pltpu.VMEM)] * 2,
        scratch_shapes=[pltpu.SMEM(x.shape, I32) for x in scalars] + [pltpu.VMEM(x.shape, F32) for x in arrays] + [
            pltpu.VMEM((incs * paths, width), BF16),
            pltpu.VMEM((width, incs * paths), BF16),
            pltpu.VMEM((128, 512), BF16),
            pltpu.VMEM((512, 128), BF16),
            pltpu.VMEM((128, 128), BF16),
            pltpu.VMEM((128, 256), BF16),
            message, message, near, near, message, pltpu.VMEM((2, shards, 8, 128), F32),
            pltpu.VMEM((8, 128), F32),
            pltpu.VMEM((clusters, 8, 128), F32),
            pltpu.VMEM((4, 128), F32),
            pltpu.VMEM((ITERS + 1, clusters, 4, 128), F32),
            pltpu.VMEM((32, 128), F32), pltpu.VMEM((32, 128), F32),
            pltpu.VMEM((2, 32, 128), F32), pltpu.VMEM((2, 32, 128), F32),
            dma((10,)), dma((6,)), dma(()), dma(()), dma((2,)), dma(()), dma((ITERS + 1,)), dma(()), dma(()),
        ],
        compiler_params=pltpu.CompilerParams(
            collective_id=0, has_side_effects=True, vmem_limit_bytes=24 * 1024 * 1024),
    )(cluster_size, *(pltpu.with_memory_space_constraint(x, pltpu.HBM) for x in scalars + arrays))
    return pl.pallas_call(
        write_out,
        out_shape=(jax.ShapeDtypeStruct(flow_start.shape, F32), jax.ShapeDtypeStruct(capacity.shape, F32)),
        in_specs=[pl.BlockSpec(memory_space=pltpu.VMEM)] * 2,
        out_specs=[pl.BlockSpec(memory_space=pltpu.HBM)] * 2,
        scratch_shapes=[dma((2,))],
    )(*(pltpu.with_memory_space_constraint(x, pltpu.VMEM) for x in results))


def solution(mesh):
    both = P(("cluster", "shard"))
    rows = P(("cluster", "shard"), None)
    return jax.shard_map(
        body,
        mesh=mesh,
        in_specs=(rows, rows, rows, both, P("cluster"), P(("cluster", "shard"), None, None), both, both, rows, rows, P("cluster", None)),
        out_specs=(rows, rows),
        check_vma=False,
    )
```

```python
import functools

import jax
import jax.numpy as jnp
from jax import lax
from jax.experimental import pallas as pl
from jax.experimental.pallas import tpu as pltpu
from jax.sharding import PartitionSpec as P

ITERS = 3
GRID = (4, 2, 4)
MESH = pl.DeviceIdType.MESH
F32, BF16, I32 = jnp.float32, jnp.bfloat16, jnp.int32


def iota(shape, axis):
    return lax.broadcasted_iota(I32, shape, axis)


def thirds(x):
    high = x.astype(BF16).astype(F32)
    rest = x - high
    mid = rest.astype(BF16).astype(F32)
    return high, mid, rest - mid


def dot(a, b):
    return jnp.dot(a.astype(BF16), b.astype(BF16), preferred_element_type=F32)


def pick(selector, x):
    high, mid, low = thirds(x)
    return (dot(selector, low) + dot(selector, mid)) + dot(selector, high)


def hops(offset):
    return sum(min(d, n - d) for d, n in zip(offset, GRID))


NEAR = sorted(((x, z, y) for x in range(4) for z in range(2) for y in range(4) if hops((x, z, y)) <= 2), key=hops)
BACK = [NEAR.index(tuple(-d % n for d, n in zip(offset, GRID))) for offset in NEAR]
FAR_FIRST = sorted(range(1, 32), key=lambda u: -(hops(NEAR[u]) if u < 16 else 5 - hops(NEAR[u - 16])))
NEAR_FAR_FIRST = [u for u in FAR_FIRST if u < 16]


def kernel(
    dims,
    cluster_size, path_count_hbm, inc_path_hbm, inc_edge_hbm, partner_hbm,
    flow_start_hbm, demand_hbm, utility_hbm, incidence_hbm, capacity_hbm, dual_start_hbm,
    flows_out, duals_out,
    path_count, inc_path, inc_edge, partner,
    flow_start, demand, utility, incidence, capacity, dual_start,
    inc, inc_t, slot_edge, slot_edge_t, choose, choose_t,
    ask_send, ask_recv, flow_send, flow_recv, sum_send, sum_recv,
    edge_send, edge_recv, border_send, border_recv, own_start, own_bounds, state, bounds, final,
    load_sem, spread_send, share_send, edge_sent, border_sent, start_sent, bounds_sent, final_sent,
    ask_sem, flow_sem, sum_sem, edge_sem, border_sem, start_sem, bounds_sem, final_sem,
):
    clusters, shards, blocks, paths, incs, edges, slots, norm_bound, unit = dims
    step_size = 1.0 / (2.0 * norm_bound)
    cluster, shard = lax.axis_index("cluster"), lax.axis_index("shard")
    interior = edges - slots

    core = lax.rem(cluster, 2)
    even = cluster - core
    host = even + 1

    barrier = pltpu.get_barrier_semaphore()

    def greet(peer_cluster, peer_shard):
        pl.semaphore_signal(barrier, inc=1, device_id=(peer_cluster, peer_shard), device_id_type=MESH)

    def greet_hosts(k, _):
        greet(host, lax.rem(shard + k, shards))
        return 0

    def greet_even(k, _):
        greet(even, lax.rem(shard + k, shards))
        return 0

    def greet_cluster(k, _):
        greet(lax.rem(cluster + k + 1 - core, clusters), shard)
        return 0

    lax.fori_loop(1, shards, greet_hosts, 0)

    @pl.when(core == 0)
    def _():
        greet(host, shard)

    @pl.when(core == 1)
    def _():
        lax.fori_loop(0, shards, greet_even, 0)

    lax.fori_loop(1, clusters - 1, greet_cluster, 0)

    loads = [
        pltpu.make_async_copy(src, dst, load_sem.at[n])
        for n, (src, dst) in enumerate((
            (inc_path_hbm, inc_path), (capacity_hbm, capacity), (dual_start_hbm, dual_start),
            (path_count_hbm, path_count), (flow_start_hbm, flow_start),
            (demand_hbm, demand), (utility_hbm, utility), (inc_edge_hbm, inc_edge), (partner_hbm, partner),
            (incidence_hbm, incidence)))]
    for copy in loads:
        copy.start()

    at_x = [lax.rem(shard // 8 + d, 4) * 8 for d in range(4)]
    at_z = [lax.rem(shard // 4 + d, 2) * 4 for d in range(2)]
    at_y = [lax.rem(shard + d, 4) for d in range(4)]
    near = [at_x[x] + at_z[z] + at_y[y] for x, z, y in NEAR]

    def other_end(index):
        return lax.rem(index // 8 + 2, 4) * 8 + lax.rem(index // 4 + 1, 2) * 4 + lax.rem(index + 2, 4)

    far = [other_end(index) for index in near]

    def remote(src, dst, sent, arrived, peer_cluster, peer_shard):
        return pltpu.make_async_remote_copy(
            src_ref=src, dst_ref=dst, send_sem=sent, recv_sem=arrived,
            device_id=(peer_cluster, peer_shard), device_id_type=MESH)

    def to_hosts(src, dst, arrived):
        for u in FAR_FIRST:
            peer, place = (near[u], BACK[u]) if u < 16 else (far[u - 16], 16 + BACK[u - 16])
            remote(src.at[u], dst.at[place], spread_send, arrived, host, peer).start()

        @pl.when(core == 0)
        def _():
            remote(src.at[0], dst.at[0], spread_send, arrived, host, shard).start()

        @pl.when(core == 1)
        def _():
            dst[0] = src[0]

    def to_clusters(src, dst, sent, arrived):
        for k in (4, 3, 5, 2, 6, 1, 7):
            remote(src, dst.at[cluster], sent, arrived, lax.rem(cluster + k, clusters), shard).start()
        dst[cluster] = src[...]

    def wait_recv(dst, arrived):
        remote(dst, dst, spread_send, arrived, cluster, far[0]).wait_recv()

    def wait_send(src, sent):
        remote(src, src, sent, final_sem, cluster, far[0]).wait_send()

    def hosts_reached(src):
        @pl.when(core == 0)
        def _():
            wait_send(src, spread_send)

        @pl.when(core == 1)
        def _():
            wait_send(src.at[pl.ds(0, shards - 1)], spread_send)

    tile_role = iota((8, 128), 0) >> 2
    rows, lanes = iota((128, 128), 0), iota((128, 128), 1)
    row_slot, row_half = (rows >> 1) & 1, rows & 1
    row_dev = jnp.concatenate([jnp.where(tile_role == 0, near[q], far[q]) for q in range(16)], axis=0)
    lane1 = iota((1, 128), 1)
    loads[0].wait()
    lane_path = jnp.full((1, 128), -1, I32)
    for i in range(incs):
        lane_path = jnp.where(lane1 == i, inc_path[i], lane_path)
    owner = (lane_path >> 4) == row_dev
    before = dot(owner.astype(F32), (rows < lanes).astype(F32))
    slot = owner & (before == row_slot.astype(F32))

    def fill(dst, x):
        for q in range(16):
            tile = x[q * 8:q * 8 + 8]
            dst[q] = tile
            dst[16 + q] = pltpu.roll(tile, 4, 0)

    wanted = jnp.sum(jnp.where(slot, (lane_path & 15) + 1, 0).astype(F32), axis=1, keepdims=True) - 1.0
    fill(ask_send, jnp.broadcast_to(wanted, (128, 128)))

    def border_first(ref):
        x = ref[...]
        return jnp.concatenate([x[interior:], jnp.zeros((8 - edges, x.shape[1]), F32), x[:interior]], axis=0)

    loads[1].wait()
    loads[2].wait()
    cap = border_first(capacity)
    dual = border_first(dual_start)
    edge_send[...] = jnp.concatenate([cap[:4], dual[:4]], axis=0)

    def halves(ref):
        x = ref[...]
        return jnp.concatenate([x[:, :128], x[:, 128:]], axis=0)

    for copy in loads[3:7]:
        copy.wait()
    row32 = iota((32, 128), 0)
    count = jnp.zeros((32, 128), I32)
    for b in range(blocks):
        count = jnp.where((row32 & 15) == b, path_count[b], count)
    live = (((row32 & 15) < cluster_size[0]) & ((row32 >> 4) * 128 + iota((32, 128), 1) < count)).astype(F32)
    top = halves(demand) * live
    own_start[...] = jnp.minimum(jnp.maximum(halves(flow_start), 0.0), top)
    own_bounds[0] = top
    own_bounds[1] = halves(utility)

    def to_both(src, dst, sent, arrived):
        remote(src, dst.at[core, 1], sent.at[1], arrived.at[core, 1], host, far[0]).start()

        @pl.when(core == 0)
        def _():
            remote(src, dst.at[core, 0], sent.at[0], arrived.at[core, 0], host, shard).start()

        @pl.when(core == 1)
        def _():
            dst[core, 0] = src[...]

    pl.semaphore_wait(barrier, shards + clusters - 2 + (shards - 1) * core)
    to_both(own_start, state, start_sent, start_sem)
    to_hosts(ask_send, ask_recv.at[core], ask_sem.at[core])
    to_clusters(edge_send, edge_recv, edge_sent, edge_sem)
    to_both(own_bounds, bounds, bounds_sent, bounds_sem)

    loads[7].wait()
    lane_q = iota((1, 512), 1)
    lane_edge = jnp.full((1, 512), -1, I32)
    for i in range(incs):
        lane_edge = jnp.where((lane_q >> 4) == i, (inc_edge[i] + (8 - interior)) & 7, lane_edge)
    spread = (iota((128, 512), 0) == (iota((128, 512), 1) >> 4)).astype(F32)
    fits = (lane_edge == (lane_q & 7)) & (((lane_q >> 3) & 1) == (iota((128, 512), 0) & 1))
    both = jnp.where(fits, dot(slot.astype(F32), spread), 0.0)
    slot_edge[...] = both.astype(BF16)
    slot_edge_t[...] = both.T.astype(BF16)

    loads[8].wait()
    partner_row = jnp.full((4, 128), -1, I32)
    for k in range(slots):
        partner_row = jnp.where(iota((4, 128), 0) == k, partner[0, k], partner_row)
    partner8 = jnp.concatenate([partner_row, partner_row], axis=0)

    loads[9].wait()

    def shrink(i, _):
        at = pl.ds(pl.multiple_of(i * paths, paths), paths)
        block = incidence[i].astype(BF16)
        inc[at, :] = block
        inc_t[:, at] = block.T
        return 0
    lax.fori_loop(0, incs, shrink, 0)

    def from_holders(src, c, arrived):
        wait_recv(src if c == 0 else src.at[pl.ds(0, shards - 1)], arrived)

    def share(c, flows):
        x = pick(choose[c, :, :64], flows)
        for q in range(16):
            flow_send[c, q] = x[q * 8:q * 8 + 8]
        for u in NEAR_FAR_FIRST + ([0] if c == 0 else []):
            remote(flow_send.at[c, u], flow_recv.at[BACK[u]], share_send.at[c], flow_sem, even + c, near[u]).start()
        if c == 1:
            flow_recv[0] = flow_send[c, 0]

    def shared():
        for c in range(2):
            wait_send(flow_send.at[c] if c == 0 else flow_send.at[c, pl.ds(0, 15)], share_send.at[c])

    @pl.when(core == 1)
    def _():
        rows2, lanes2 = iota((256, 128), 0), iota((256, 128), 1)
        fit = (((lanes2 >> 4) & 1) == (rows2 & 1)) & ((lanes2 >> 5) == ((rows2 >> 2) & 1))
        block_of_lane = (lanes2 & 15).astype(F32)
        for c in range(2):
            from_holders(ask_recv.at[c], c, ask_sem.at[c])
            chosen = ((ask_recv[c].reshape(256, 128) == block_of_lane) & fit).astype(F32)
            choose[c] = chosen[:128].astype(BF16)
            choose_t[c] = chosen.T.astype(BF16)
            for role in range(c, 2):
                wait_recv(state.at[c, role], start_sem.at[c, role])
            share(c, state[c].reshape(64, 128))
        for c in range(2):
            for role in range(c, 2):
                wait_recv(bounds.at[c, role], bounds_sem.at[c, role])

    def total_load(t):
        @pl.when(core == 0)
        def _():
            wait_recv(flow_recv, flow_sem)

        @pl.when(core == 1)
        def _():
            wait_recv(flow_recv.at[pl.ds(0, 15)], flow_sem)

        got = flow_recv[...].reshape(128, 128)
        parts = dot(slot_edge_t[...], jnp.concatenate(thirds(got), axis=1))
        columns = []
        for q in range(2 * incs):
            chunk = parts[q * 8:q * 8 + 8]
            columns.append(jnp.concatenate([chunk[:, :128], chunk[:, 128:256], chunk[:, 256:]], axis=0).astype(BF16))
        sums = dot(jnp.concatenate(columns, axis=1), inc[...])
        own = (sums[16:] + sums[8:16]) + sums[:8]
        border_send[...] = own[:4]
        to_clusters(border_send, border_recv.at[t], border_sent, border_sem.at[t])
        wait_recv(border_recv.at[t, pl.ds(0, clusters - 1)], border_sem.at[t])
        twin = jnp.zeros((4, 128), F32)
        for c in range(clusters):
            twin = twin + jnp.where(partner_row == c, border_recv[t, c], 0.0)
        return jnp.concatenate([own[:4] + twin, own[4:]], axis=0)

    def settle(load, duals):
        split = jnp.minimum(limit, load + duals)
        duals = (duals + load) - split
        return (load - split) + duals, duals

    wait_recv(edge_recv.at[pl.ds(0, clusters - 1)], edge_sem)
    twin = jnp.zeros((8, 128), F32)
    for c in range(clusters):
        twin = twin + jnp.where(partner8 == c, edge_recv[c], 0.0)
    limit = unit * jnp.concatenate([0.5 * (cap[:4] + twin[:4]), cap[4:]], axis=0)
    duals = jnp.concatenate([0.5 * (dual[:4] + twin[4:]), dual[4:]], axis=0)

    residual, duals = settle(total_load(0), duals)

    hosts_reached(ask_send)
    wait_send(edge_recv.at[pl.ds(0, clusters - 1)], edge_sent)
    for src, sem in ((own_start, start_sent), (own_bounds, bounds_sent)):
        wait_send(src, sem.at[1])

        @pl.when(core == 0)
        def _():
            wait_send(src, sem.at[0])

    def iterate(t, carry):
        residual, duals = carry
        turn = lax.rem(t, 2)
        parts = dot(jnp.concatenate(thirds(residual), axis=0), inc_t[...])
        back = (parts[16:] + parts[8:16]) + parts[:8]
        back = jnp.concatenate([back[:, q * 128:q * 128 + 128] for q in range(2 * incs)], axis=0)
        fill(sum_send, pick(slot_edge[...], back))
        to_hosts(sum_send, sum_recv.at[turn, core], sum_sem.at[turn, core])
        wait_send(border_recv.at[t, pl.ds(0, clusters - 1)], border_sent)

        @pl.when(core == 1)
        def _():
            shared()
            for c in range(2):
                from_holders(sum_recv.at[turn, c], c, sum_sem.at[turn, c])
                grad = pick(choose_t[c, :64, :], sum_recv[turn, c].reshape(256, 128))
                top = bounds[c, :, 0].reshape(64, 128)
                gain = bounds[c, :, 1].reshape(64, 128)
                flows = state[c].reshape(64, 128)
                flows = jnp.minimum(jnp.maximum(flows - step_size * (grad - gain), 0.0), top)
                state[c] = flows.reshape(2, 32, 128)
                share(c, flows)

            @pl.when(t == ITERS)
            def _():
                remote(state.at[0, 0], final, final_sent, final_sem, even, shard).start()

        hosts_reached(sum_send)
        return settle(total_load(t), duals)

    residual, duals = lax.fori_loop(1, ITERS + 1, iterate, (residual, duals))
    wait_send(border_recv.at[0, pl.ds(0, clusters - 1)], border_sent)

    @pl.when(core == 0)
    def _():
        wait_recv(final, final_sem)

    @pl.when(core == 1)
    def _():
        shared()
        wait_send(state.at[0, 0], final_sent)
        final[...] = state[1, 0]

    flows = final[...]
    flows_out[...] = jnp.concatenate([flows[:16], flows[16:]], axis=1)
    duals_out[...] = jnp.concatenate([duals[4:], duals[:slots]], axis=0)


def write_out(flows, duals, flows_out, duals_out, sems):
    copies = [pltpu.make_async_copy(flows, flows_out, sems.at[0]), pltpu.make_async_copy(duals, duals_out, sems.at[1])]
    for copy in copies:
        copy.start()
    for copy in copies:
        copy.wait()


def body(flow_start, demand, utility, path_count, cluster_size, incidence, inc_path, inc_edge, capacity, dual_start, partner):
    blocks, paths = flow_start.shape
    incs, _, width = incidence.shape
    edges, slots = capacity.shape[0], partner.shape[1]
    clusters, shards = lax.axis_size("cluster"), lax.axis_size("shard")
    norm_bound = max(2, incs * incs * paths * width // (1024 * edges * blocks))
    unit = float(max(1, incs * paths // (160 * edges)))
    dims = (clusters, shards, blocks, paths, incs, edges, slots, norm_bound, unit)
    scalars = (path_count, inc_path, inc_edge, partner)
    arrays = (flow_start, demand, utility, incidence, capacity, dual_start)
    dma = pltpu.SemaphoreType.DMA
    results = pl.pallas_call(
        functools.partial(kernel, dims),
        out_shape=(pltpu.VMEM(flow_start.shape, F32), pltpu.VMEM(capacity.shape, F32)),
        in_specs=[pl.BlockSpec(memory_space=pltpu.SMEM)] + [pl.BlockSpec(memory_space=pltpu.HBM)] * (len(scalars) + len(arrays)),
        out_specs=[pl.BlockSpec(memory_space=pltpu.VMEM)] * 2,
        scratch_shapes=[pltpu.SMEM(x.shape, I32) for x in scalars] + [pltpu.VMEM(x.shape, F32) for x in arrays] + [
            pltpu.VMEM((incs * paths, width), BF16),
            pltpu.VMEM((width, incs * paths), BF16),
            pltpu.VMEM((128, 512), BF16),
            pltpu.VMEM((512, 128), BF16),
            pltpu.VMEM((2, 128, 128), BF16),
            pltpu.VMEM((2, 128, 256), BF16),
            pltpu.VMEM((shards, 8, 128), F32),
            pltpu.VMEM((2, shards, 8, 128), F32),
            pltpu.VMEM((2, 16, 8, 128), F32),
            pltpu.VMEM((16, 8, 128), F32),
            pltpu.VMEM((shards, 8, 128), F32),
            pltpu.VMEM((2, 2, shards, 8, 128), F32),
            pltpu.VMEM((8, 128), F32),
            pltpu.VMEM((clusters, 8, 128), F32),
            pltpu.VMEM((4, 128), F32),
            pltpu.VMEM((ITERS + 1, clusters, 4, 128), F32),
            pltpu.VMEM((32, 128), F32),
            pltpu.VMEM((2, 32, 128), F32),
            pltpu.VMEM((2, 2, 32, 128), F32),
            pltpu.VMEM((2, 2, 2, 32, 128), F32),
            pltpu.VMEM((32, 128), F32),
            dma((10,)), dma(()), dma((2,)), dma(()), dma(()), dma((2,)), dma((2,)), dma(()),
            dma((2,)), dma(()), dma((2, 2)), dma(()), dma((ITERS + 1,)), dma((2, 2)), dma((2, 2)), dma(()),
        ],
        compiler_params=pltpu.CompilerParams(
            collective_id=0, has_side_effects=True, vmem_limit_bytes=24 * 1024 * 1024),
    )(cluster_size, *(pltpu.with_memory_space_constraint(x, pltpu.HBM) for x in scalars + arrays))
    return pl.pallas_call(
        write_out,
        out_shape=(jax.ShapeDtypeStruct(flow_start.shape, F32), jax.ShapeDtypeStruct(capacity.shape, F32)),
        in_specs=[pl.BlockSpec(memory_space=pltpu.VMEM)] * 2,
        out_specs=[pl.BlockSpec(memory_space=pltpu.HBM)] * 2,
        scratch_shapes=[dma((2,))],
    )(*(pltpu.with_memory_space_constraint(x, pltpu.VMEM) for x in results))


def solution(mesh):
    both = P(("cluster", "shard"))
    rows = P(("cluster", "shard"), None)
    return jax.shard_map(
        body,
        mesh=mesh,
        in_specs=(rows, rows, rows, both, P("cluster"), P(("cluster", "shard"), None, None), both, both, rows, rows, P("cluster", None)),
        out_specs=(rows, rows),
        check_vma=False,
    )
```

```python
import functools

import jax
import jax.numpy as jnp
from jax import lax
from jax.experimental import pallas as pl
from jax.experimental.pallas import tpu as pltpu
from jax.sharding import PartitionSpec as P

ITERS = 3
GRID = (4, 2, 4)
MESH = pl.DeviceIdType.MESH
F32, BF16, I32 = jnp.float32, jnp.bfloat16, jnp.int32


def iota(shape, axis):
    return lax.broadcasted_iota(I32, shape, axis)


def thirds(x):
    high = x.astype(BF16).astype(F32)
    rest = x - high
    mid = rest.astype(BF16).astype(F32)
    return high, mid, rest - mid


def dot(a, b):
    return jnp.dot(a.astype(BF16), b.astype(BF16), preferred_element_type=F32)


def pick(selector, x):
    high, mid, low = thirds(x)
    return (dot(selector, low) + dot(selector, mid)) + dot(selector, high)


def hops(offset):
    return sum(min(d, n - d) for d, n in zip(offset, GRID))


NEAR = sorted(((x, z, y) for x in range(4) for z in range(2) for y in range(4) if hops((x, z, y)) <= 2), key=hops)
BACK = [NEAR.index(tuple(-d % n for d, n in zip(offset, GRID))) for offset in NEAR]


def distance(u):
    return hops(NEAR[u]) if u < 16 else 5 - hops(NEAR[u - 16])


def place_x(u):
    return NEAR[u][0] if u < 16 else (NEAR[u - 16][0] + 2) % 4


FAR_FIRST = sorted(range(1, 32), key=lambda u: (-distance(u), -min(place_x(u), 4 - place_x(u))))
NEAR_FAR_FIRST = [u for u in FAR_FIRST if u < 16]
DISTANT = [u for u in FAR_FIRST if u >= 16]


def kernel(
    dims,
    cluster_size, path_count_hbm, inc_path_hbm, inc_edge_hbm, partner_hbm,
    flow_start_hbm, demand_hbm, utility_hbm, incidence_hbm, capacity_hbm, dual_start_hbm,
    flows_out, duals_out,
    path_count, inc_path, inc_edge, partner,
    flow_start, demand, utility, incidence, capacity, dual_start,
    inc, inc_t, slot_edge, slot_edge_t, choose, choose_t,
    ask_send, ask_recv, flow_send, flow_recv, sum_send, sum_recv,
    edge_send, edge_recv, border_send, border_recv, own_start, own_bounds, state, bounds, final,
    load_sem, spread_send, share_send, edge_sent, border_sent, start_sent, bounds_sent, final_sent,
    ask_sem, distant_sem, flow_sem, sum_sem, edge_sem, border_sem, start_sem, bounds_sem, final_sem,
):
    clusters, shards, blocks, paths, incs, edges, slots, norm_bound, unit = dims
    step_size = 1.0 / (2.0 * norm_bound)
    cluster, shard = lax.axis_index("cluster"), lax.axis_index("shard")
    interior = edges - slots

    core = lax.rem(cluster, 2)
    even = cluster - core
    host = even + 1

    barrier = pltpu.get_barrier_semaphore()

    def greet(peer_cluster, peer_shard):
        pl.semaphore_signal(barrier, inc=1, device_id=(peer_cluster, peer_shard), device_id_type=MESH)

    def greet_hosts(k, _):
        greet(host, lax.rem(shard + k, shards))
        return 0

    def greet_even(k, _):
        greet(even, lax.rem(shard + k, shards))
        return 0

    def greet_cluster(k, _):
        greet(lax.rem(cluster + k + 1 - core, clusters), shard)
        return 0

    lax.fori_loop(1, shards, greet_hosts, 0)

    @pl.when(core == 0)
    def _():
        greet(host, shard)

    @pl.when(core == 1)
    def _():
        lax.fori_loop(0, shards, greet_even, 0)

    lax.fori_loop(1, clusters - 1, greet_cluster, 0)

    loads = [
        pltpu.make_async_copy(src, dst, load_sem.at[n])
        for n, (src, dst) in enumerate((
            (inc_path_hbm, inc_path), (capacity_hbm, capacity), (dual_start_hbm, dual_start),
            (path_count_hbm, path_count), (flow_start_hbm, flow_start),
            (demand_hbm, demand), (utility_hbm, utility), (inc_edge_hbm, inc_edge), (partner_hbm, partner),
            (incidence_hbm, incidence)))]
    for copy in loads:
        copy.start()

    at_x = [lax.rem(shard // 8 + d, 4) * 8 for d in range(4)]
    at_z = [lax.rem(shard // 4 + d, 2) * 4 for d in range(2)]
    at_y = [lax.rem(shard + d, 4) for d in range(4)]
    near = [at_x[x] + at_z[z] + at_y[y] for x, z, y in NEAR]

    def other_end(index):
        return lax.rem(index // 8 + 2, 4) * 8 + lax.rem(index // 4 + 1, 2) * 4 + lax.rem(index + 2, 4)

    far = [other_end(index) for index in near]

    def remote(src, dst, sent, arrived, peer_cluster, peer_shard):
        return pltpu.make_async_remote_copy(
            src_ref=src, dst_ref=dst, send_sem=sent, recv_sem=arrived,
            device_id=(peer_cluster, peer_shard), device_id_type=MESH)

    def to_hosts(places, src, dst, arrived):
        for u in places:
            peer, place = (near[u], BACK[u]) if u < 16 else (far[u - 16], 16 + BACK[u - 16])
            remote(src.at[u], dst.at[place], spread_send, arrived, host, peer).start()

    def to_own_host(src, dst, arrived):
        @pl.when(core == 0)
        def _():
            remote(src.at[0], dst.at[0], spread_send, arrived, host, shard).start()

        @pl.when(core == 1)
        def _():
            dst[0] = src[0]

    def to_clusters(src, dst, sent, arrived):
        for k in (4, 3, 5, 2, 6, 1, 7):
            remote(src, dst.at[cluster], sent, arrived, lax.rem(cluster + k, clusters), shard).start()
        dst[cluster] = src[...]

    def wait_recv(dst, arrived):
        remote(dst, dst, spread_send, arrived, cluster, far[0]).wait_recv()

    def wait_send(src, sent):
        remote(src, src, sent, final_sem, cluster, far[0]).wait_send()

    def hosts_reached(src):
        @pl.when(core == 0)
        def _():
            wait_send(src, spread_send)

        @pl.when(core == 1)
        def _():
            wait_send(src.at[pl.ds(0, shards - 1)], spread_send)

    tile_role = iota((8, 128), 0) >> 2
    rows, lanes = iota((128, 128), 0), iota((128, 128), 1)
    row_slot, row_half = (rows >> 1) & 1, rows & 1
    row_dev = jnp.concatenate([jnp.where(tile_role == 0, near[q], far[q]) for q in range(16)], axis=0)
    lane1 = iota((1, 128), 1)
    loads[0].wait()
    lane_path = jnp.full((1, 128), -1, I32)
    for i in range(incs):
        lane_path = jnp.where(lane1 == i, inc_path[i], lane_path)
    owner = (lane_path >> 4) == row_dev
    before = dot(owner.astype(F32), (rows < lanes).astype(F32))
    slot = owner & (before == row_slot.astype(F32))

    def fill(dst, x):
        for q in range(16):
            tile = x[q * 8:q * 8 + 8]
            dst[q] = tile
            dst[16 + q] = pltpu.roll(tile, 4, 0)

    wanted = jnp.sum(jnp.where(slot, (lane_path & 15) + 1, 0).astype(F32), axis=1, keepdims=True) - 1.0
    fill(ask_send, jnp.broadcast_to(wanted, (128, 128)))

    def border_first(ref):
        x = ref[...]
        return jnp.concatenate([x[interior:], jnp.zeros((8 - edges, x.shape[1]), F32), x[:interior]], axis=0)

    loads[1].wait()
    loads[2].wait()
    cap = border_first(capacity)
    dual = border_first(dual_start)
    edge_send[...] = jnp.concatenate([cap[:4], dual[:4]], axis=0)

    def halves(ref):
        x = ref[...]
        return jnp.concatenate([x[:, :128], x[:, 128:]], axis=0)

    for copy in loads[3:7]:
        copy.wait()
    row32 = iota((32, 128), 0)
    count = jnp.zeros((32, 128), I32)
    for b in range(blocks):
        count = jnp.where((row32 & 15) == b, path_count[b], count)
    live = (((row32 & 15) < cluster_size[0]) & ((row32 >> 4) * 128 + iota((32, 128), 1) < count)).astype(F32)
    top = halves(demand) * live
    own_start[...] = jnp.minimum(jnp.maximum(halves(flow_start), 0.0), top)
    own_bounds[0] = top
    own_bounds[1] = halves(utility)

    def to_both(src, dst, sent, arrived):
        remote(src, dst.at[core, 1], sent.at[1], arrived.at[core, 1], host, far[0]).start()

        @pl.when(core == 0)
        def _():
            remote(src, dst.at[core, 0], sent.at[0], arrived.at[core, 0], host, shard).start()

        @pl.when(core == 1)
        def _():
            dst[core, 0] = src[...]

    pl.semaphore_wait(barrier, shards + clusters - 2 + (shards - 1) * core)
    to_both(own_start, state, start_sent, start_sem)
    to_hosts(NEAR_FAR_FIRST, ask_send, ask_recv.at[core], ask_sem.at[core])
    to_own_host(ask_send, ask_recv.at[core], ask_sem.at[core])
    to_clusters(edge_send, edge_recv, edge_sent, edge_sem)
    to_hosts(DISTANT, ask_send, ask_recv.at[core], distant_sem.at[core])
    to_both(own_bounds, bounds, bounds_sent, bounds_sem)

    loads[7].wait()
    lane_q = iota((1, 512), 1)
    lane_edge = jnp.full((1, 512), -1, I32)
    for i in range(incs):
        lane_edge = jnp.where((lane_q >> 4) == i, (inc_edge[i] + (8 - interior)) & 7, lane_edge)
    spread = (iota((128, 512), 0) == (iota((128, 512), 1) >> 4)).astype(F32)
    fits = (lane_edge == (lane_q & 7)) & (((lane_q >> 3) & 1) == (iota((128, 512), 0) & 1))
    both = jnp.where(fits, dot(slot.astype(F32), spread), 0.0)
    slot_edge[...] = both.astype(BF16)
    slot_edge_t[...] = both.T.astype(BF16)

    loads[8].wait()
    partner_row = jnp.full((4, 128), -1, I32)
    for k in range(slots):
        partner_row = jnp.where(iota((4, 128), 0) == k, partner[0, k], partner_row)
    partner8 = jnp.concatenate([partner_row, partner_row], axis=0)

    loads[9].wait()

    def shrink(i, _):
        at = pl.ds(pl.multiple_of(i * paths, paths), paths)
        block = incidence[i].astype(BF16)
        inc[at, :] = block
        inc_t[:, at] = block.T
        return 0
    lax.fori_loop(0, incs, shrink, 0)

    def from_holders(src, c, arrived):
        wait_recv(src if c == 0 else src.at[pl.ds(0, shards - 1)], arrived)

    def share(c, flows):
        x = pick(choose[c, :, :64], flows)
        for q in range(16):
            flow_send[c, q] = x[q * 8:q * 8 + 8]
        for u in NEAR_FAR_FIRST + ([0] if c == 0 else []):
            remote(flow_send.at[c, u], flow_recv.at[BACK[u]], share_send.at[c], flow_sem, even + c, near[u]).start()
        if c == 1:
            flow_recv[0] = flow_send[c, 0]

    def shared():
        for c in range(2):
            wait_send(flow_send.at[c] if c == 0 else flow_send.at[c, pl.ds(0, 15)], share_send.at[c])

    @pl.when(core == 1)
    def _():
        rows2, lanes2 = iota((256, 128), 0), iota((256, 128), 1)
        fit = (((lanes2 >> 4) & 1) == (rows2 & 1)) & ((lanes2 >> 5) == ((rows2 >> 2) & 1))
        block_of_lane = (lanes2 & 15).astype(F32)
        for c in range(2):
            wait_recv(ask_recv.at[c, pl.ds(0, 16 - c)], ask_sem.at[c])
            chosen = (ask_recv[c, :16].reshape(128, 128) == block_of_lane[:128]) & fit[:128]
            choose[c] = chosen.astype(F32).astype(BF16)
        for c in range(2):
            for role in range(c, 2):
                wait_recv(state.at[c, role], start_sem.at[c, role])
            share(c, state[c].reshape(64, 128))
        for c in range(2):
            wait_recv(ask_recv.at[c, pl.ds(16, 16)], distant_sem.at[c])
            chosen = (ask_recv[c].reshape(256, 128) == block_of_lane) & fit
            choose_t[c] = chosen.astype(F32).T.astype(BF16)
            for role in range(c, 2):
                wait_recv(bounds.at[c, role], bounds_sem.at[c, role])

    def total_load(t):
        @pl.when(core == 0)
        def _():
            wait_recv(flow_recv, flow_sem)

        @pl.when(core == 1)
        def _():
            wait_recv(flow_recv.at[pl.ds(0, 15)], flow_sem)

        got = flow_recv[...].reshape(128, 128)
        parts = dot(slot_edge_t[...], jnp.concatenate(thirds(got), axis=1))
        columns = []
        for q in range(2 * incs):
            chunk = parts[q * 8:q * 8 + 8]
            columns.append(jnp.concatenate([chunk[:, :128], chunk[:, 128:256], chunk[:, 256:]], axis=0).astype(BF16))
        sums = dot(jnp.concatenate(columns, axis=1), inc[...])
        own = (sums[16:] + sums[8:16]) + sums[:8]
        border_send[...] = own[:4]
        to_clusters(border_send, border_recv.at[t], border_sent, border_sem.at[t])
        wait_recv(border_recv.at[t, pl.ds(0, clusters - 1)], border_sem.at[t])
        twin = jnp.zeros((4, 128), F32)
        for c in range(clusters):
            twin = twin + jnp.where(partner_row == c, border_recv[t, c], 0.0)
        return jnp.concatenate([own[:4] + twin, own[4:]], axis=0)

    def settle(load, duals):
        split = jnp.minimum(limit, load + duals)
        duals = (duals + load) - split
        return (load - split) + duals, duals

    wait_recv(edge_recv.at[pl.ds(0, clusters - 1)], edge_sem)
    twin = jnp.zeros((8, 128), F32)
    for c in range(clusters):
        twin = twin + jnp.where(partner8 == c, edge_recv[c], 0.0)
    limit = unit * jnp.concatenate([0.5 * (cap[:4] + twin[:4]), cap[4:]], axis=0)
    duals = jnp.concatenate([0.5 * (dual[:4] + twin[4:]), dual[4:]], axis=0)

    residual, duals = settle(total_load(0), duals)

    hosts_reached(ask_send)
    wait_send(edge_recv.at[pl.ds(0, clusters - 1)], edge_sent)
    for src, sem in ((own_start, start_sent), (own_bounds, bounds_sent)):
        wait_send(src, sem.at[1])

        @pl.when(core == 0)
        def _():
            wait_send(src, sem.at[0])

    def iterate(t, carry):
        residual, duals = carry
        turn = lax.rem(t, 2)
        parts = dot(jnp.concatenate(thirds(residual), axis=0), inc_t[...])
        back = (parts[16:] + parts[8:16]) + parts[:8]
        back = jnp.concatenate([back[:, q * 128:q * 128 + 128] for q in range(2 * incs)], axis=0)
        fill(sum_send, pick(slot_edge[...], back))
        to_hosts(FAR_FIRST, sum_send, sum_recv.at[turn, core], sum_sem.at[turn, core])
        to_own_host(sum_send, sum_recv.at[turn, core], sum_sem.at[turn, core])
        wait_send(border_recv.at[t, pl.ds(0, clusters - 1)], border_sent)

        @pl.when(core == 1)
        def _():
            shared()
            for c in range(2):
                from_holders(sum_recv.at[turn, c], c, sum_sem.at[turn, c])
                grad = pick(choose_t[c, :64, :], sum_recv[turn, c].reshape(256, 128))
                top = bounds[c, :, 0].reshape(64, 128)
                gain = bounds[c, :, 1].reshape(64, 128)
                flows = state[c].reshape(64, 128)
                flows = jnp.minimum(jnp.maximum(flows - step_size * (grad - gain), 0.0), top)
                state[c] = flows.reshape(2, 32, 128)
                share(c, flows)

            @pl.when(t == ITERS)
            def _():
                remote(state.at[0, 0], final, final_sent, final_sem, even, shard).start()

        hosts_reached(sum_send)
        return settle(total_load(t), duals)

    residual, duals = lax.fori_loop(1, ITERS + 1, iterate, (residual, duals))
    wait_send(border_recv.at[0, pl.ds(0, clusters - 1)], border_sent)

    @pl.when(core == 0)
    def _():
        wait_recv(final, final_sem)

    @pl.when(core == 1)
    def _():
        shared()
        wait_send(state.at[0, 0], final_sent)
        final[...] = state[1, 0]

    flows = final[...]
    flows_out[...] = jnp.concatenate([flows[:16], flows[16:]], axis=1)
    duals_out[...] = jnp.concatenate([duals[4:], duals[:slots]], axis=0)


def write_out(flows, duals, flows_out, duals_out, sems):
    copies = [pltpu.make_async_copy(flows, flows_out, sems.at[0]), pltpu.make_async_copy(duals, duals_out, sems.at[1])]
    for copy in copies:
        copy.start()
    for copy in copies:
        copy.wait()


def body(flow_start, demand, utility, path_count, cluster_size, incidence, inc_path, inc_edge, capacity, dual_start, partner):
    blocks, paths = flow_start.shape
    incs, _, width = incidence.shape
    edges, slots = capacity.shape[0], partner.shape[1]
    clusters, shards = lax.axis_size("cluster"), lax.axis_size("shard")
    norm_bound = max(2, incs * incs * paths * width // (1024 * edges * blocks))
    unit = float(max(1, incs * paths // (160 * edges)))
    dims = (clusters, shards, blocks, paths, incs, edges, slots, norm_bound, unit)
    scalars = (path_count, inc_path, inc_edge, partner)
    arrays = (flow_start, demand, utility, incidence, capacity, dual_start)
    dma = pltpu.SemaphoreType.DMA
    results = pl.pallas_call(
        functools.partial(kernel, dims),
        out_shape=(pltpu.VMEM(flow_start.shape, F32), pltpu.VMEM(capacity.shape, F32)),
        in_specs=[pl.BlockSpec(memory_space=pltpu.SMEM)] + [pl.BlockSpec(memory_space=pltpu.HBM)] * (len(scalars) + len(arrays)),
        out_specs=[pl.BlockSpec(memory_space=pltpu.VMEM)] * 2,
        scratch_shapes=[pltpu.SMEM(x.shape, I32) for x in scalars] + [pltpu.VMEM(x.shape, F32) for x in arrays] + [
            pltpu.VMEM((incs * paths, width), BF16),
            pltpu.VMEM((width, incs * paths), BF16),
            pltpu.VMEM((128, 512), BF16),
            pltpu.VMEM((512, 128), BF16),
            pltpu.VMEM((2, 128, 128), BF16),
            pltpu.VMEM((2, 128, 256), BF16),
            pltpu.VMEM((shards, 8, 128), F32),
            pltpu.VMEM((2, shards, 8, 128), F32),
            pltpu.VMEM((2, 16, 8, 128), F32),
            pltpu.VMEM((16, 8, 128), F32),
            pltpu.VMEM((shards, 8, 128), F32),
            pltpu.VMEM((2, 2, shards, 8, 128), F32),
            pltpu.VMEM((8, 128), F32),
            pltpu.VMEM((clusters, 8, 128), F32),
            pltpu.VMEM((4, 128), F32),
            pltpu.VMEM((ITERS + 1, clusters, 4, 128), F32),
            pltpu.VMEM((32, 128), F32),
            pltpu.VMEM((2, 32, 128), F32),
            pltpu.VMEM((2, 2, 32, 128), F32),
            pltpu.VMEM((2, 2, 2, 32, 128), F32),
            pltpu.VMEM((32, 128), F32),
            dma((10,)), dma(()), dma((2,)), dma(()), dma(()), dma((2,)), dma((2,)), dma(()),
            dma((2,)), dma((2,)), dma(()), dma((2, 2)), dma(()), dma((ITERS + 1,)), dma((2, 2)), dma((2, 2)), dma(()),
        ],
        compiler_params=pltpu.CompilerParams(
            collective_id=0, has_side_effects=True, vmem_limit_bytes=24 * 1024 * 1024),
    )(cluster_size, *(pltpu.with_memory_space_constraint(x, pltpu.HBM) for x in scalars + arrays))
    return pl.pallas_call(
        write_out,
        out_shape=(jax.ShapeDtypeStruct(flow_start.shape, F32), jax.ShapeDtypeStruct(capacity.shape, F32)),
        in_specs=[pl.BlockSpec(memory_space=pltpu.VMEM)] * 2,
        out_specs=[pl.BlockSpec(memory_space=pltpu.HBM)] * 2,
        scratch_shapes=[dma((2,))],
    )(*(pltpu.with_memory_space_constraint(x, pltpu.VMEM) for x in results))


def solution(mesh):
    both = P(("cluster", "shard"))
    rows = P(("cluster", "shard"), None)
    return jax.shard_map(
        body,
        mesh=mesh,
        in_specs=(rows, rows, rows, both, P("cluster"), P(("cluster", "shard"), None, None), both, both, rows, rows, P("cluster", None)),
        out_specs=(rows, rows),
        check_vma=False,
    )
```

```python
import functools

import jax
import jax.numpy as jnp
from jax import lax
from jax.experimental import pallas as pl
from jax.experimental.pallas import tpu as pltpu
from jax.sharding import PartitionSpec as P

ITERS = 3
GRID = (4, 2, 4)
MESH = pl.DeviceIdType.MESH
F32, BF16, I32 = jnp.float32, jnp.bfloat16, jnp.int32


def iota(shape, axis):
    return lax.broadcasted_iota(I32, shape, axis)


def thirds(x):
    high = x.astype(BF16).astype(F32)
    rest = x - high
    mid = rest.astype(BF16).astype(F32)
    return high, mid, rest - mid


def dot(a, b):
    return jnp.dot(a.astype(BF16), b.astype(BF16), preferred_element_type=F32)


def pick(selector, x):
    high, mid, low = thirds(x)
    x = dot(selector, jnp.concatenate([low, mid, high], axis=1))
    return (x[:, :128] + x[:, 128:256]) + x[:, 256:]


def hops(offset):
    return sum(min(d, n - d) for d, n in zip(offset, GRID))


NEAR = sorted(((x, z, y) for x in range(4) for z in range(2) for y in range(4) if hops((x, z, y)) <= 2), key=hops)
BACK = [NEAR.index(tuple(-d % n for d, n in zip(offset, GRID))) for offset in NEAR]


def distance(u):
    return hops(NEAR[u]) if u < 16 else 5 - hops(NEAR[u - 16])


def place_x(u):
    return NEAR[u][0] if u < 16 else (NEAR[u - 16][0] + 2) % 4


FAR_FIRST = sorted(range(1, 32), key=lambda u: (-distance(u), -min(place_x(u), 4 - place_x(u))))
NEAR_FAR_FIRST = [u for u in FAR_FIRST if u < 16]
DISTANT = [u for u in FAR_FIRST if u >= 16]


def kernel(
    dims,
    cluster_size, path_count_hbm, inc_path_hbm, inc_edge_hbm, partner_hbm,
    flow_start_hbm, demand_hbm, utility_hbm, incidence_hbm, capacity_hbm, dual_start_hbm,
    flows_out, duals_out,
    path_count, inc_path, inc_edge, partner,
    flow_start, demand, utility, incidence, capacity, dual_start,
    inc, inc_t, slot_edge, slot_edge_t, choose, choose_t,
    ask_send, ask_recv, flow_send, flow_recv, sum_send, sum_recv,
    edge_send, edge_recv, border_send, border_recv, own_start, own_bounds, state, bounds, final,
    load_sem, spread_send, share_send, edge_sent, border_sent, start_sent, bounds_sent, final_sent,
    ask_sem, distant_sem, flow_sem, sum_sem, edge_sem, border_sem, start_sem, bounds_sem, final_sem,
):
    clusters, shards, blocks, paths, incs, edges, slots, norm_bound, unit = dims
    step_size = 1.0 / (2.0 * norm_bound)
    cluster, shard = lax.axis_index("cluster"), lax.axis_index("shard")
    interior = edges - slots

    core = lax.rem(cluster, 2)
    even = cluster - core
    host = even + 1

    barrier = pltpu.get_barrier_semaphore()

    def greet(peer_cluster, peer_shard):
        pl.semaphore_signal(barrier, inc=1, device_id=(peer_cluster, peer_shard), device_id_type=MESH)

    def greet_hosts(k, _):
        greet(host, lax.rem(shard + k, shards))
        return 0

    def greet_even(k, _):
        greet(even, lax.rem(shard + k, shards))
        return 0

    def greet_cluster(k, _):
        greet(lax.rem(cluster + k + 1 - core, clusters), shard)
        return 0

    lax.fori_loop(1, shards, greet_hosts, 0)

    @pl.when(core == 0)
    def _():
        greet(host, shard)

    @pl.when(core == 1)
    def _():
        lax.fori_loop(0, shards, greet_even, 0)

    lax.fori_loop(1, clusters - 1, greet_cluster, 0)

    loads = [
        pltpu.make_async_copy(src, dst, load_sem.at[n])
        for n, (src, dst) in enumerate((
            (inc_path_hbm, inc_path), (capacity_hbm, capacity), (dual_start_hbm, dual_start),
            (path_count_hbm, path_count), (flow_start_hbm, flow_start),
            (demand_hbm, demand), (utility_hbm, utility), (inc_edge_hbm, inc_edge), (partner_hbm, partner),
            (incidence_hbm, incidence)))]
    for copy in loads:
        copy.start()

    at_x = [lax.rem(shard // 8 + d, 4) * 8 for d in range(4)]
    at_z = [lax.rem(shard // 4 + d, 2) * 4 for d in range(2)]
    at_y = [lax.rem(shard + d, 4) for d in range(4)]
    near = [at_x[x] + at_z[z] + at_y[y] for x, z, y in NEAR]

    def other_end(index):
        return lax.rem(index // 8 + 2, 4) * 8 + lax.rem(index // 4 + 1, 2) * 4 + lax.rem(index + 2, 4)

    far = [other_end(index) for index in near]

    def remote(src, dst, sent, arrived, peer_cluster, peer_shard):
        return pltpu.make_async_remote_copy(
            src_ref=src, dst_ref=dst, send_sem=sent, recv_sem=arrived,
            device_id=(peer_cluster, peer_shard), device_id_type=MESH)

    def to_hosts(places, src, dst, arrived):
        for u in places:
            peer, place = (near[u], BACK[u]) if u < 16 else (far[u - 16], 16 + BACK[u - 16])
            remote(src.at[u], dst.at[place], spread_send, arrived, host, peer).start()

    def to_own_host(src, dst, arrived):
        @pl.when(core == 0)
        def _():
            remote(src.at[0], dst.at[0], spread_send, arrived, host, shard).start()

        @pl.when(core == 1)
        def _():
            dst[0] = src[0]

    def to_clusters(src, dst, sent, arrived):
        for k in (4, 3, 5, 2, 6, 1, 7):
            remote(src, dst.at[cluster], sent, arrived, lax.rem(cluster + k, clusters), shard).start()
        dst[cluster] = src[...]

    def wait_recv(dst, arrived):
        remote(dst, dst, spread_send, arrived, cluster, far[0]).wait_recv()

    def wait_send(src, sent):
        remote(src, src, sent, final_sem, cluster, far[0]).wait_send()

    def hosts_reached(src):
        @pl.when(core == 0)
        def _():
            wait_send(src, spread_send)

        @pl.when(core == 1)
        def _():
            wait_send(src.at[pl.ds(0, shards - 1)], spread_send)

    tile_role = iota((8, 128), 0) >> 2
    rows, lanes = iota((128, 128), 0), iota((128, 128), 1)
    row_slot, row_half = (rows >> 1) & 1, rows & 1
    row_dev = jnp.concatenate([jnp.where(tile_role == 0, near[q], far[q]) for q in range(16)], axis=0)
    lane1 = iota((1, 128), 1)
    loads[0].wait()
    lane_path = jnp.full((1, 128), -1, I32)
    for i in range(incs):
        lane_path = jnp.where(lane1 == i, inc_path[i], lane_path)
    owner = (lane_path >> 4) == row_dev
    before = dot(owner.astype(F32), (rows < lanes).astype(F32))
    slot = owner & (before == row_slot.astype(F32))

    def fill(dst, x):
        for q in range(16):
            tile = x[q * 8:q * 8 + 8]
            dst[q] = tile
            dst[16 + q] = pltpu.roll(tile, 4, 0)

    wanted = jnp.sum(jnp.where(slot, (lane_path & 15) + 1, 0).astype(F32), axis=1, keepdims=True) - 1.0
    fill(ask_send, jnp.broadcast_to(wanted, (128, 128)))

    def border_first(ref):
        x = ref[...]
        return jnp.concatenate([x[interior:], jnp.zeros((8 - edges, x.shape[1]), F32), x[:interior]], axis=0)

    loads[1].wait()
    loads[2].wait()
    cap = border_first(capacity)
    dual = border_first(dual_start)
    edge_send[...] = jnp.concatenate([cap[:4], dual[:4]], axis=0)

    def halves(ref):
        x = ref[...]
        return jnp.concatenate([x[:, :128], x[:, 128:]], axis=0)

    for copy in loads[3:7]:
        copy.wait()
    row32 = iota((32, 128), 0)
    count = jnp.zeros((32, 128), I32)
    for b in range(blocks):
        count = jnp.where((row32 & 15) == b, path_count[b], count)
    live = (((row32 & 15) < cluster_size[0]) & ((row32 >> 4) * 128 + iota((32, 128), 1) < count)).astype(F32)
    top = halves(demand) * live
    own_start[...] = jnp.minimum(jnp.maximum(halves(flow_start), 0.0), top)
    own_bounds[0] = top
    own_bounds[1] = halves(utility)

    def to_both(src, dst, sent, arrived):
        remote(src, dst.at[core, 1], sent.at[1], arrived.at[core, 1], host, far[0]).start()

        @pl.when(core == 0)
        def _():
            remote(src, dst.at[core, 0], sent.at[0], arrived.at[core, 0], host, shard).start()

        @pl.when(core == 1)
        def _():
            dst[core, 0] = src[...]

    pl.semaphore_wait(barrier, shards + clusters - 2 + (shards - 1) * core)
    to_both(own_start, state, start_sent, start_sem)
    to_hosts(NEAR_FAR_FIRST, ask_send, ask_recv.at[core], ask_sem.at[core])
    to_own_host(ask_send, ask_recv.at[core], ask_sem.at[core])
    to_clusters(edge_send, edge_recv, edge_sent, edge_sem)

    loads[7].wait()
    lane_q = iota((1, 512), 1)
    lane_edge = jnp.full((1, 512), -1, I32)
    for i in range(incs):
        lane_edge = jnp.where((lane_q >> 4) == i, (inc_edge[i] + (8 - interior)) & 7, lane_edge)
    spread = (iota((128, 512), 0) == (iota((128, 512), 1) >> 4)).astype(F32)
    fits = (lane_edge == (lane_q & 7)) & (((lane_q >> 3) & 1) == (iota((128, 512), 0) & 1))
    both = jnp.where(fits, dot(slot.astype(F32), spread), 0.0)
    slot_edge[...] = both.astype(BF16)
    slot_edge_t[...] = both.T.astype(BF16)

    loads[8].wait()
    partner_row = jnp.full((4, 128), -1, I32)
    for k in range(slots):
        partner_row = jnp.where(iota((4, 128), 0) == k, partner[0, k], partner_row)
    partner8 = jnp.concatenate([partner_row, partner_row], axis=0)

    to_hosts(DISTANT, ask_send, ask_recv.at[core], distant_sem.at[core])
    to_both(own_bounds, bounds, bounds_sent, bounds_sem)

    loads[9].wait()

    def shrink(i, _):
        at = pl.ds(pl.multiple_of(i * paths, paths), paths)
        block = incidence[i].astype(BF16)
        inc[at, :] = block
        inc_t[:, at] = block.T
        return 0
    lax.fori_loop(0, incs, shrink, 0)

    def from_holders(src, c, arrived):
        wait_recv(src if c == 0 else src.at[pl.ds(0, shards - 1)], arrived)

    def share(c, flows):
        x = pick(choose[c, :, :64], flows)
        for q in range(16):
            flow_send[c, q] = x[q * 8:q * 8 + 8]
        for u in NEAR_FAR_FIRST + ([0] if c == 0 else []):
            remote(flow_send.at[c, u], flow_recv.at[BACK[u]], share_send.at[c], flow_sem, even + c, near[u]).start()
        if c == 1:
            flow_recv[0] = flow_send[c, 0]

    def shared():
        for c in range(2):
            wait_send(flow_send.at[c] if c == 0 else flow_send.at[c, pl.ds(0, 15)], share_send.at[c])

    @pl.when(core == 1)
    def _():
        rows2, lanes2 = iota((256, 128), 0), iota((256, 128), 1)
        fit = (((lanes2 >> 4) & 1) == (rows2 & 1)) & ((lanes2 >> 5) == ((rows2 >> 2) & 1))
        block_of_lane = (lanes2 & 15).astype(F32)
        for c in range(2):
            wait_recv(ask_recv.at[c, pl.ds(0, 16 - c)], ask_sem.at[c])
            chosen = (ask_recv[c, :16].reshape(128, 128) == block_of_lane[:128]) & fit[:128]
            choose[c] = chosen.astype(F32).astype(BF16)
        for c in range(2):
            for role in range(c, 2):
                wait_recv(state.at[c, role], start_sem.at[c, role])
            share(c, state[c].reshape(64, 128))
        for c in range(2):
            wait_recv(ask_recv.at[c, pl.ds(16, 16)], distant_sem.at[c])
            chosen = (ask_recv[c].reshape(256, 128) == block_of_lane) & fit
            choose_t[c] = chosen.astype(F32).T.astype(BF16)
            for role in range(c, 2):
                wait_recv(bounds.at[c, role], bounds_sem.at[c, role])

    def total_load(t):
        @pl.when(core == 0)
        def _():
            wait_recv(flow_recv, flow_sem)

        @pl.when(core == 1)
        def _():
            wait_recv(flow_recv.at[pl.ds(0, 15)], flow_sem)

        got = flow_recv[...].reshape(128, 128)
        parts = dot(slot_edge_t[...], jnp.concatenate(thirds(got), axis=1))
        columns = []
        for q in range(2 * incs):
            chunk = parts[q * 8:q * 8 + 8]
            columns.append(jnp.concatenate([chunk[:, :128], chunk[:, 128:256], chunk[:, 256:]], axis=0).astype(BF16))
        sums = dot(jnp.concatenate(columns, axis=1), inc[...])
        own = (sums[16:] + sums[8:16]) + sums[:8]
        border_send[...] = own[:4]
        to_clusters(border_send, border_recv.at[t], border_sent, border_sem.at[t])
        wait_recv(border_recv.at[t, pl.ds(0, clusters - 1)], border_sem.at[t])
        twin = jnp.zeros((4, 128), F32)
        for c in range(clusters):
            twin = twin + jnp.where(partner_row == c, border_recv[t, c], 0.0)
        return jnp.concatenate([own[:4] + twin, own[4:]], axis=0)

    def settle(load, duals):
        split = jnp.minimum(limit, load + duals)
        duals = (duals + load) - split
        return (load - split) + duals, duals

    wait_recv(edge_recv.at[pl.ds(0, clusters - 1)], edge_sem)
    twin = jnp.zeros((8, 128), F32)
    for c in range(clusters):
        twin = twin + jnp.where(partner8 == c, edge_recv[c], 0.0)
    limit = unit * jnp.concatenate([0.5 * (cap[:4] + twin[:4]), cap[4:]], axis=0)
    duals = jnp.concatenate([0.5 * (dual[:4] + twin[4:]), dual[4:]], axis=0)

    residual, duals = settle(total_load(0), duals)

    hosts_reached(ask_send)
    wait_send(edge_recv.at[pl.ds(0, clusters - 1)], edge_sent)
    for src, sem in ((own_start, start_sent), (own_bounds, bounds_sent)):
        wait_send(src, sem.at[1])

        @pl.when(core == 0)
        def _():
            wait_send(src, sem.at[0])

    def iterate(t, carry):
        residual, duals = carry
        turn = lax.rem(t, 2)
        parts = dot(jnp.concatenate(thirds(residual), axis=0), inc_t[...])
        back = (parts[16:] + parts[8:16]) + parts[:8]
        back = jnp.concatenate([back[:, q * 128:q * 128 + 128] for q in range(2 * incs)], axis=0)
        fill(sum_send, pick(slot_edge[...], back))
        to_hosts(FAR_FIRST, sum_send, sum_recv.at[turn, core], sum_sem.at[turn, core])
        to_own_host(sum_send, sum_recv.at[turn, core], sum_sem.at[turn, core])
        wait_send(border_recv.at[t, pl.ds(0, clusters - 1)], border_sent)

        @pl.when(core == 1)
        def _():
            shared()
            for c in range(2):
                from_holders(sum_recv.at[turn, c], c, sum_sem.at[turn, c])
                grad = pick(choose_t[c, :64, :], sum_recv[turn, c].reshape(256, 128))
                top = bounds[c, :, 0].reshape(64, 128)
                gain = bounds[c, :, 1].reshape(64, 128)
                flows = state[c].reshape(64, 128)
                flows = jnp.minimum(jnp.maximum(flows - step_size * (grad - gain), 0.0), top)
                share(c, flows)
                state[c] = flows.reshape(2, 32, 128)

            @pl.when(t == ITERS)
            def _():
                remote(state.at[0, 0], final, final_sent, final_sem, even, shard).start()

        hosts_reached(sum_send)
        return settle(total_load(t), duals)

    residual, duals = lax.fori_loop(1, ITERS + 1, iterate, (residual, duals))
    wait_send(border_recv.at[0, pl.ds(0, clusters - 1)], border_sent)

    @pl.when(core == 0)
    def _():
        wait_recv(final, final_sem)

    @pl.when(core == 1)
    def _():
        shared()
        wait_send(state.at[0, 0], final_sent)
        final[...] = state[1, 0]

    flows = final[...]
    flows_out[...] = jnp.concatenate([flows[:16], flows[16:]], axis=1)
    duals_out[...] = jnp.concatenate([duals[4:], duals[:slots]], axis=0)


def write_out(flows, duals, flows_out, duals_out, sems):
    copies = [pltpu.make_async_copy(flows, flows_out, sems.at[0]), pltpu.make_async_copy(duals, duals_out, sems.at[1])]
    for copy in copies:
        copy.start()
    for copy in copies:
        copy.wait()


def body(flow_start, demand, utility, path_count, cluster_size, incidence, inc_path, inc_edge, capacity, dual_start, partner):
    blocks, paths = flow_start.shape
    incs, _, width = incidence.shape
    edges, slots = capacity.shape[0], partner.shape[1]
    clusters, shards = lax.axis_size("cluster"), lax.axis_size("shard")
    norm_bound = max(2, incs * incs * paths * width // (1024 * edges * blocks))
    unit = float(max(1, incs * paths // (160 * edges)))
    dims = (clusters, shards, blocks, paths, incs, edges, slots, norm_bound, unit)
    scalars = (path_count, inc_path, inc_edge, partner)
    arrays = (flow_start, demand, utility, incidence, capacity, dual_start)
    dma = pltpu.SemaphoreType.DMA
    results = pl.pallas_call(
        functools.partial(kernel, dims),
        out_shape=(pltpu.VMEM(flow_start.shape, F32), pltpu.VMEM(capacity.shape, F32)),
        in_specs=[pl.BlockSpec(memory_space=pltpu.SMEM)] + [pl.BlockSpec(memory_space=pltpu.HBM)] * (len(scalars) + len(arrays)),
        out_specs=[pl.BlockSpec(memory_space=pltpu.VMEM)] * 2,
        scratch_shapes=[pltpu.SMEM(x.shape, I32) for x in scalars] + [pltpu.VMEM(x.shape, F32) for x in arrays] + [
            pltpu.VMEM((incs * paths, width), BF16),
            pltpu.VMEM((width, incs * paths), BF16),
            pltpu.VMEM((128, 512), BF16),
            pltpu.VMEM((512, 128), BF16),
            pltpu.VMEM((2, 128, 128), BF16),
            pltpu.VMEM((2, 128, 256), BF16),
            pltpu.VMEM((shards, 8, 128), F32),
            pltpu.VMEM((2, shards, 8, 128), F32),
            pltpu.VMEM((2, 16, 8, 128), F32),
            pltpu.VMEM((16, 8, 128), F32),
            pltpu.VMEM((shards, 8, 128), F32),
            pltpu.VMEM((2, 2, shards, 8, 128), F32),
            pltpu.VMEM((8, 128), F32),
            pltpu.VMEM((clusters, 8, 128), F32),
            pltpu.VMEM((4, 128), F32),
            pltpu.VMEM((ITERS + 1, clusters, 4, 128), F32),
            pltpu.VMEM((32, 128), F32),
            pltpu.VMEM((2, 32, 128), F32),
            pltpu.VMEM((2, 2, 32, 128), F32),
            pltpu.VMEM((2, 2, 2, 32, 128), F32),
            pltpu.VMEM((32, 128), F32),
            dma((10,)), dma(()), dma((2,)), dma(()), dma(()), dma((2,)), dma((2,)), dma(()),
            dma((2,)), dma((2,)), dma(()), dma((2, 2)), dma(()), dma((ITERS + 1,)), dma((2, 2)), dma((2, 2)), dma(()),
        ],
        compiler_params=pltpu.CompilerParams(
            collective_id=0, has_side_effects=True, vmem_limit_bytes=24 * 1024 * 1024),
    )(cluster_size, *(pltpu.with_memory_space_constraint(x, pltpu.HBM) for x in scalars + arrays))
    return pl.pallas_call(
        write_out,
        out_shape=(jax.ShapeDtypeStruct(flow_start.shape, F32), jax.ShapeDtypeStruct(capacity.shape, F32)),
        in_specs=[pl.BlockSpec(memory_space=pltpu.VMEM)] * 2,
        out_specs=[pl.BlockSpec(memory_space=pltpu.HBM)] * 2,
        scratch_shapes=[dma((2,))],
    )(*(pltpu.with_memory_space_constraint(x, pltpu.VMEM) for x in results))


def solution(mesh):
    both = P(("cluster", "shard"))
    rows = P(("cluster", "shard"), None)
    return jax.shard_map(
        body,
        mesh=mesh,
        in_specs=(rows, rows, rows, both, P("cluster"), P(("cluster", "shard"), None, None), both, both, rows, rows, P("cluster", None)),
        out_specs=(rows, rows),
        check_vma=False,
    )
```

```python
import functools

import jax
import jax.numpy as jnp
from jax import lax
from jax.experimental import pallas as pl
from jax.experimental.pallas import tpu as pltpu
from jax.sharding import PartitionSpec as P

ITERS = 3
GRID = (4, 2, 4)
MESH = pl.DeviceIdType.MESH
F32, BF16, I32 = jnp.float32, jnp.bfloat16, jnp.int32


def iota(shape, axis):
    return lax.broadcasted_iota(I32, shape, axis)


def thirds(x):
    high = x.astype(BF16).astype(F32)
    rest = x - high
    mid = rest.astype(BF16).astype(F32)
    return high, mid, rest - mid


def dot(a, b):
    return jnp.dot(a.astype(BF16), b.astype(BF16), preferred_element_type=F32)


def pick(selector, x):
    high, mid, low = thirds(x)
    x = dot(selector, jnp.concatenate([low, mid, high], axis=1))
    return (x[:, :128] + x[:, 128:256]) + x[:, 256:]


def hops(offset):
    return sum(min(d, n - d) for d, n in zip(offset, GRID))


NEAR = sorted(((x, z, y) for x in range(4) for z in range(2) for y in range(4) if hops((x, z, y)) <= 2), key=hops)
BACK = [NEAR.index(tuple(-d % n for d, n in zip(offset, GRID))) for offset in NEAR]


def distance(u):
    return hops(NEAR[u]) if u < 16 else 5 - hops(NEAR[u - 16])


def place_x(u):
    return NEAR[u][0] if u < 16 else (NEAR[u - 16][0] + 2) % 4


FAR_FIRST = sorted(range(1, 32), key=lambda u: (-distance(u), -min(place_x(u), 4 - place_x(u))))
NEAR_FAR_FIRST = [u for u in FAR_FIRST if u < 16]
DISTANT = [u for u in FAR_FIRST if u >= 16]


def kernel(
    dims,
    cluster_size, path_count_hbm, inc_path_hbm, inc_edge_hbm, partner_hbm,
    flow_start_hbm, demand_hbm, utility_hbm, incidence_hbm, capacity_hbm, dual_start_hbm,
    flows_out, duals_out,
    path_count, inc_path, inc_edge, partner,
    flow_start, demand, utility, incidence, capacity, dual_start,
    inc, inc_t, slot_edge, slot_edge_t, choose, choose_t,
    ask_send, ask_recv, flow_send, flow_recv, sum_send, sum_recv,
    edge_send, edge_recv, border_send, border_recv, own_start, own_bounds, state, bounds, final,
    load_sem, spread_send, share_send, edge_sent, border_sent, start_sent, bounds_sent, final_sent,
    ask_sem, distant_sem, flow_sem, sum_sem, edge_sem, border_sem, start_sem, bounds_sem, final_sem,
):
    clusters, shards, blocks, paths, incs, edges, slots, norm_bound, unit = dims
    step_size = 1.0 / (2.0 * norm_bound)
    cluster, shard = lax.axis_index("cluster"), lax.axis_index("shard")
    interior = edges - slots

    core = lax.rem(cluster, 2)
    even = cluster - core
    host = even + 1

    barrier = pltpu.get_barrier_semaphore()

    def greet(peer_cluster, peer_shard):
        pl.semaphore_signal(barrier, inc=1, device_id=(peer_cluster, peer_shard), device_id_type=MESH)

    def greet_hosts(k, _):
        greet(host, lax.rem(shard + k, shards))
        return 0

    def greet_even(k, _):
        greet(even, lax.rem(shard + k, shards))
        return 0

    def greet_cluster(k, _):
        greet(lax.rem(cluster + k + 1 - core, clusters), shard)
        return 0

    lax.fori_loop(1, shards, greet_hosts, 0)

    @pl.when(core == 0)
    def _():
        greet(host, shard)

    @pl.when(core == 1)
    def _():
        lax.fori_loop(0, shards, greet_even, 0)

    lax.fori_loop(1, clusters - 1, greet_cluster, 0)

    loads = [
        pltpu.make_async_copy(src, dst, load_sem.at[n])
        for n, (src, dst) in enumerate((
            (inc_path_hbm, inc_path), (capacity_hbm, capacity), (dual_start_hbm, dual_start),
            (path_count_hbm, path_count), (flow_start_hbm, flow_start),
            (demand_hbm, demand), (utility_hbm, utility), (inc_edge_hbm, inc_edge), (partner_hbm, partner),
            (incidence_hbm, incidence)))]
    for copy in loads:
        copy.start()

    at_x = [lax.rem(shard // 8 + d, 4) * 8 for d in range(4)]
    at_z = [lax.rem(shard // 4 + d, 2) * 4 for d in range(2)]
    at_y = [lax.rem(shard + d, 4) for d in range(4)]
    near = [at_x[x] + at_z[z] + at_y[y] for x, z, y in NEAR]

    def other_end(index):
        return lax.rem(index // 8 + 2, 4) * 8 + lax.rem(index // 4 + 1, 2) * 4 + lax.rem(index + 2, 4)

    far = [other_end(index) for index in near]

    def remote(src, dst, sent, arrived, peer_cluster, peer_shard):
        return pltpu.make_async_remote_copy(
            src_ref=src, dst_ref=dst, send_sem=sent, recv_sem=arrived,
            device_id=(peer_cluster, peer_shard), device_id_type=MESH)

    def to_hosts(places, src, dst, arrived):
        for u in places:
            peer, place = (near[u], BACK[u]) if u < 16 else (far[u - 16], 16 + BACK[u - 16])
            remote(src.at[u], dst.at[place], spread_send, arrived, host, peer).start()

    def to_own_host(src, dst, arrived):
        @pl.when(core == 0)
        def _():
            remote(src.at[0], dst.at[0], spread_send, arrived, host, shard).start()

        @pl.when(core == 1)
        def _():
            dst[0] = src[0]

    def to_clusters(src, dst, sent, arrived):
        for k in (4, 3, 5, 2, 6, 1, 7):
            remote(src, dst.at[cluster], sent, arrived, lax.rem(cluster + k, clusters), shard).start()
        dst[cluster] = src[...]

    def wait_recv(dst, arrived):
        remote(dst, dst, spread_send, arrived, cluster, far[0]).wait_recv()

    def wait_send(src, sent):
        remote(src, src, sent, final_sem, cluster, far[0]).wait_send()

    def hosts_reached(src):
        @pl.when(core == 0)
        def _():
            wait_send(src, spread_send)

        @pl.when(core == 1)
        def _():
            wait_send(src.at[pl.ds(0, shards - 1)], spread_send)

    tile_role = iota((8, 128), 0) >> 2
    rows, lanes = iota((128, 128), 0), iota((128, 128), 1)
    row_slot, row_half = (rows >> 1) & 1, rows & 1
    row_dev = jnp.concatenate([jnp.where(tile_role == 0, near[q], far[q]) for q in range(16)], axis=0)
    lane1 = iota((1, 128), 1)
    loads[0].wait()
    lane_path = jnp.full((1, 128), -1, I32)
    for i in range(incs):
        lane_path = jnp.where(lane1 == i, inc_path[i], lane_path)
    owner = (lane_path >> 4) == row_dev
    before = dot(owner.astype(F32), (rows < lanes).astype(F32))
    slot = owner & (before == row_slot.astype(F32))

    def fill(dst, x):
        for q in range(16):
            tile = x[q * 8:q * 8 + 8]
            dst[q] = tile
            dst[16 + q] = pltpu.roll(tile, 4, 0)

    wanted = jnp.sum(jnp.where(slot, (lane_path & 15) + 1, 0).astype(F32), axis=1, keepdims=True) - 1.0
    fill(ask_send, jnp.broadcast_to(wanted, (128, 128)))

    def border_first(ref):
        x = ref[...]
        return jnp.concatenate([x[interior:], jnp.zeros((8 - edges, x.shape[1]), F32), x[:interior]], axis=0)

    loads[1].wait()
    loads[2].wait()
    cap = border_first(capacity)
    dual = border_first(dual_start)
    edge_send[...] = jnp.concatenate([cap[:4], dual[:4]], axis=0)

    def halves(ref):
        x = ref[...]
        return jnp.concatenate([x[:, :128], x[:, 128:]], axis=0)

    for copy in loads[3:7]:
        copy.wait()
    row32 = iota((32, 128), 0)
    count = jnp.zeros((32, 128), I32)
    for b in range(blocks):
        count = jnp.where((row32 & 15) == b, path_count[b], count)
    live = (((row32 & 15) < cluster_size[0]) & ((row32 >> 4) * 128 + iota((32, 128), 1) < count)).astype(F32)
    top = halves(demand) * live
    own_start[...] = jnp.minimum(jnp.maximum(halves(flow_start), 0.0), top)
    own_bounds[0] = top
    own_bounds[1] = halves(utility)

    def to_both(src, dst, sent, arrived):
        remote(src, dst.at[core, 1], sent.at[1], arrived.at[core, 1], host, far[0]).start()

        @pl.when(core == 0)
        def _():
            remote(src, dst.at[core, 0], sent.at[0], arrived.at[core, 0], host, shard).start()

        @pl.when(core == 1)
        def _():
            dst[core, 0] = src[...]

    pl.semaphore_wait(barrier, shards + clusters - 2 + (shards - 1) * core)
    to_both(own_start, state, start_sent, start_sem)
    to_hosts(NEAR_FAR_FIRST, ask_send, ask_recv.at[core], ask_sem.at[core])
    to_own_host(ask_send, ask_recv.at[core], ask_sem.at[core])
    to_clusters(edge_send, edge_recv, edge_sent, edge_sem)

    loads[7].wait()
    lane_q = iota((1, 512), 1)
    lane_edge = jnp.full((1, 512), -1, I32)
    for i in range(incs):
        lane_edge = jnp.where((lane_q >> 4) == i, (inc_edge[i] + (8 - interior)) & 7, lane_edge)
    spread = (iota((128, 512), 0) == (iota((128, 512), 1) >> 4)).astype(F32)
    fits = (lane_edge == (lane_q & 7)) & (((lane_q >> 3) & 1) == (iota((128, 512), 0) & 1))
    both = jnp.where(fits, dot(slot.astype(F32), spread), 0.0)
    slot_edge[...] = both.astype(BF16)
    slot_edge_t[...] = both.T.astype(BF16)

    loads[8].wait()
    partner_row = jnp.full((4, 128), -1, I32)
    for k in range(slots):
        partner_row = jnp.where(iota((4, 128), 0) == k, partner[0, k], partner_row)
    partner8 = jnp.concatenate([partner_row, partner_row], axis=0)

    to_hosts(DISTANT, ask_send, ask_recv.at[core], distant_sem.at[core])
    to_both(own_bounds, bounds, bounds_sent, bounds_sem)

    loads[9].wait()

    def shrink(i, _):
        at = pl.ds(pl.multiple_of(i * paths, paths), paths)
        block = incidence[i].astype(BF16)
        inc[at, :] = block
        inc_t[:, at] = block.T
        return 0
    lax.fori_loop(0, incs, shrink, 0)

    def from_holders(src, c, arrived):
        wait_recv(src if c == 0 else src.at[pl.ds(0, shards - 1)], arrived)

    def share(c, flows):
        x = pick(choose[c, :, :64], flows)
        for q in range(16):
            flow_send[c, q] = x[q * 8:q * 8 + 8]
        for u in NEAR_FAR_FIRST + ([0] if c == 0 else []):
            remote(flow_send.at[c, u], flow_recv.at[BACK[u]], share_send.at[c], flow_sem, even + c, near[u]).start()
        if c == 1:
            flow_recv[0] = flow_send[c, 0]

    def shared():
        for c in range(2):
            wait_send(flow_send.at[c] if c == 0 else flow_send.at[c, pl.ds(0, 15)], share_send.at[c])

    @pl.when(core == 1)
    def _():
        rows2, lanes2 = iota((256, 128), 0), iota((256, 128), 1)
        fit = (((lanes2 >> 4) & 1) == (rows2 & 1)) & ((lanes2 >> 5) == ((rows2 >> 2) & 1))
        block_of_lane = (lanes2 & 15).astype(F32)
        for c in range(2):
            wait_recv(ask_recv.at[c, pl.ds(0, 16 - c)], ask_sem.at[c])
            chosen = (ask_recv[c, :16].reshape(128, 128) == block_of_lane[:128]) & fit[:128]
            choose[c] = chosen.astype(F32).astype(BF16)
        for c in range(2):
            for role in range(c, 2):
                wait_recv(state.at[c, role], start_sem.at[c, role])
            share(c, state[c].reshape(64, 128))
        for c in range(2):
            wait_recv(ask_recv.at[c, pl.ds(16, 16)], distant_sem.at[c])
            chosen = (ask_recv[c].reshape(256, 128) == block_of_lane) & fit
            choose_t[c] = chosen.astype(F32).T.astype(BF16)
            for role in range(c, 2):
                wait_recv(bounds.at[c, role], bounds_sem.at[c, role])

    def total_load(t):
        @pl.when(core == 0)
        def _():
            wait_recv(flow_recv, flow_sem)

        @pl.when(core == 1)
        def _():
            wait_recv(flow_recv.at[pl.ds(0, 15)], flow_sem)

        got = flow_recv[...].reshape(128, 128)
        parts = dot(slot_edge_t[...], jnp.concatenate(thirds(got), axis=1))
        columns = []
        for q in range(2 * incs):
            chunk = parts[q * 8:q * 8 + 8]
            columns.append(jnp.concatenate([chunk[:, :128], chunk[:, 128:256], chunk[:, 256:]], axis=0).astype(BF16))
        sums = dot(jnp.concatenate(columns, axis=1), inc[...])
        own = (sums[16:] + sums[8:16]) + sums[:8]
        border_send[...] = own[:4]
        to_clusters(border_send, border_recv.at[t], border_sent, border_sem.at[t])
        wait_recv(border_recv.at[t, pl.ds(0, clusters - 1)], border_sem.at[t])
        twin = jnp.zeros((4, 128), F32)
        for c in range(clusters):
            twin = twin + jnp.where(partner_row == c, border_recv[t, c], 0.0)
        return jnp.concatenate([own[:4] + twin, own[4:]], axis=0)

    def settle(load, duals):
        split = jnp.minimum(limit, load + duals)
        duals = (duals + load) - split
        return (load - split) + duals, duals

    wait_recv(edge_recv.at[pl.ds(0, clusters - 1)], edge_sem)
    twin = jnp.zeros((8, 128), F32)
    for c in range(clusters):
        twin = twin + jnp.where(partner8 == c, edge_recv[c], 0.0)
    limit = unit * jnp.concatenate([0.5 * (cap[:4] + twin[:4]), cap[4:]], axis=0)
    duals = jnp.concatenate([0.5 * (dual[:4] + twin[4:]), dual[4:]], axis=0)

    residual, duals = settle(total_load(0), duals)

    hosts_reached(ask_send)
    wait_send(edge_recv.at[pl.ds(0, clusters - 1)], edge_sent)
    for src, sem in ((own_start, start_sent), (own_bounds, bounds_sent)):
        wait_send(src, sem.at[1])

        @pl.when(core == 0)
        def _():
            wait_send(src, sem.at[0])

    def iterate(t, carry):
        residual, duals = carry
        turn = lax.rem(t, 2)
        parts = dot(jnp.concatenate(thirds(residual), axis=0), inc_t[...])
        back = (parts[16:] + parts[8:16]) + parts[:8]
        back = jnp.concatenate([back[:, q * 128:q * 128 + 128] for q in range(2 * incs)], axis=0)
        sums = pick(slot_edge[...], back)
        for q in range(16):
            sum_send[16 + q] = pltpu.roll(sums[q * 8:q * 8 + 8], 4, 0)
        to_hosts(DISTANT, sum_send, sum_recv.at[turn, core], sum_sem.at[turn, core])
        for q in range(16):
            sum_send[q] = sums[q * 8:q * 8 + 8]
        to_hosts(NEAR_FAR_FIRST, sum_send, sum_recv.at[turn, core], sum_sem.at[turn, core])
        to_own_host(sum_send, sum_recv.at[turn, core], sum_sem.at[turn, core])
        wait_send(border_recv.at[t, pl.ds(0, clusters - 1)], border_sent)

        @pl.when(core == 1)
        def _():
            shared()
            for c in range(2):
                from_holders(sum_recv.at[turn, c], c, sum_sem.at[turn, c])
                grad = pick(choose_t[c, :64, :], sum_recv[turn, c].reshape(256, 128))
                top = bounds[c, :, 0].reshape(64, 128)
                gain = bounds[c, :, 1].reshape(64, 128)
                flows = state[c].reshape(64, 128)
                flows = jnp.minimum(jnp.maximum(flows - step_size * (grad - gain), 0.0), top)
                share(c, flows)
                state[c] = flows.reshape(2, 32, 128)

            @pl.when(t == ITERS)
            def _():
                remote(state.at[0, 0], final, final_sent, final_sem, even, shard).start()

        hosts_reached(sum_send)
        return settle(total_load(t), duals)

    residual, duals = lax.fori_loop(1, ITERS + 1, iterate, (residual, duals))
    wait_send(border_recv.at[0, pl.ds(0, clusters - 1)], border_sent)

    @pl.when(core == 0)
    def _():
        wait_recv(final, final_sem)

    @pl.when(core == 1)
    def _():
        shared()
        wait_send(state.at[0, 0], final_sent)
        final[...] = state[1, 0]

    flows = final[...]
    flows_out[...] = jnp.concatenate([flows[:16], flows[16:]], axis=1)
    duals_out[...] = jnp.concatenate([duals[4:], duals[:slots]], axis=0)


def write_out(flows, duals, flows_out, duals_out, sems):
    copies = [pltpu.make_async_copy(flows, flows_out, sems.at[0]), pltpu.make_async_copy(duals, duals_out, sems.at[1])]
    for copy in copies:
        copy.start()
    for copy in copies:
        copy.wait()


def body(flow_start, demand, utility, path_count, cluster_size, incidence, inc_path, inc_edge, capacity, dual_start, partner):
    blocks, paths = flow_start.shape
    incs, _, width = incidence.shape
    edges, slots = capacity.shape[0], partner.shape[1]
    clusters, shards = lax.axis_size("cluster"), lax.axis_size("shard")
    norm_bound = max(2, incs * incs * paths * width // (1024 * edges * blocks))
    unit = float(max(1, incs * paths // (160 * edges)))
    dims = (clusters, shards, blocks, paths, incs, edges, slots, norm_bound, unit)
    scalars = (path_count, inc_path, inc_edge, partner)
    arrays = (flow_start, demand, utility, incidence, capacity, dual_start)
    dma = pltpu.SemaphoreType.DMA
    results = pl.pallas_call(
        functools.partial(kernel, dims),
        out_shape=(pltpu.VMEM(flow_start.shape, F32), pltpu.VMEM(capacity.shape, F32)),
        in_specs=[pl.BlockSpec(memory_space=pltpu.SMEM)] + [pl.BlockSpec(memory_space=pltpu.HBM)] * (len(scalars) + len(arrays)),
        out_specs=[pl.BlockSpec(memory_space=pltpu.VMEM)] * 2,
        scratch_shapes=[pltpu.SMEM(x.shape, I32) for x in scalars] + [pltpu.VMEM(x.shape, F32) for x in arrays] + [
            pltpu.VMEM((incs * paths, width), BF16),
            pltpu.VMEM((width, incs * paths), BF16),
            pltpu.VMEM((128, 512), BF16),
            pltpu.VMEM((512, 128), BF16),
            pltpu.VMEM((2, 128, 128), BF16),
            pltpu.VMEM((2, 128, 256), BF16),
            pltpu.VMEM((shards, 8, 128), F32),
            pltpu.VMEM((2, shards, 8, 128), F32),
            pltpu.VMEM((2, 16, 8, 128), F32),
            pltpu.VMEM((16, 8, 128), F32),
            pltpu.VMEM((shards, 8, 128), F32),
            pltpu.VMEM((2, 2, shards, 8, 128), F32),
            pltpu.VMEM((8, 128), F32),
            pltpu.VMEM((clusters, 8, 128), F32),
            pltpu.VMEM((4, 128), F32),
            pltpu.VMEM((ITERS + 1, clusters, 4, 128), F32),
            pltpu.VMEM((32, 128), F32),
            pltpu.VMEM((2, 32, 128), F32),
            pltpu.VMEM((2, 2, 32, 128), F32),
            pltpu.VMEM((2, 2, 2, 32, 128), F32),
            pltpu.VMEM((32, 128), F32),
            dma((10,)), dma(()), dma((2,)), dma(()), dma(()), dma((2,)), dma((2,)), dma(()),
            dma((2,)), dma((2,)), dma(()), dma((2, 2)), dma(()), dma((ITERS + 1,)), dma((2, 2)), dma((2, 2)), dma(()),
        ],
        compiler_params=pltpu.CompilerParams(
            collective_id=0, has_side_effects=True, vmem_limit_bytes=24 * 1024 * 1024),
    )(cluster_size, *(pltpu.with_memory_space_constraint(x, pltpu.HBM) for x in scalars + arrays))
    return pl.pallas_call(
        write_out,
        out_shape=(jax.ShapeDtypeStruct(flow_start.shape, F32), jax.ShapeDtypeStruct(capacity.shape, F32)),
        in_specs=[pl.BlockSpec(memory_space=pltpu.VMEM)] * 2,
        out_specs=[pl.BlockSpec(memory_space=pltpu.HBM)] * 2,
        scratch_shapes=[dma((2,))],
    )(*(pltpu.with_memory_space_constraint(x, pltpu.VMEM) for x in results))


def solution(mesh):
    both = P(("cluster", "shard"))
    rows = P(("cluster", "shard"), None)
    return jax.shard_map(
        body,
        mesh=mesh,
        in_specs=(rows, rows, rows, both, P("cluster"), P(("cluster", "shard"), None, None), both, both, rows, rows, P("cluster", None)),
        out_specs=(rows, rows),
        check_vma=False,
    )
```

```python
import functools

import jax
import jax.numpy as jnp
from jax import lax
from jax.experimental import pallas as pl
from jax.experimental.pallas import tpu as pltpu
from jax.sharding import PartitionSpec as P

ITERS = 3
GRID = (4, 2, 4)
MESH = pl.DeviceIdType.MESH
F32, BF16, I32 = jnp.float32, jnp.bfloat16, jnp.int32


def iota(shape, axis):
    return lax.broadcasted_iota(I32, shape, axis)


def thirds(x):
    high = x.astype(BF16).astype(F32)
    rest = x - high
    mid = rest.astype(BF16).astype(F32)
    return high, mid, rest - mid


def dot(a, b):
    return jnp.dot(a.astype(BF16), b.astype(BF16), preferred_element_type=F32)


def pick(selector, x):
    high, mid, low = thirds(x)
    x = dot(selector, jnp.concatenate([low, mid, high], axis=1))
    return (x[:, :128] + x[:, 128:256]) + x[:, 256:]


def hops(offset):
    return sum(min(d, n - d) for d, n in zip(offset, GRID))


NEAR = sorted(((x, z, y) for x in range(4) for z in range(2) for y in range(4) if hops((x, z, y)) <= 2), key=hops)
BACK = [NEAR.index(tuple(-d % n for d, n in zip(offset, GRID))) for offset in NEAR]


def distance(u):
    return hops(NEAR[u]) if u < 16 else 5 - hops(NEAR[u - 16])


def place_x(u):
    return NEAR[u][0] if u < 16 else (NEAR[u - 16][0] + 2) % 4


FAR_FIRST = sorted(range(1, 32), key=lambda u: (-distance(u), -min(place_x(u), 4 - place_x(u))))
NEAR_FAR_FIRST = [u for u in FAR_FIRST if u < 16]
DISTANT = [u for u in FAR_FIRST if u >= 16]


def kernel(
    dims,
    cluster_size, path_count_hbm, inc_path_hbm, inc_edge_hbm, partner_hbm,
    flow_start_hbm, demand_hbm, utility_hbm, incidence_hbm, capacity_hbm, dual_start_hbm,
    flows_out, duals_out,
    path_count, inc_path, inc_edge, partner,
    flow_start, demand, utility, incidence, capacity, dual_start,
    inc, inc_t, slot_edge, slot_edge_t, choose, choose_t,
    ask_send, ask_recv, flow_send, flow_recv, sum_send, sum_recv,
    edge_send, edge_recv, border_send, border_recv, own_start, own_bounds, state, bounds, final,
    load_sem, spread_send, share_send, edge_sent, border_sent, start_sent, bounds_sent, final_sent,
    ask_sem, distant_sem, flow_sem, sum_sem, edge_sem, border_sem, start_sem, bounds_sem, final_sem,
):
    clusters, shards, blocks, paths, incs, edges, slots, norm_bound, unit = dims
    step_size = 1.0 / (2.0 * norm_bound)
    cluster, shard = lax.axis_index("cluster"), lax.axis_index("shard")
    interior = edges - slots

    core = lax.rem(cluster, 2)
    even = cluster - core
    host = even + 1

    barrier = pltpu.get_barrier_semaphore()

    def greet(peer_cluster, peer_shard):
        pl.semaphore_signal(barrier, inc=1, device_id=(peer_cluster, peer_shard), device_id_type=MESH)

    def greet_hosts(k, _):
        greet(host, lax.rem(shard + k, shards))
        return 0

    def greet_even(k, _):
        greet(even, lax.rem(shard + k, shards))
        return 0

    def greet_cluster(k, _):
        greet(lax.rem(cluster + k + 1 - core, clusters), shard)
        return 0

    lax.fori_loop(1, shards, greet_hosts, 0)

    @pl.when(core == 0)
    def _():
        greet(host, shard)

    @pl.when(core == 1)
    def _():
        lax.fori_loop(0, shards, greet_even, 0)

    lax.fori_loop(1, clusters - 1, greet_cluster, 0)

    loads = [
        pltpu.make_async_copy(src, dst, load_sem.at[n])
        for n, (src, dst) in enumerate((
            (inc_path_hbm, inc_path), (capacity_hbm, capacity), (dual_start_hbm, dual_start),
            (path_count_hbm, path_count), (flow_start_hbm, flow_start),
            (demand_hbm, demand), (utility_hbm, utility), (inc_edge_hbm, inc_edge), (partner_hbm, partner),
            (incidence_hbm, incidence)))]
    for copy in loads:
        copy.start()

    at_x = [lax.rem(shard // 8 + d, 4) * 8 for d in range(4)]
    at_z = [lax.rem(shard // 4 + d, 2) * 4 for d in range(2)]
    at_y = [lax.rem(shard + d, 4) for d in range(4)]
    near = [at_x[x] + at_z[z] + at_y[y] for x, z, y in NEAR]

    def other_end(index):
        return lax.rem(index // 8 + 2, 4) * 8 + lax.rem(index // 4 + 1, 2) * 4 + lax.rem(index + 2, 4)

    far = [other_end(index) for index in near]

    def remote(src, dst, sent, arrived, peer_cluster, peer_shard):
        return pltpu.make_async_remote_copy(
            src_ref=src, dst_ref=dst, send_sem=sent, recv_sem=arrived,
            device_id=(peer_cluster, peer_shard), device_id_type=MESH)

    def to_hosts(places, src, dst, arrived):
        for u in places:
            peer, place = (near[u], BACK[u]) if u < 16 else (far[u - 16], 16 + BACK[u - 16])
            remote(src.at[u], dst.at[place], spread_send, arrived, host, peer).start()

    def to_own_host(src, dst, arrived):
        @pl.when(core == 0)
        def _():
            remote(src.at[0], dst.at[0], spread_send, arrived, host, shard).start()

        @pl.when(core == 1)
        def _():
            dst[0] = src[0]

    def to_clusters(src, dst, sent, arrived):
        for k in (4, 3, 5, 2, 6, 1, 7):
            remote(src, dst.at[cluster], sent, arrived, lax.rem(cluster + k, clusters), shard).start()
        dst[cluster] = src[...]

    def wait_recv(dst, arrived):
        remote(dst, dst, spread_send, arrived, cluster, far[0]).wait_recv()

    def wait_send(src, sent):
        remote(src, src, sent, final_sem, cluster, far[0]).wait_send()

    def hosts_reached(src):
        @pl.when(core == 0)
        def _():
            wait_send(src, spread_send)

        @pl.when(core == 1)
        def _():
            wait_send(src.at[pl.ds(0, shards - 1)], spread_send)

    tile_role = iota((8, 128), 0) >> 2
    rows, lanes = iota((128, 128), 0), iota((128, 128), 1)
    row_slot, row_half = (rows >> 1) & 1, rows & 1
    row_dev = jnp.concatenate([jnp.where(tile_role == 0, near[q], far[q]) for q in range(16)], axis=0)
    lane1 = iota((1, 128), 1)
    loads[0].wait()
    lane_path = jnp.full((1, 128), -1, I32)
    for i in range(incs):
        lane_path = jnp.where(lane1 == i, inc_path[i], lane_path)
    owner = (lane_path >> 4) == row_dev
    before = dot(owner.astype(F32), (rows < lanes).astype(F32))
    slot = owner & (before == row_slot.astype(F32))

    def fill(dst, x):
        for q in range(16):
            tile = x[q * 8:q * 8 + 8]
            dst[q] = tile
            dst[16 + q] = pltpu.roll(tile, 4, 0)

    wanted = jnp.sum(jnp.where(slot, (lane_path & 15) + 1, 0).astype(F32), axis=1, keepdims=True) - 1.0
    fill(ask_send, jnp.broadcast_to(wanted, (128, 128)))

    def border_first(ref):
        x = ref[...]
        return jnp.concatenate([x[interior:], jnp.zeros((8 - edges, x.shape[1]), F32), x[:interior]], axis=0)

    loads[1].wait()
    loads[2].wait()
    cap = border_first(capacity)
    dual = border_first(dual_start)
    edge_send[...] = jnp.concatenate([cap[:4], dual[:4]], axis=0)

    def halves(ref):
        x = ref[...]
        return jnp.concatenate([x[:, :128], x[:, 128:]], axis=0)

    for copy in loads[3:7]:
        copy.wait()
    row32 = iota((32, 128), 0)
    count = jnp.zeros((32, 128), I32)
    for b in range(blocks):
        count = jnp.where((row32 & 15) == b, path_count[b], count)
    live = (((row32 & 15) < cluster_size[0]) & ((row32 >> 4) * 128 + iota((32, 128), 1) < count)).astype(F32)
    top = halves(demand) * live
    own_start[...] = jnp.minimum(jnp.maximum(halves(flow_start), 0.0), top)
    own_bounds[0] = top
    own_bounds[1] = halves(utility)

    def to_both(src, dst, sent, arrived):
        remote(src, dst.at[core, 1], sent.at[1], arrived.at[core, 1], host, far[0]).start()

        @pl.when(core == 0)
        def _():
            remote(src, dst.at[core, 0], sent.at[0], arrived.at[core, 0], host, shard).start()

        @pl.when(core == 1)
        def _():
            dst[core, 0] = src[...]

    pl.semaphore_wait(barrier, shards + clusters - 2 + (shards - 1) * core)
    to_both(own_start, state, start_sent, start_sem)
    to_hosts(NEAR_FAR_FIRST, ask_send, ask_recv.at[core], ask_sem.at[core])
    to_own_host(ask_send, ask_recv.at[core], ask_sem.at[core])
    to_clusters(edge_send, edge_recv, edge_sent, edge_sem)

    loads[7].wait()
    lane_q = iota((1, 512), 1)
    lane_edge = jnp.full((1, 512), -1, I32)
    for i in range(incs):
        lane_edge = jnp.where((lane_q >> 4) == i, (inc_edge[i] + (8 - interior)) & 7, lane_edge)
    spread = (iota((128, 512), 0) == (iota((128, 512), 1) >> 4)).astype(F32)
    fits = (lane_edge == (lane_q & 7)) & (((lane_q >> 3) & 1) == (iota((128, 512), 0) & 1))
    both = jnp.where(fits, dot(slot.astype(F32), spread), 0.0)
    slot_edge[...] = both.astype(BF16)
    slot_edge_t[...] = both.T.astype(BF16)

    loads[8].wait()
    partner_row = jnp.full((4, 128), -1, I32)
    for k in range(slots):
        partner_row = jnp.where(iota((4, 128), 0) == k, partner[0, k], partner_row)
    partner8 = jnp.concatenate([partner_row, partner_row], axis=0)

    to_hosts(DISTANT, ask_send, ask_recv.at[core], distant_sem.at[core])
    to_both(own_bounds, bounds, bounds_sent, bounds_sem)

    loads[9].wait()

    def shrink(i, _):
        at = pl.ds(pl.multiple_of(i * paths, paths), paths)
        block = incidence[i].astype(BF16)
        inc[at, :] = block
        inc_t[:, at] = block.T
        return 0
    lax.fori_loop(0, incs, shrink, 0)

    def from_holders(src, c, arrived):
        wait_recv(src if c == 0 else src.at[pl.ds(0, shards - 1)], arrived)

    def share(c, flows):
        x = pick(choose[c, :, :64], flows)
        for places in ([u for u in NEAR_FAR_FIRST if distance(u) == 2], [u for u in NEAR_FAR_FIRST if distance(u) == 1] + [0]):
            for u in places:
                flow_send[c, u] = x[u * 8:u * 8 + 8]
            for u in places:
                if u == 0 and c == 1:
                    flow_recv[0] = x[:8]
                else:
                    remote(flow_send.at[c, u], flow_recv.at[BACK[u]], share_send.at[c], flow_sem, even + c, near[u]).start()

    def shared():
        for c in range(2):
            wait_send(flow_send.at[c] if c == 0 else flow_send.at[c, pl.ds(0, 15)], share_send.at[c])

    @pl.when(core == 1)
    def _():
        rows2, lanes2 = iota((256, 128), 0), iota((256, 128), 1)
        fit = (((lanes2 >> 4) & 1) == (rows2 & 1)) & ((lanes2 >> 5) == ((rows2 >> 2) & 1))
        block_of_lane = (lanes2 & 15).astype(F32)
        for c in range(2):
            wait_recv(ask_recv.at[c, pl.ds(0, 16 - c)], ask_sem.at[c])
            chosen = (ask_recv[c, :16].reshape(128, 128) == block_of_lane[:128]) & fit[:128]
            choose[c] = chosen.astype(F32).astype(BF16)
        for c in range(2):
            for role in range(c, 2):
                wait_recv(state.at[c, role], start_sem.at[c, role])
            share(c, state[c].reshape(64, 128))
        for c in range(2):
            wait_recv(ask_recv.at[c, pl.ds(16, 16)], distant_sem.at[c])
            chosen = (ask_recv[c].reshape(256, 128) == block_of_lane) & fit
            choose_t[c] = chosen.astype(F32).T.astype(BF16)
            for role in range(c, 2):
                wait_recv(bounds.at[c, role], bounds_sem.at[c, role])

    def total_load(t):
        @pl.when(core == 0)
        def _():
            wait_recv(flow_recv, flow_sem)

        @pl.when(core == 1)
        def _():
            wait_recv(flow_recv.at[pl.ds(0, 15)], flow_sem)

        got = flow_recv[...].reshape(128, 128)
        parts = dot(slot_edge_t[...], jnp.concatenate(thirds(got), axis=1))
        columns = []
        for q in range(2 * incs):
            chunk = parts[q * 8:q * 8 + 8]
            columns.append(jnp.concatenate([chunk[:, :128], chunk[:, 128:256], chunk[:, 256:]], axis=0).astype(BF16))
        sums = dot(jnp.concatenate(columns, axis=1), inc[...])
        own = (sums[16:] + sums[8:16]) + sums[:8]
        border_send[...] = own[:4]
        to_clusters(border_send, border_recv.at[t], border_sent, border_sem.at[t])
        wait_recv(border_recv.at[t, pl.ds(0, clusters - 1)], border_sem.at[t])
        twin = jnp.zeros((4, 128), F32)
        for c in range(clusters):
            twin = twin + jnp.where(partner_row == c, border_recv[t, c], 0.0)
        return jnp.concatenate([own[:4] + twin, own[4:]], axis=0)

    def settle(load, duals):
        split = jnp.minimum(limit, load + duals)
        duals = (duals + load) - split
        return (load - split) + duals, duals

    wait_recv(edge_recv.at[pl.ds(0, clusters - 1)], edge_sem)
    twin = jnp.zeros((8, 128), F32)
    for c in range(clusters):
        twin = twin + jnp.where(partner8 == c, edge_recv[c], 0.0)
    limit = unit * jnp.concatenate([0.5 * (cap[:4] + twin[:4]), cap[4:]], axis=0)
    duals = jnp.concatenate([0.5 * (dual[:4] + twin[4:]), dual[4:]], axis=0)

    residual, duals = settle(total_load(0), duals)

    hosts_reached(ask_send)
    wait_send(edge_recv.at[pl.ds(0, clusters - 1)], edge_sent)
    for src, sem in ((own_start, start_sent), (own_bounds, bounds_sent)):
        wait_send(src, sem.at[1])

        @pl.when(core == 0)
        def _():
            wait_send(src, sem.at[0])

    def iterate(t, carry):
        residual, duals = carry
        turn = lax.rem(t, 2)
        parts = dot(jnp.concatenate(thirds(residual), axis=0), inc_t[...])
        back = (parts[16:] + parts[8:16]) + parts[:8]
        back = jnp.concatenate([back[:, q * 128:q * 128 + 128] for q in range(2 * incs)], axis=0)
        sums = pick(slot_edge[...], back)
        for q in range(16):
            sum_send[16 + q] = pltpu.roll(sums[q * 8:q * 8 + 8], 4, 0)
        to_hosts(DISTANT, sum_send, sum_recv.at[turn, core], sum_sem.at[turn, core])
        for q in range(16):
            sum_send[q] = sums[q * 8:q * 8 + 8]
        to_hosts(NEAR_FAR_FIRST, sum_send, sum_recv.at[turn, core], sum_sem.at[turn, core])
        to_own_host(sum_send, sum_recv.at[turn, core], sum_sem.at[turn, core])
        wait_send(border_recv.at[t, pl.ds(0, clusters - 1)], border_sent)

        @pl.when(core == 1)
        def _():
            shared()
            for c in range(2):
                from_holders(sum_recv.at[turn, c], c, sum_sem.at[turn, c])
                grad = pick(choose_t[c, :64, :], sum_recv[turn, c].reshape(256, 128))
                top = bounds[c, :, 0].reshape(64, 128)
                gain = bounds[c, :, 1].reshape(64, 128)
                flows = state[c].reshape(64, 128)
                flows = jnp.minimum(jnp.maximum(flows - step_size * (grad - gain), 0.0), top)
                share(c, flows)
                state[c] = flows.reshape(2, 32, 128)

            @pl.when(t == ITERS)
            def _():
                remote(state.at[0, 0], final, final_sent, final_sem, even, shard).start()

        hosts_reached(sum_send)
        return settle(total_load(t), duals)

    residual, duals = lax.fori_loop(1, ITERS + 1, iterate, (residual, duals))
    wait_send(border_recv.at[0, pl.ds(0, clusters - 1)], border_sent)

    @pl.when(core == 0)
    def _():
        wait_recv(final, final_sem)

    @pl.when(core == 1)
    def _():
        shared()
        wait_send(state.at[0, 0], final_sent)
        final[...] = state[1, 0]

    flows = final[...]
    flows_out[...] = jnp.concatenate([flows[:16], flows[16:]], axis=1)
    duals_out[...] = jnp.concatenate([duals[4:], duals[:slots]], axis=0)


def write_out(flows, duals, flows_out, duals_out, sems):
    copies = [pltpu.make_async_copy(flows, flows_out, sems.at[0]), pltpu.make_async_copy(duals, duals_out, sems.at[1])]
    for copy in copies:
        copy.start()
    for copy in copies:
        copy.wait()


def body(flow_start, demand, utility, path_count, cluster_size, incidence, inc_path, inc_edge, capacity, dual_start, partner):
    blocks, paths = flow_start.shape
    incs, _, width = incidence.shape
    edges, slots = capacity.shape[0], partner.shape[1]
    clusters, shards = lax.axis_size("cluster"), lax.axis_size("shard")
    norm_bound = max(2, incs * incs * paths * width // (1024 * edges * blocks))
    unit = float(max(1, incs * paths // (160 * edges)))
    dims = (clusters, shards, blocks, paths, incs, edges, slots, norm_bound, unit)
    scalars = (path_count, inc_path, inc_edge, partner)
    arrays = (flow_start, demand, utility, incidence, capacity, dual_start)
    dma = pltpu.SemaphoreType.DMA
    results = pl.pallas_call(
        functools.partial(kernel, dims),
        out_shape=(pltpu.VMEM(flow_start.shape, F32), pltpu.VMEM(capacity.shape, F32)),
        in_specs=[pl.BlockSpec(memory_space=pltpu.SMEM)] + [pl.BlockSpec(memory_space=pltpu.HBM)] * (len(scalars) + len(arrays)),
        out_specs=[pl.BlockSpec(memory_space=pltpu.VMEM)] * 2,
        scratch_shapes=[pltpu.SMEM(x.shape, I32) for x in scalars] + [pltpu.VMEM(x.shape, F32) for x in arrays] + [
            pltpu.VMEM((incs * paths, width), BF16),
            pltpu.VMEM((width, incs * paths), BF16),
            pltpu.VMEM((128, 512), BF16),
            pltpu.VMEM((512, 128), BF16),
            pltpu.VMEM((2, 128, 128), BF16),
            pltpu.VMEM((2, 128, 256), BF16),
            pltpu.VMEM((shards, 8, 128), F32),
            pltpu.VMEM((2, shards, 8, 128), F32),
            pltpu.VMEM((2, 16, 8, 128), F32),
            pltpu.VMEM((16, 8, 128), F32),
            pltpu.VMEM((shards, 8, 128), F32),
            pltpu.VMEM((2, 2, shards, 8, 128), F32),
            pltpu.VMEM((8, 128), F32),
            pltpu.VMEM((clusters, 8, 128), F32),
            pltpu.VMEM((4, 128), F32),
            pltpu.VMEM((ITERS + 1, clusters, 4, 128), F32),
            pltpu.VMEM((32, 128), F32),
            pltpu.VMEM((2, 32, 128), F32),
            pltpu.VMEM((2, 2, 32, 128), F32),
            pltpu.VMEM((2, 2, 2, 32, 128), F32),
            pltpu.VMEM((32, 128), F32),
            dma((10,)), dma(()), dma((2,)), dma(()), dma(()), dma((2,)), dma((2,)), dma(()),
            dma((2,)), dma((2,)), dma(()), dma((2, 2)), dma(()), dma((ITERS + 1,)), dma((2, 2)), dma((2, 2)), dma(()),
        ],
        compiler_params=pltpu.CompilerParams(
            collective_id=0, has_side_effects=True, vmem_limit_bytes=24 * 1024 * 1024),
    )(cluster_size, *(pltpu.with_memory_space_constraint(x, pltpu.HBM) for x in scalars + arrays))
    return pl.pallas_call(
        write_out,
        out_shape=(jax.ShapeDtypeStruct(flow_start.shape, F32), jax.ShapeDtypeStruct(capacity.shape, F32)),
        in_specs=[pl.BlockSpec(memory_space=pltpu.VMEM)] * 2,
        out_specs=[pl.BlockSpec(memory_space=pltpu.HBM)] * 2,
        scratch_shapes=[dma((2,))],
    )(*(pltpu.with_memory_space_constraint(x, pltpu.VMEM) for x in results))


def solution(mesh):
    both = P(("cluster", "shard"))
    rows = P(("cluster", "shard"), None)
    return jax.shard_map(
        body,
        mesh=mesh,
        in_specs=(rows, rows, rows, both, P("cluster"), P(("cluster", "shard"), None, None), both, both, rows, rows, P("cluster", None)),
        out_specs=(rows, rows),
        check_vma=False,
    )
```

```python
import functools

import jax
import jax.numpy as jnp
from jax import lax
from jax.experimental import pallas as pl
from jax.experimental.pallas import tpu as pltpu
from jax.sharding import PartitionSpec as P

ITERS = 3
GRID = (4, 2, 4)
MESH = pl.DeviceIdType.MESH
F32, BF16, I32 = jnp.float32, jnp.bfloat16, jnp.int32


def iota(shape, axis):
    return lax.broadcasted_iota(I32, shape, axis)


def thirds(x):
    high = x.astype(BF16).astype(F32)
    rest = x - high
    mid = rest.astype(BF16).astype(F32)
    return high, mid, rest - mid


def dot(a, b):
    return jnp.dot(a.astype(BF16), b.astype(BF16), preferred_element_type=F32)


def pick(selector, x):
    high, mid, low = thirds(x)
    x = dot(selector, jnp.concatenate([low, mid, high], axis=1))
    return (x[:, :128] + x[:, 128:256]) + x[:, 256:]


def hops(offset):
    return sum(min(d, n - d) for d, n in zip(offset, GRID))


NEAR = sorted(((x, z, y) for x in range(4) for z in range(2) for y in range(4) if hops((x, z, y)) <= 2), key=hops)
BACK = [NEAR.index(tuple(-d % n for d, n in zip(offset, GRID))) for offset in NEAR]


def distance(u):
    return hops(NEAR[u]) if u < 16 else 5 - hops(NEAR[u - 16])


def place_x(u):
    return NEAR[u][0] if u < 16 else (NEAR[u - 16][0] + 2) % 4


FAR_FIRST = sorted(range(1, 32), key=lambda u: (-distance(u), -min(place_x(u), 4 - place_x(u))))
NEAR_FAR_FIRST = [u for u in FAR_FIRST if u < 16]
DISTANT = [u for u in FAR_FIRST if u >= 16]


def kernel(
    dims,
    cluster_size, path_count_hbm, inc_path_hbm, inc_edge_hbm, partner_hbm,
    flow_start_hbm, demand_hbm, utility_hbm, incidence_hbm, capacity_hbm, dual_start_hbm,
    flows_out, duals_out,
    path_count, inc_path, inc_edge, partner,
    flow_start, demand, utility, incidence, capacity, dual_start,
    inc, inc_t, slot_edge, slot_edge_t, choose, choose_t,
    ask_send, ask_recv, flow_send, flow_recv, sum_send, sum_recv,
    edge_send, edge_recv, border_send, border_recv, own_start, own_bounds, state, bounds, final,
    load_sem, spread_send, share_send, edge_sent, border_sent, start_sent, bounds_sent, final_sent,
    ask_sem, distant_sem, flow_sem, sum_sem, edge_sem, border_sem, start_sem, bounds_sem, final_sem,
):
    clusters, shards, blocks, paths, incs, edges, slots, norm_bound, unit = dims
    step_size = 1.0 / (2.0 * norm_bound)
    cluster, shard = lax.axis_index("cluster"), lax.axis_index("shard")
    interior = edges - slots

    core = lax.rem(cluster, 2)
    even = cluster - core
    host = even + 1

    barrier = pltpu.get_barrier_semaphore()

    def greet(peer_cluster, peer_shard):
        pl.semaphore_signal(barrier, inc=1, device_id=(peer_cluster, peer_shard), device_id_type=MESH)

    def greet_hosts(k, _):
        greet(host, lax.rem(shard + k, shards))
        return 0

    def greet_even(k, _):
        greet(even, lax.rem(shard + k, shards))
        return 0

    def greet_cluster(k, _):
        greet(lax.rem(cluster + k + 1 - core, clusters), shard)
        return 0

    lax.fori_loop(1, shards, greet_hosts, 0)

    @pl.when(core == 0)
    def _():
        greet(host, shard)

    @pl.when(core == 1)
    def _():
        lax.fori_loop(0, shards, greet_even, 0)

    lax.fori_loop(1, clusters - 1, greet_cluster, 0)

    loads = [
        pltpu.make_async_copy(src, dst, load_sem.at[n])
        for n, (src, dst) in enumerate((
            (inc_path_hbm, inc_path), (capacity_hbm, capacity), (dual_start_hbm, dual_start),
            (path_count_hbm, path_count), (flow_start_hbm, flow_start),
            (demand_hbm, demand), (utility_hbm, utility), (inc_edge_hbm, inc_edge), (partner_hbm, partner),
            (incidence_hbm, incidence)))]
    for copy in loads:
        copy.start()

    at_x = [lax.rem(shard // 8 + d, 4) * 8 for d in range(4)]
    at_z = [lax.rem(shard // 4 + d, 2) * 4 for d in range(2)]
    at_y = [lax.rem(shard + d, 4) for d in range(4)]
    near = [at_x[x] + at_z[z] + at_y[y] for x, z, y in NEAR]

    def other_end(index):
        return lax.rem(index // 8 + 2, 4) * 8 + lax.rem(index // 4 + 1, 2) * 4 + lax.rem(index + 2, 4)

    far = [other_end(index) for index in near]

    def remote(src, dst, sent, arrived, peer_cluster, peer_shard):
        return pltpu.make_async_remote_copy(
            src_ref=src, dst_ref=dst, send_sem=sent, recv_sem=arrived,
            device_id=(peer_cluster, peer_shard), device_id_type=MESH)

    def to_hosts(places, src, dst, arrived):
        for u in places:
            peer, place = (near[u], BACK[u]) if u < 16 else (far[u - 16], 16 + BACK[u - 16])
            remote(src.at[u], dst.at[place], spread_send, arrived, host, peer).start()

    def to_own_host(src, dst, arrived):
        @pl.when(core == 0)
        def _():
            remote(src.at[0], dst.at[0], spread_send, arrived, host, shard).start()

        @pl.when(core == 1)
        def _():
            dst[0] = src[0]

    def to_clusters(src, dst, sent, arrived):
        for k in (4, 3, 5, 2, 6, 1, 7):
            remote(src, dst.at[cluster], sent, arrived, lax.rem(cluster + k, clusters), shard).start()
        dst[cluster] = src[...]

    def wait_recv(dst, arrived):
        remote(dst, dst, spread_send, arrived, cluster, far[0]).wait_recv()

    def wait_send(src, sent):
        remote(src, src, sent, final_sem, cluster, far[0]).wait_send()

    def hosts_reached(src):
        @pl.when(core == 0)
        def _():
            wait_send(src, spread_send)

        @pl.when(core == 1)
        def _():
            wait_send(src.at[pl.ds(0, shards - 1)], spread_send)

    tile_role = iota((8, 128), 0) >> 2
    rows, lanes = iota((128, 128), 0), iota((128, 128), 1)
    row_slot, row_half = (rows >> 1) & 1, rows & 1
    row_dev = jnp.concatenate([jnp.where(tile_role == 0, near[q], far[q]) for q in range(16)], axis=0)
    lane1 = iota((1, 128), 1)
    loads[0].wait()
    lane_path = jnp.full((1, 128), -1, I32)
    for i in range(incs):
        lane_path = jnp.where(lane1 == i, inc_path[i], lane_path)
    owner = (lane_path >> 4) == row_dev
    before = dot(owner.astype(F32), (rows < lanes).astype(F32))
    slot = owner & (before == row_slot.astype(F32))

    def fill(dst, x):
        for q in range(16):
            tile = x[q * 8:q * 8 + 8]
            dst[q] = tile
            dst[16 + q] = pltpu.roll(tile, 4, 0)

    wanted = jnp.sum(jnp.where(slot, (lane_path & 15) + 1, 0).astype(F32), axis=1, keepdims=True) - 1.0
    fill(ask_send, jnp.broadcast_to(wanted, (128, 128)))

    def border_first(ref):
        x = ref[...]
        return jnp.concatenate([x[interior:], jnp.zeros((8 - edges, x.shape[1]), F32), x[:interior]], axis=0)

    loads[1].wait()
    loads[2].wait()
    cap = border_first(capacity)
    dual = border_first(dual_start)
    edge_send[...] = jnp.concatenate([cap[:4], dual[:4]], axis=0)

    def halves(ref):
        x = ref[...]
        return jnp.concatenate([x[:, :128], x[:, 128:]], axis=0)

    for copy in loads[3:7]:
        copy.wait()
    row32 = iota((32, 128), 0)
    count = jnp.zeros((32, 128), I32)
    for b in range(blocks):
        count = jnp.where((row32 & 15) == b, path_count[b], count)
    live = (((row32 & 15) < cluster_size[0]) & ((row32 >> 4) * 128 + iota((32, 128), 1) < count)).astype(F32)
    top = halves(demand) * live
    own_start[...] = jnp.minimum(jnp.maximum(halves(flow_start), 0.0), top)
    own_bounds[0] = top
    own_bounds[1] = halves(utility)

    def to_both(src, dst, sent, arrived):
        remote(src, dst.at[core, 1], sent.at[1], arrived.at[core, 1], host, far[0]).start()

        @pl.when(core == 0)
        def _():
            remote(src, dst.at[core, 0], sent.at[0], arrived.at[core, 0], host, shard).start()

        @pl.when(core == 1)
        def _():
            dst[core, 0] = src[...]

    pl.semaphore_wait(barrier, shards + clusters - 2 + (shards - 1) * core)
    to_both(own_start, state, start_sent, start_sem)
    to_hosts(NEAR_FAR_FIRST, ask_send, ask_recv.at[core], ask_sem.at[core])
    to_own_host(ask_send, ask_recv.at[core], ask_sem.at[core])
    to_clusters(edge_send, edge_recv, edge_sent, edge_sem)

    loads[7].wait()
    lane_q = iota((1, 512), 1)
    lane_edge = jnp.full((1, 512), -1, I32)
    for i in range(incs):
        lane_edge = jnp.where((lane_q >> 4) == i, (inc_edge[i] + (8 - interior)) & 7, lane_edge)
    spread = (iota((128, 512), 0) == (iota((128, 512), 1) >> 4)).astype(F32)
    fits = (lane_edge == (lane_q & 7)) & (((lane_q >> 3) & 1) == (iota((128, 512), 0) & 1))
    both = jnp.where(fits, dot(slot.astype(F32), spread), 0.0)
    slot_edge[...] = both.astype(BF16)
    slot_edge_t[...] = both.T.astype(BF16)

    loads[8].wait()
    partner_row = jnp.full((4, 128), -1, I32)
    for k in range(slots):
        partner_row = jnp.where(iota((4, 128), 0) == k, partner[0, k], partner_row)
    partner8 = jnp.concatenate([partner_row, partner_row], axis=0)

    to_hosts(DISTANT, ask_send, ask_recv.at[core], distant_sem.at[core])
    to_both(own_bounds, bounds, bounds_sent, bounds_sem)

    loads[9].wait()

    def shrink(i, _):
        at = pl.ds(pl.multiple_of(i * paths, paths), paths)
        block = incidence[i].astype(BF16)
        inc[at, :] = block
        inc_t[:, at] = block.T
        return 0
    lax.fori_loop(0, incs, shrink, 0)

    def from_holders(src, c, arrived):
        wait_recv(src if c == 0 else src.at[pl.ds(0, shards - 1)], arrived)

    def share(c, flows):
        x = pick(choose[c, :, :64], flows)
        for q in range(16):
            flow_send[c, q] = x[q * 8:q * 8 + 8]
        for u in NEAR_FAR_FIRST + ([0] if c == 0 else []):
            remote(flow_send.at[c, u], flow_recv.at[BACK[u]], share_send.at[c], flow_sem, even + c, near[u]).start()
        if c == 1:
            flow_recv[0] = flow_send[c, 0]

    def shared():
        for c in range(2):
            wait_send(flow_send.at[c] if c == 0 else flow_send.at[c, pl.ds(0, 15)], share_send.at[c])

    @pl.when(core == 1)
    def _():
        rows2, lanes2 = iota((256, 128), 0), iota((256, 128), 1)
        fit = (((lanes2 >> 4) & 1) == (rows2 & 1)) & ((lanes2 >> 5) == ((rows2 >> 2) & 1))
        block_of_lane = (lanes2 & 15).astype(F32)
        for c in range(2):
            wait_recv(ask_recv.at[c, pl.ds(0, 16 - c)], ask_sem.at[c])
            chosen = (ask_recv[c, :16].reshape(128, 128) == block_of_lane[:128]) & fit[:128]
            choose[c] = chosen.astype(F32).astype(BF16)
        for c in range(2):
            for role in range(c, 2):
                wait_recv(state.at[c, role], start_sem.at[c, role])
            share(c, state[c].reshape(64, 128))
        for c in range(2):
            wait_recv(ask_recv.at[c, pl.ds(16, 16)], distant_sem.at[c])
            chosen = (ask_recv[c].reshape(256, 128) == block_of_lane) & fit
            choose_t[c] = chosen.astype(F32).T.astype(BF16)
            for role in range(c, 2):
                wait_recv(bounds.at[c, role], bounds_sem.at[c, role])

    def total_load(t):
        @pl.when(core == 0)
        def _():
            wait_recv(flow_recv, flow_sem)

        @pl.when(core == 1)
        def _():
            wait_recv(flow_recv.at[pl.ds(0, 15)], flow_sem)

        got = flow_recv[...].reshape(128, 128)
        parts = dot(slot_edge_t[...], jnp.concatenate(thirds(got), axis=1))
        columns = []
        for q in range(2 * incs):
            chunk = parts[q * 8:q * 8 + 8]
            columns.append(jnp.concatenate([chunk[:, :128], chunk[:, 128:256], chunk[:, 256:]], axis=0).astype(BF16))
        sums = dot(jnp.concatenate(columns, axis=1), inc[...])
        own = (sums[16:] + sums[8:16]) + sums[:8]
        border_send[...] = own[:4]
        to_clusters(border_send, border_recv.at[t], border_sent, border_sem.at[t])
        wait_recv(border_recv.at[t, pl.ds(0, clusters - 1)], border_sem.at[t])
        twin = jnp.zeros((4, 128), F32)
        for c in range(clusters):
            twin = twin + jnp.where(partner_row == c, border_recv[t, c], 0.0)
        return jnp.concatenate([own[:4] + twin, own[4:]], axis=0)

    def settle(load, duals):
        split = jnp.minimum(limit, load + duals)
        duals = (duals + load) - split
        return (load - split) + duals, duals

    wait_recv(edge_recv.at[pl.ds(0, clusters - 1)], edge_sem)
    twin = jnp.zeros((8, 128), F32)
    for c in range(clusters):
        twin = twin + jnp.where(partner8 == c, edge_recv[c], 0.0)
    limit = unit * jnp.concatenate([0.5 * (cap[:4] + twin[:4]), cap[4:]], axis=0)
    duals = jnp.concatenate([0.5 * (dual[:4] + twin[4:]), dual[4:]], axis=0)

    residual, duals = settle(total_load(0), duals)

    hosts_reached(ask_send)
    wait_send(edge_recv.at[pl.ds(0, clusters - 1)], edge_sent)
    for src, sem in ((own_start, start_sent), (own_bounds, bounds_sent)):
        wait_send(src, sem.at[1])

        @pl.when(core == 0)
        def _():
            wait_send(src, sem.at[0])

    def iterate(t, carry):
        residual, duals = carry
        turn = lax.rem(t, 2)
        parts = dot(jnp.concatenate(thirds(residual), axis=0), inc_t[...])
        back = (parts[16:] + parts[8:16]) + parts[:8]
        back = jnp.concatenate([back[:, q * 128:q * 128 + 128] for q in range(2 * incs)], axis=0)
        sums = pick(slot_edge[...], back)
        for q in range(16):
            sum_send[16 + q] = pltpu.roll(sums[q * 8:q * 8 + 8], 4, 0)
        to_hosts(DISTANT, sum_send, sum_recv.at[turn, core], sum_sem.at[turn, core])
        for q in range(16):
            sum_send[q] = sums[q * 8:q * 8 + 8]
        to_hosts(NEAR_FAR_FIRST, sum_send, sum_recv.at[turn, core], sum_sem.at[turn, core])
        to_own_host(sum_send, sum_recv.at[turn, core], sum_sem.at[turn, core])
        wait_send(border_recv.at[t, pl.ds(0, clusters - 1)], border_sent)

        @pl.when(core == 1)
        def _():
            shared()
            for c in (1, 0):
                from_holders(sum_recv.at[turn, c], c, sum_sem.at[turn, c])
                grad = pick(choose_t[c, :64, :], sum_recv[turn, c].reshape(256, 128))
                top = bounds[c, :, 0].reshape(64, 128)
                gain = bounds[c, :, 1].reshape(64, 128)
                flows = state[c].reshape(64, 128)
                flows = jnp.minimum(jnp.maximum(flows - step_size * (grad - gain), 0.0), top)
                share(c, flows)
                state[c] = flows.reshape(2, 32, 128)

            @pl.when(t == ITERS)
            def _():
                remote(state.at[0, 0], final, final_sent, final_sem, even, shard).start()

        hosts_reached(sum_send)
        return settle(total_load(t), duals)

    residual, duals = lax.fori_loop(1, ITERS + 1, iterate, (residual, duals))
    wait_send(border_recv.at[0, pl.ds(0, clusters - 1)], border_sent)

    @pl.when(core == 0)
    def _():
        wait_recv(final, final_sem)

    @pl.when(core == 1)
    def _():
        shared()
        wait_send(state.at[0, 0], final_sent)
        final[...] = state[1, 0]

    flows = final[...]
    flows_out[...] = jnp.concatenate([flows[:16], flows[16:]], axis=1)
    duals_out[...] = jnp.concatenate([duals[4:], duals[:slots]], axis=0)


def write_out(flows, duals, flows_out, duals_out, sems):
    copies = [pltpu.make_async_copy(flows, flows_out, sems.at[0]), pltpu.make_async_copy(duals, duals_out, sems.at[1])]
    for copy in copies:
        copy.start()
    for copy in copies:
        copy.wait()


def body(flow_start, demand, utility, path_count, cluster_size, incidence, inc_path, inc_edge, capacity, dual_start, partner):
    blocks, paths = flow_start.shape
    incs, _, width = incidence.shape
    edges, slots = capacity.shape[0], partner.shape[1]
    clusters, shards = lax.axis_size("cluster"), lax.axis_size("shard")
    norm_bound = max(2, incs * incs * paths * width // (1024 * edges * blocks))
    unit = float(max(1, incs * paths // (160 * edges)))
    dims = (clusters, shards, blocks, paths, incs, edges, slots, norm_bound, unit)
    scalars = (path_count, inc_path, inc_edge, partner)
    arrays = (flow_start, demand, utility, incidence, capacity, dual_start)
    dma = pltpu.SemaphoreType.DMA
    results = pl.pallas_call(
        functools.partial(kernel, dims),
        out_shape=(pltpu.VMEM(flow_start.shape, F32), pltpu.VMEM(capacity.shape, F32)),
        in_specs=[pl.BlockSpec(memory_space=pltpu.SMEM)] + [pl.BlockSpec(memory_space=pltpu.HBM)] * (len(scalars) + len(arrays)),
        out_specs=[pl.BlockSpec(memory_space=pltpu.VMEM)] * 2,
        scratch_shapes=[pltpu.SMEM(x.shape, I32) for x in scalars] + [pltpu.VMEM(x.shape, F32) for x in arrays] + [
            pltpu.VMEM((incs * paths, width), BF16),
            pltpu.VMEM((width, incs * paths), BF16),
            pltpu.VMEM((128, 512), BF16),
            pltpu.VMEM((512, 128), BF16),
            pltpu.VMEM((2, 128, 128), BF16),
            pltpu.VMEM((2, 128, 256), BF16),
            pltpu.VMEM((shards, 8, 128), F32),
            pltpu.VMEM((2, shards, 8, 128), F32),
            pltpu.VMEM((2, 16, 8, 128), F32),
            pltpu.VMEM((16, 8, 128), F32),
            pltpu.VMEM((shards, 8, 128), F32),
            pltpu.VMEM((2, 2, shards, 8, 128), F32),
            pltpu.VMEM((8, 128), F32),
            pltpu.VMEM((clusters, 8, 128), F32),
            pltpu.VMEM((4, 128), F32),
            pltpu.VMEM((ITERS + 1, clusters, 4, 128), F32),
            pltpu.VMEM((32, 128), F32),
            pltpu.VMEM((2, 32, 128), F32),
            pltpu.VMEM((2, 2, 32, 128), F32),
            pltpu.VMEM((2, 2, 2, 32, 128), F32),
            pltpu.VMEM((32, 128), F32),
            dma((10,)), dma(()), dma((2,)), dma(()), dma(()), dma((2,)), dma((2,)), dma(()),
            dma((2,)), dma((2,)), dma(()), dma((2, 2)), dma(()), dma((ITERS + 1,)), dma((2, 2)), dma((2, 2)), dma(()),
        ],
        compiler_params=pltpu.CompilerParams(
            collective_id=0, has_side_effects=True, vmem_limit_bytes=24 * 1024 * 1024),
    )(cluster_size, *(pltpu.with_memory_space_constraint(x, pltpu.HBM) for x in scalars + arrays))
    return pl.pallas_call(
        write_out,
        out_shape=(jax.ShapeDtypeStruct(flow_start.shape, F32), jax.ShapeDtypeStruct(capacity.shape, F32)),
        in_specs=[pl.BlockSpec(memory_space=pltpu.VMEM)] * 2,
        out_specs=[pl.BlockSpec(memory_space=pltpu.HBM)] * 2,
        scratch_shapes=[dma((2,))],
    )(*(pltpu.with_memory_space_constraint(x, pltpu.VMEM) for x in results))


def solution(mesh):
    both = P(("cluster", "shard"))
    rows = P(("cluster", "shard"), None)
    return jax.shard_map(
        body,
        mesh=mesh,
        in_specs=(rows, rows, rows, both, P("cluster"), P(("cluster", "shard"), None, None), both, both, rows, rows, P("cluster", None)),
        out_specs=(rows, rows),
        check_vma=False,
    )
```
